256 devices in a mesh: seq: 32 (over z_hi, x, core), head: 8 (over y, z_lo).
Axes of the slice: x: 4, y: 4, z: 8 (z_hi: 4, z_lo: 2; z = z_hi * 2 + z_lo), core: 2. Of those that a mesh axis runs over, the one named last changes fastest.
Arguments:
- queries: bfloat16 [6144, 4096], P('seq', 'head'), may hold values from -12.5 to 12.5
- keys: bfloat16 [6144, 1024], P('seq', 'head'), may hold values from -10.5 to 10.5
- values: bfloat16 [6144, 1024], P('seq', 'head'), may hold values from -6 to 6
- d_out: bfloat16 [6144, 4096], P('seq', 'head'), may hold values from -6 to 6
- w_out: bfloat16 [4096, 4096], P('head'), may hold values from -0.09375 to 0.09375
- doc_starts: int32 [4], replicated, may hold values from 0 to 6128, as said below
Outputs:
- query_grad: bfloat16 [6144, 4096], P('seq', 'head')
- key_grad: bfloat16 [6144, 1024], P('seq', 'head')
- value_grad: bfloat16 [6144, 1024], P('seq', 'head')
The draws below stay inside these ranges and needn't reach their ends.
Inputs may be any that keep to these rules, and one draw needn't show every extreme that they name: doc_starts[0] is 0, the entries rise strictly, every entry is a multiple of 16, and the last entry is 6128, so the last document has 16 positions; a document runs from its start to the next start or to the end of the sequence.
All inputs are finite; a program needn't handle non-finite values.
Results may differ from the reference program's by a relative error of at most 0.0163.
Values may be sent and summed in bfloat16 or wider, within the bound.
A program may use at most 128 MiB of HBM per device.

```python
import math
import jax
import jax.numpy as jnp
from jax import lax

D = 4096
QH = 32
KVH = 8
DH = 128
NDOC = 4
TOKENS = 6144


def row_scales(key, row_count):
    return jnp.exp(jax.random.uniform(key, (row_count, 1), jnp.float32, math.log(0.4), math.log(2.5)))


def base_block(key, shape):
    return jnp.clip(jax.random.normal(key, shape, jnp.float32), -4.0, 4.0)


def draw_queries(key, part):
    base = base_block(jax.random.fold_in(key, 11), (TOKENS, QH * DH)) * row_scales(jax.random.fold_in(key, 12), TOKENS)
    return base.astype(jnp.bfloat16)


def draw_keys(key, part):
    base = base_block(jax.random.fold_in(key, 21), (TOKENS, KVH * DH)) * row_scales(jax.random.fold_in(key, 22), TOKENS)
    return base.astype(jnp.bfloat16)


def draw_doc_starts(key, part):
    slot_count = TOKENS // 16
    shuffled = jax.random.permutation(jax.random.fold_in(key, 41), slot_count - 2) + 1
    cut_points = jnp.sort(shuffled[:NDOC - 2]) * 16
    final_start = jnp.full((1,), (slot_count - 1) * 16, jnp.int32)
    return jnp.concatenate([jnp.zeros((1,), jnp.int32), cut_points.astype(jnp.int32), final_start])


def level_of(stream_key, shape, shards, low, high):
    def one(position, blocks):
        steps = jax.random.uniform(jax.random.fold_in(jax.random.fold_in(stream_key, 6), position), (blocks,), jnp.float32, low / len(shards), high / len(shards))
        return jnp.repeat(jnp.exp(steps), shape[position] // blocks).reshape((-1,) + (1,) * (len(shape) - position - 1))

    level = one(*shards[0])
    for cut in shards[1:]:
        level = level * one(*cut)
    return level


def centred(stream_key, dims, scale, bound, pieces=(), kind=jnp.bfloat16):
    values = jax.random.normal(stream_key, dims, jnp.float32) * scale
    if len(pieces) > 0:
        values = level_of(stream_key, dims, pieces, -0.22, 0.18) * values
    return jnp.clip(values, min=-bound, max=bound).astype(kind)


def setup_inputs(seed: int = 0) -> dict:
    key_of = jax.random.split(jax.random.key(seed), 7)
    return {
        "queries": draw_queries(jax.random.fold_in(key_of[6], 71), 0),
        "keys": draw_keys(jax.random.fold_in(key_of[6], 71), 0),
        "values": centred(key_of[2], (TOKENS, KVH * DH), 1.0, 6.0, ((0, 32), (1, 8))),
        "d_out": centred(key_of[3], (TOKENS, D), 1.0, 6.0, ((0, 32), (1, 8))),
        "w_out": centred(key_of[4], (QH * DH, D), D ** -0.5, 0.09375, ((0, 8),)),
        "doc_starts": draw_doc_starts(jax.random.fold_in(key_of[6], 71), 0),
    }


NEG_FILL = -1e+30

def doc_index(doc_starts, places):
    return lax.optimization_barrier(jnp.sum((places[:, None] >= doc_starts[None, :]).astype(jnp.int32), axis=1))

def rounded(values_in):
    return lax.optimization_barrier(values_in.astype(jnp.bfloat16)).astype(jnp.float32)

def reference(queries, keys, values, d_out, w_out, doc_starts):
    seq_length = queries.shape[0]
    per_group = QH // KVH
    scaling = 1.0 / math.sqrt(DH)
    attn_grad = lax.dot_general(d_out, w_out, (((1,), (1,)), ((), ())), preferred_element_type=jnp.float32).astype(jnp.bfloat16)
    places = jnp.arange(seq_length, dtype=jnp.int32)
    doc_of = doc_index(doc_starts, places)
    block_rows = math.gcd(seq_length, 512)
    query_parts = []
    key_parts = []
    value_parts = []
    for group_id in range(KVH):
        key_one = keys[:, group_id * DH:(group_id + 1) * DH].astype(jnp.float32)
        value_one = values[:, group_id * DH:(group_id + 1) * DH].astype(jnp.float32)
        first_col = group_id * per_group * DH
        last_col = (group_id + 1) * per_group * DH
        query_grp = queries[:, first_col:last_col].astype(jnp.float32).reshape(seq_length, per_group, DH)
        grad_grp = attn_grad[:, first_col:last_col].astype(jnp.float32).reshape(seq_length, per_group, DH)

        def one_block(carried, block_no):
            key_acc, value_acc = carried
            offset = block_no * block_rows
            row_ids = offset + jnp.arange(block_rows, dtype=jnp.int32)
            q_blk = lax.dynamic_slice_in_dim(query_grp, offset, block_rows, 0)
            g_blk = lax.dynamic_slice_in_dim(grad_grp, offset, block_rows, 0)
            row_docs = lax.dynamic_slice_in_dim(doc_of, offset, block_rows, 0)
            allowed = ((places[None, :] <= row_ids[:, None]) & (doc_of[None, :] == row_docs[:, None]))[None]
            scores = jnp.einsum('shd,kd->hsk', q_blk, key_one) * scaling
            masked = jnp.where(allowed, scores, NEG_FILL)
            highest = lax.optimization_barrier(jnp.max(masked, axis=-1, keepdims=True))
            summed = lax.optimization_barrier(jnp.sum(jnp.where(allowed, jnp.exp(masked - highest), 0.0), axis=-1, keepdims=True))
            log_total = highest + jnp.log(summed)
            prob_full = jnp.where(allowed, jnp.exp(scores - log_total), 0.0)
            grad_dots = jnp.einsum('shd,kd->hsk', g_blk, value_one)
            row_delta = lax.optimization_barrier(jnp.sum(prob_full * grad_dots, axis=-1, keepdims=True))
            dscores = rounded(prob_full * (grad_dots - row_delta) * scaling)
            prob_half = rounded(prob_full)
            query_out = jnp.einsum('hsk,kd->shd', dscores, key_one)
            key_acc = key_acc + jnp.einsum('hsk,shd->kd', dscores, q_blk)
            value_acc = value_acc + jnp.einsum('hsk,shd->kd', prob_half, g_blk)
            return ((key_acc, value_acc), query_out)
        empty_acc = jnp.zeros((seq_length, DH), jnp.float32)
        finals, query_out = lax.scan(one_block, (empty_acc, empty_acc), jnp.arange(seq_length // block_rows, dtype=jnp.int32))
        query_parts.append(query_out.reshape(seq_length, per_group * DH))
        key_parts.append(finals[0])
        value_parts.append(finals[1])
    query_grad = jnp.concatenate(query_parts, axis=1).astype(jnp.bfloat16)
    key_grad = jnp.concatenate(key_parts, axis=1).astype(jnp.bfloat16)
    value_grad = jnp.concatenate(value_parts, axis=1).astype(jnp.bfloat16)
    return (query_grad, key_grad, value_grad)
```

```python
import math

import jax
import jax.numpy as jnp
from jax import lax
from jax.sharding import PartitionSpec as P

DH = 128


NEG_FILL = -1e30


def doc_index(doc_starts, places):
    return jnp.sum((places[:, None] >= doc_starts[None, :]).astype(jnp.int32), axis=1)


def allowed_pairs(doc_starts, row_ids, col_ids):
    earlier = col_ids[None, :] <= row_ids[:, None]
    same_doc = doc_index(doc_starts, row_ids)[:, None] == doc_index(doc_starts, col_ids)[None, :]
    return (earlier & same_doc)[None, None]


def shards(queries, keys, values, d_out, w_out, doc_starts):
    rows_here = queries.shape[0]
    head_size = DH
    groups = keys.shape[1] // head_size
    per_group = queries.shape[1] // keys.shape[1]
    kv_cols = keys.shape[1]
    scaling = 1.0 / math.sqrt(head_size)
    first_row = lax.axis_index("seq") * rows_here
    my_rows = first_row + jnp.arange(rows_here, dtype=jnp.int32)
    kv_block = lax.all_gather(
        jnp.concatenate([keys, values], axis=1), "seq", axis=0, tiled=True
    )
    attn_grad = lax.dot_general(
        lax.all_gather(d_out, "head", axis=1, tiled=True),
        w_out,
        (((1,), (1,)), ((), ())),
        preferred_element_type=jnp.float32,
    ).astype(jnp.bfloat16)
    query_four = queries.reshape(rows_here, groups, per_group, head_size)
    grad_four = attn_grad.reshape(rows_here, groups, per_group, head_size)
    piece_rows = kv_block.shape[0]
    allowed = allowed_pairs(doc_starts, my_rows, jnp.arange(piece_rows, dtype=jnp.int32))
    key_three = kv_block[:, :kv_cols].reshape(piece_rows, groups, head_size)
    value_three = kv_block[:, kv_cols:].reshape(piece_rows, groups, head_size)
    scores = (
        jnp.einsum("sghd,kgd->ghsk", query_four, key_three, preferred_element_type=jnp.float32)
        * scaling
    )
    scores = jnp.where(allowed, scores, NEG_FILL)
    high = jnp.max(scores, axis=-1)
    weights = jnp.where(allowed, jnp.exp(scores - high[..., None]), 0.0)
    total = jnp.sum(weights, axis=-1)
    log_total = high + jnp.log(total)
    prob_full = jnp.where(allowed, jnp.exp(scores - log_total[..., None]), 0.0)
    grad_dots = jnp.einsum(
        "sghd,kgd->ghsk", grad_four, value_three, preferred_element_type=jnp.float32
    )
    row_delta = jnp.sum(prob_full * grad_dots, axis=-1)
    dscores = (prob_full * (grad_dots - row_delta[..., None]) * scaling).astype(jnp.bfloat16)
    prob_half = prob_full.astype(jnp.bfloat16)
    query_acc = jnp.einsum("ghsk,kgd->sghd", dscores, key_three, preferred_element_type=jnp.float32)
    key_terms = jnp.einsum(
        "ghsk,sghd->kgd", dscores, query_four, preferred_element_type=jnp.float32
    ).reshape(piece_rows, kv_cols)
    value_terms = jnp.einsum(
        "ghsk,sghd->kgd", prob_half, grad_four, preferred_element_type=jnp.float32
    ).reshape(piece_rows, kv_cols)
    kv_grad = lax.psum_scatter(
        jnp.concatenate([key_terms, value_terms], axis=1).astype(jnp.bfloat16),
        "seq", scatter_dimension=0, tiled=True,
    )
    query_grad = query_acc.reshape(rows_here, groups * per_group * head_size).astype(jnp.bfloat16)
    key_grad = kv_grad[:, :kv_cols]
    value_grad = kv_grad[:, kv_cols:]
    return (query_grad, key_grad, value_grad)


def solution(mesh):
    return jax.shard_map(
        shards,
        mesh=mesh,
        in_specs=(
            P("seq", "head"),
            P("seq", "head"),
            P("seq", "head"),
            P("seq", "head"),
            P("head", None),
            P(),
        ),
        out_specs=(P("seq", "head"), P("seq", "head"), P("seq", "head")),
        check_vma=False,
    )
```

```python
import functools
import math

import jax
import jax.numpy as jnp
from jax import lax
from jax.sharding import PartitionSpec as P
from jax.experimental import pallas as pl
from jax.experimental.pallas import tpu as pltpu

DH = 128


NEG_FILL = -1e30


def doc_index(doc_starts, places):
    return jnp.sum((places[:, None] >= doc_starts[None, :]).astype(jnp.int32), axis=1)


def allowed_pairs(doc_starts, row_ids, col_ids):
    earlier = col_ids[None, :] <= row_ids[:, None]
    same_doc = doc_index(doc_starts, row_ids)[:, None] == doc_index(doc_starts, col_ids)[None, :]
    return (earlier & same_doc)[None, None]


def _peer_kernel(n, axis, upward, per_target, src_ref, out_ref, send_sem, recv_sem):
    me = lax.axis_index(axis)
    step = 1 if upward else -1

    def send_desc(k):
        tgt = me + step * k
        src = src_ref.at[tgt] if per_target else src_ref
        return pltpu.make_async_remote_copy(
            src, out_ref.at[me], send_sem.at[k - 1], recv_sem.at[k - 1],
            device_id={axis: tgt}, device_id_type=pl.DeviceIdType.MESH)

    def recv_desc(k):
        origin = me - step * k
        src = src_ref.at[me] if per_target else src_ref
        return pltpu.make_async_remote_copy(
            src, out_ref.at[origin], send_sem.at[k - 1], recv_sem.at[k - 1],
            device_id={axis: origin}, device_id_type=pl.DeviceIdType.MESH)

    def can_send(k):
        return (me + k < n) if upward else (me - k >= 0)

    def can_recv(k):
        return (me - k >= 0) if upward else (me + k < n)

    def start_one(k, carry):
        @pl.when(can_send(k))
        def _():
            send_desc(k).start()
        return carry

    def finish_one(k, carry):
        @pl.when(can_send(k))
        def _():
            send_desc(k).wait_send()

        @pl.when(can_recv(k))
        def _():
            recv_desc(k).wait_recv()
        return carry

    lax.fori_loop(1, n, start_one, 0)
    lax.fori_loop(1, n, finish_one, 0)


def peer_blocks(src, n, axis, upward, per_target):
    blk = src.shape[1:] if per_target else src.shape
    return pl.pallas_call(
        functools.partial(_peer_kernel, n, axis, upward, per_target),
        out_shape=jax.ShapeDtypeStruct((n,) + tuple(blk), src.dtype),
        in_specs=[pl.BlockSpec(memory_space=pl.ANY)],
        out_specs=pl.BlockSpec(memory_space=pl.ANY),
        scratch_shapes=[pltpu.SemaphoreType.DMA((n - 1,)), pltpu.SemaphoreType.DMA((n - 1,))],
        compiler_params=pltpu.CompilerParams(has_side_effects=True),
    )(src)


def shards(queries, keys, values, d_out, w_out, doc_starts):
    rows_here = queries.shape[0]
    head_size = DH
    groups = keys.shape[1] // head_size
    per_group = queries.shape[1] // keys.shape[1]
    kv_cols = keys.shape[1]
    scaling = 1.0 / math.sqrt(head_size)
    first_row = lax.axis_index("seq") * rows_here
    my_rows = first_row + jnp.arange(rows_here, dtype=jnp.int32)
    n_seq = lax.axis_size("seq")
    me = lax.axis_index("seq")
    kv_here = jnp.concatenate([keys, values], axis=1)
    kv_slots = peer_blocks(kv_here, n_seq, "seq", True, False)
    slot_ids = jnp.arange(n_seq, dtype=jnp.int32)[:, None, None]
    kv_block = jnp.where(
        slot_ids == me, kv_here[None], jnp.where(slot_ids < me, kv_slots, 0)
    ).reshape(n_seq * rows_here, 2 * keys.shape[1])
    attn_grad = lax.dot_general(
        lax.all_gather(d_out, "head", axis=1, tiled=True),
        w_out,
        (((1,), (1,)), ((), ())),
        preferred_element_type=jnp.float32,
    ).astype(jnp.bfloat16)
    query_four = queries.reshape(rows_here, groups, per_group, head_size)
    grad_four = attn_grad.reshape(rows_here, groups, per_group, head_size)
    piece_rows = kv_block.shape[0]
    allowed = allowed_pairs(doc_starts, my_rows, jnp.arange(piece_rows, dtype=jnp.int32))
    key_three = kv_block[:, :kv_cols].reshape(piece_rows, groups, head_size)
    value_three = kv_block[:, kv_cols:].reshape(piece_rows, groups, head_size)
    scores = (
        jnp.einsum("sghd,kgd->ghsk", query_four, key_three, preferred_element_type=jnp.float32)
        * scaling
    )
    scores = jnp.where(allowed, scores, NEG_FILL)
    high = jnp.max(scores, axis=-1)
    weights = jnp.where(allowed, jnp.exp(scores - high[..., None]), 0.0)
    total = jnp.sum(weights, axis=-1)
    log_total = high + jnp.log(total)
    prob_full = jnp.where(allowed, jnp.exp(scores - log_total[..., None]), 0.0)
    grad_dots = jnp.einsum(
        "sghd,kgd->ghsk", grad_four, value_three, preferred_element_type=jnp.float32
    )
    row_delta = jnp.sum(prob_full * grad_dots, axis=-1)
    dscores = (prob_full * (grad_dots - row_delta[..., None]) * scaling).astype(jnp.bfloat16)
    prob_half = prob_full.astype(jnp.bfloat16)
    query_acc = jnp.einsum("ghsk,kgd->sghd", dscores, key_three, preferred_element_type=jnp.float32)
    key_terms = jnp.einsum(
        "ghsk,sghd->kgd", dscores, query_four, preferred_element_type=jnp.float32
    ).reshape(piece_rows, kv_cols)
    value_terms = jnp.einsum(
        "ghsk,sghd->kgd", prob_half, grad_four, preferred_element_type=jnp.float32
    ).reshape(piece_rows, kv_cols)
    kv_terms = jnp.concatenate([key_terms, value_terms], axis=1).reshape(
        n_seq, rows_here, 2 * kv_cols
    )
    kv_recv = peer_blocks(kv_terms.astype(jnp.bfloat16), n_seq, "seq", False, True)
    kv_grad = (
        jnp.sum(jnp.where(slot_ids > me, kv_recv.astype(jnp.float32), 0.0), axis=0)
        + lax.dynamic_index_in_dim(kv_terms, me, 0, keepdims=False)
    ).astype(jnp.bfloat16)
    query_grad = query_acc.reshape(rows_here, groups * per_group * head_size).astype(jnp.bfloat16)
    key_grad = kv_grad[:, :kv_cols]
    value_grad = kv_grad[:, kv_cols:]
    return (query_grad, key_grad, value_grad)


def solution(mesh):
    return jax.shard_map(
        shards,
        mesh=mesh,
        in_specs=(
            P("seq", "head"),
            P("seq", "head"),
            P("seq", "head"),
            P("seq", "head"),
            P("head", None),
            P(),
        ),
        out_specs=(P("seq", "head"), P("seq", "head"), P("seq", "head")),
        check_vma=False,
    )
```

```python
import functools
import math

import jax
import jax.numpy as jnp
from jax import lax
from jax.sharding import PartitionSpec as P
from jax.experimental import pallas as pl
from jax.experimental.pallas import tpu as pltpu

DH = 128


NEG_FILL = -1e30


def doc_index(doc_starts, places):
    return jnp.sum((places[:, None] >= doc_starts[None, :]).astype(jnp.int32), axis=1)


def allowed_pairs(doc_starts, row_ids, col_ids):
    earlier = col_ids[None, :] <= row_ids[:, None]
    same_doc = doc_index(doc_starts, row_ids)[:, None] == doc_index(doc_starts, col_ids)[None, :]
    return (earlier & same_doc)[None, None]


def _peer_kernel(n, axis, upward, per_target, src_ref, out_ref, send_sem, recv_sem):
    me = lax.axis_index(axis)
    step = -1 if upward is False else 1

    def send_desc(k):
        tgt = lax.rem(me + k, n) if upward is None else me + step * k
        src = src_ref.at[tgt] if per_target else src_ref
        return pltpu.make_async_remote_copy(
            src, out_ref.at[me], send_sem.at[k - 1], recv_sem.at[k - 1],
            device_id={axis: tgt}, device_id_type=pl.DeviceIdType.MESH)

    def recv_desc(k):
        origin = lax.rem(me + n - k, n) if upward is None else me - step * k
        src = src_ref.at[me] if per_target else src_ref
        return pltpu.make_async_remote_copy(
            src, out_ref.at[origin], send_sem.at[k - 1], recv_sem.at[k - 1],
            device_id={axis: origin}, device_id_type=pl.DeviceIdType.MESH)

    def can_send(k):
        if upward is None:
            return k > 0
        return (me + k < n) if upward else (me - k >= 0)

    def can_recv(k):
        if upward is None:
            return k > 0
        return (me - k >= 0) if upward else (me + k < n)

    def start_one(k, carry):
        @pl.when(can_send(k))
        def _():
            send_desc(k).start()
        return carry

    def finish_one(k, carry):
        @pl.when(can_send(k))
        def _():
            send_desc(k).wait_send()

        @pl.when(can_recv(k))
        def _():
            recv_desc(k).wait_recv()
        return carry

    lax.fori_loop(1, n, start_one, 0)
    lax.fori_loop(1, n, finish_one, 0)


def peer_blocks(src, n, axis, upward, per_target):
    blk = src.shape[1:] if per_target else src.shape
    return pl.pallas_call(
        functools.partial(_peer_kernel, n, axis, upward, per_target),
        out_shape=jax.ShapeDtypeStruct((n,) + tuple(blk), src.dtype),
        in_specs=[pl.BlockSpec(memory_space=pl.ANY)],
        out_specs=pl.BlockSpec(memory_space=pl.ANY),
        scratch_shapes=[pltpu.SemaphoreType.DMA((n - 1,)), pltpu.SemaphoreType.DMA((n - 1,))],
        compiler_params=pltpu.CompilerParams(has_side_effects=True),
    )(src)


def shards(queries, keys, values, d_out, w_out, doc_starts):
    rows_here = queries.shape[0]
    head_size = DH
    groups = keys.shape[1] // head_size
    per_group = queries.shape[1] // keys.shape[1]
    kv_cols = keys.shape[1]
    scaling = 1.0 / math.sqrt(head_size)
    first_row = lax.axis_index("seq") * rows_here
    my_rows = first_row + jnp.arange(rows_here, dtype=jnp.int32)
    kv_block = lax.all_gather(
        jnp.concatenate([keys, values], axis=1), "seq", axis=0, tiled=True
    )
    n_head = lax.axis_size("head")
    me_head = lax.axis_index("head")
    d_slots = peer_blocks(d_out, n_head, "head", None, False)
    head_ids = jnp.arange(n_head, dtype=jnp.int32)[:, None, None]
    d_all = jnp.where(head_ids == me_head, d_out[None], d_slots)
    attn_grad = jnp.einsum(
        "hte,che->tc",
        d_all,
        w_out.reshape(w_out.shape[0], n_head, d_out.shape[1]),
        preferred_element_type=jnp.float32,
    ).astype(jnp.bfloat16)
    query_four = queries.reshape(rows_here, groups, per_group, head_size)
    grad_four = attn_grad.reshape(rows_here, groups, per_group, head_size)
    piece_rows = kv_block.shape[0]
    allowed = allowed_pairs(doc_starts, my_rows, jnp.arange(piece_rows, dtype=jnp.int32))
    key_three = kv_block[:, :kv_cols].reshape(piece_rows, groups, head_size)
    value_three = kv_block[:, kv_cols:].reshape(piece_rows, groups, head_size)
    scores = (
        jnp.einsum("sghd,kgd->ghsk", query_four, key_three, preferred_element_type=jnp.float32)
        * scaling
    )
    scores = jnp.where(allowed, scores, NEG_FILL)
    high = jnp.max(scores, axis=-1)
    weights = jnp.where(allowed, jnp.exp(scores - high[..., None]), 0.0)
    total = jnp.sum(weights, axis=-1)
    log_total = high + jnp.log(total)
    prob_full = jnp.where(allowed, jnp.exp(scores - log_total[..., None]), 0.0)
    grad_dots = jnp.einsum(
        "sghd,kgd->ghsk", grad_four, value_three, preferred_element_type=jnp.float32
    )
    row_delta = jnp.sum(prob_full * grad_dots, axis=-1)
    dscores = (prob_full * (grad_dots - row_delta[..., None]) * scaling).astype(jnp.bfloat16)
    prob_half = prob_full.astype(jnp.bfloat16)
    query_acc = jnp.einsum("ghsk,kgd->sghd", dscores, key_three, preferred_element_type=jnp.float32)
    key_terms = jnp.einsum(
        "ghsk,sghd->kgd", dscores, query_four, preferred_element_type=jnp.float32
    ).reshape(piece_rows, kv_cols)
    value_terms = jnp.einsum(
        "ghsk,sghd->kgd", prob_half, grad_four, preferred_element_type=jnp.float32
    ).reshape(piece_rows, kv_cols)
    kv_grad = lax.psum_scatter(
        jnp.concatenate([key_terms, value_terms], axis=1).astype(jnp.bfloat16),
        "seq", scatter_dimension=0, tiled=True,
    )
    query_grad = query_acc.reshape(rows_here, groups * per_group * head_size).astype(jnp.bfloat16)
    key_grad = kv_grad[:, :kv_cols]
    value_grad = kv_grad[:, kv_cols:]
    return (query_grad, key_grad, value_grad)


def solution(mesh):
    return jax.shard_map(
        shards,
        mesh=mesh,
        in_specs=(
            P("seq", "head"),
            P("seq", "head"),
            P("seq", "head"),
            P("seq", "head"),
            P("head", None),
            P(),
        ),
        out_specs=(P("seq", "head"), P("seq", "head"), P("seq", "head")),
        check_vma=False,
    )
```

```python
import functools
import math

import jax
import jax.numpy as jnp
from jax import lax
from jax.sharding import PartitionSpec as P
from jax.experimental import pallas as pl
from jax.experimental.pallas import tpu as pltpu

DH = 128


NEG_FILL = -1e30


def doc_index(doc_starts, places):
    return jnp.sum((places[:, None] >= doc_starts[None, :]).astype(jnp.int32), axis=1)


def allowed_pairs(doc_starts, row_ids, col_ids):
    earlier = col_ids[None, :] <= row_ids[:, None]
    same_doc = doc_index(doc_starts, row_ids)[:, None] == doc_index(doc_starts, col_ids)[None, :]
    return (earlier & same_doc)[None, None]


def _peer_kernel(n, axis, upward, per_target, src_ref, out_ref, send_sem, recv_sem):
    me = lax.axis_index(axis)
    step = -1 if upward is False else 1

    def send_desc(k):
        tgt = lax.rem(me + k, n) if upward is None else me + step * k
        src = src_ref.at[tgt] if per_target else src_ref
        return pltpu.make_async_remote_copy(
            src, out_ref.at[me], send_sem.at[k - 1], recv_sem.at[k - 1],
            device_id={axis: tgt}, device_id_type=pl.DeviceIdType.MESH)

    def recv_desc(k):
        origin = lax.rem(me + n - k, n) if upward is None else me - step * k
        src = src_ref.at[me] if per_target else src_ref
        return pltpu.make_async_remote_copy(
            src, out_ref.at[origin], send_sem.at[k - 1], recv_sem.at[k - 1],
            device_id={axis: origin}, device_id_type=pl.DeviceIdType.MESH)

    def can_send(k):
        if upward is None:
            return k > 0
        return (me + k < n) if upward else (me - k >= 0)

    def can_recv(k):
        if upward is None:
            return k > 0
        return (me - k >= 0) if upward else (me + k < n)

    def start_one(k, carry):
        @pl.when(can_send(k))
        def _():
            send_desc(k).start()
        return carry

    def finish_one(k, carry):
        @pl.when(can_send(k))
        def _():
            send_desc(k).wait_send()

        @pl.when(can_recv(k))
        def _():
            recv_desc(k).wait_recv()
        return carry

    lax.fori_loop(1, n, start_one, 0)
    lax.fori_loop(1, n, finish_one, 0)


def peer_blocks(src, n, axis, upward, per_target):
    blk = src.shape[1:] if per_target else src.shape
    return pl.pallas_call(
        functools.partial(_peer_kernel, n, axis, upward, per_target),
        out_shape=jax.ShapeDtypeStruct((n,) + tuple(blk), src.dtype),
        in_specs=[pl.BlockSpec(memory_space=pl.ANY)],
        out_specs=pl.BlockSpec(memory_space=pl.ANY),
        scratch_shapes=[pltpu.SemaphoreType.DMA((n - 1,)), pltpu.SemaphoreType.DMA((n - 1,))],
        compiler_params=pltpu.CompilerParams(has_side_effects=True),
    )(src)


def shards(queries, keys, values, d_out, w_out, doc_starts):
    rows_here = queries.shape[0]
    head_size = DH
    groups = keys.shape[1] // head_size
    per_group = queries.shape[1] // keys.shape[1]
    kv_cols = keys.shape[1]
    scaling = 1.0 / math.sqrt(head_size)
    n_hi = lax.axis_size("seqhi")
    n_core = lax.axis_size("core")
    my_core = lax.axis_index("core")
    me = lax.axis_index("seqhi") * n_core + my_core
    first_row = me * rows_here
    my_rows = first_row + jnp.arange(rows_here, dtype=jnp.int32)
    kv_block = lax.all_gather(
        lax.all_gather(jnp.concatenate([keys, values], axis=1), "seqhi", axis=0),
        "core", axis=0,
    )
    n_head = lax.axis_size("head")
    me_head = lax.axis_index("head")
    d_slots = peer_blocks(d_out, n_head, "head", None, False)
    head_ids = jnp.arange(n_head, dtype=jnp.int32)[:, None, None]
    d_all = jnp.where(head_ids == me_head, d_out[None], d_slots)
    attn_grad = jnp.einsum(
        "hte,che->tc",
        d_all,
        w_out.reshape(w_out.shape[0], n_head, d_out.shape[1]),
        preferred_element_type=jnp.float32,
    ).astype(jnp.bfloat16)
    query_four = queries.reshape(rows_here, groups, per_group, head_size)
    grad_four = attn_grad.reshape(rows_here, groups, per_group, head_size)
    kv_block = kv_block.reshape(n_core * n_hi * rows_here, 2 * kv_cols)
    piece_rows = kv_block.shape[0]
    slot_core = jnp.arange(piece_rows, dtype=jnp.int32) // (n_hi * rows_here)
    slot_hi = (jnp.arange(piece_rows, dtype=jnp.int32) // rows_here) % n_hi
    col_ids = (slot_hi * n_core + slot_core) * rows_here + jnp.arange(piece_rows, dtype=jnp.int32) % rows_here
    allowed = allowed_pairs(doc_starts, my_rows, col_ids)
    key_three = kv_block[:, :kv_cols].reshape(piece_rows, groups, head_size)
    value_three = kv_block[:, kv_cols:].reshape(piece_rows, groups, head_size)
    scores = (
        jnp.einsum("sghd,kgd->ghsk", query_four, key_three, preferred_element_type=jnp.float32)
        * scaling
    )
    scores = jnp.where(allowed, scores, NEG_FILL)
    high = jnp.max(scores, axis=-1)
    weights = jnp.where(allowed, jnp.exp(scores - high[..., None]), 0.0)
    total = jnp.sum(weights, axis=-1)
    log_total = high + jnp.log(total)
    prob_full = jnp.where(allowed, jnp.exp(scores - log_total[..., None]), 0.0)
    grad_dots = jnp.einsum(
        "sghd,kgd->ghsk", grad_four, value_three, preferred_element_type=jnp.float32
    )
    row_delta = jnp.sum(prob_full * grad_dots, axis=-1)
    dscores = (prob_full * (grad_dots - row_delta[..., None]) * scaling).astype(jnp.bfloat16)
    prob_half = prob_full.astype(jnp.bfloat16)
    query_acc = jnp.einsum("ghsk,kgd->sghd", dscores, key_three, preferred_element_type=jnp.float32)
    key_terms = jnp.einsum(
        "ghsk,sghd->kgd", dscores, query_four, preferred_element_type=jnp.float32
    ).reshape(piece_rows, kv_cols)
    value_terms = jnp.einsum(
        "ghsk,sghd->kgd", prob_half, grad_four, preferred_element_type=jnp.float32
    ).reshape(piece_rows, kv_cols)
    kv_terms = jnp.concatenate([key_terms, value_terms], axis=1).astype(jnp.bfloat16)
    kv_grad = lax.psum_scatter(
        lax.psum_scatter(
            kv_terms.reshape(n_core, n_hi * rows_here, 2 * kv_cols), "core",
            scatter_dimension=0, tiled=False,
        ),
        "seqhi", scatter_dimension=0, tiled=True,
    )
    query_grad = query_acc.reshape(rows_here, groups * per_group * head_size).astype(jnp.bfloat16)
    key_grad = kv_grad[:, :kv_cols]
    value_grad = kv_grad[:, kv_cols:]
    return (query_grad, key_grad, value_grad)


def solution(mesh):
    n_seq, n_head = mesh.shape["seq"], mesh.shape["head"]
    split = jax.sharding.Mesh(
        mesh.devices.reshape(n_seq // 2, 2, n_head), ("seqhi", "core", "head")
    )
    rows = ("seqhi", "core")
    return jax.shard_map(
        shards,
        mesh=split,
        in_specs=(
            P(rows, "head"),
            P(rows, "head"),
            P(rows, "head"),
            P(rows, "head"),
            P("head", None),
            P(),
        ),
        out_specs=(P(rows, "head"), P(rows, "head"), P(rows, "head")),
        check_vma=False,
    )
```

```python
import functools
import math

import jax
import jax.numpy as jnp
from jax import lax
from jax.sharding import PartitionSpec as P
from jax.experimental import pallas as pl
from jax.experimental.pallas import tpu as pltpu

DH = 128


NEG_FILL = -1e30


def doc_index(doc_starts, places):
    return jnp.sum((places[:, None] >= doc_starts[None, :]).astype(jnp.int32), axis=1)


def allowed_pairs(doc_starts, row_ids, col_ids):
    earlier = col_ids[None, :] <= row_ids[:, None]
    same_doc = doc_index(doc_starts, row_ids)[:, None] == doc_index(doc_starts, col_ids)[None, :]
    return (earlier & same_doc)[None, None]


def _peer_kernel(n, axis, upward, per_target, src_ref, out_ref, send_sem, recv_sem):
    me = lax.axis_index(axis)
    step = -1 if upward is False else 1

    def send_desc(k):
        tgt = lax.rem(me + k, n) if upward is None else me + step * k
        src = src_ref.at[tgt] if per_target else src_ref
        return pltpu.make_async_remote_copy(
            src, out_ref.at[me], send_sem.at[k - 1], recv_sem.at[k - 1],
            device_id={axis: tgt}, device_id_type=pl.DeviceIdType.MESH)

    def recv_desc(k):
        origin = lax.rem(me + n - k, n) if upward is None else me - step * k
        src = src_ref.at[me] if per_target else src_ref
        return pltpu.make_async_remote_copy(
            src, out_ref.at[origin], send_sem.at[k - 1], recv_sem.at[k - 1],
            device_id={axis: origin}, device_id_type=pl.DeviceIdType.MESH)

    def can_send(k):
        if upward is None:
            return k > 0
        return (me + k < n) if upward else (me - k >= 0)

    def can_recv(k):
        if upward is None:
            return k > 0
        return (me - k >= 0) if upward else (me + k < n)

    def start_one(k, carry):
        @pl.when(can_send(k))
        def _():
            send_desc(k).start()
        return carry

    def finish_one(k, carry):
        @pl.when(can_send(k))
        def _():
            send_desc(k).wait_send()

        @pl.when(can_recv(k))
        def _():
            recv_desc(k).wait_recv()
        return carry

    lax.fori_loop(1, n, start_one, 0)
    lax.fori_loop(1, n, finish_one, 0)


def peer_blocks(src, n, axis, upward, per_target):
    blk = src.shape[1:] if per_target else src.shape
    return pl.pallas_call(
        functools.partial(_peer_kernel, n, axis, upward, per_target),
        out_shape=jax.ShapeDtypeStruct((n,) + tuple(blk), src.dtype),
        in_specs=[pl.BlockSpec(memory_space=pl.ANY)],
        out_specs=pl.BlockSpec(memory_space=pl.ANY),
        scratch_shapes=[pltpu.SemaphoreType.DMA((n - 1,)), pltpu.SemaphoreType.DMA((n - 1,))],
        compiler_params=pltpu.CompilerParams(has_side_effects=True),
    )(src)


def shards(queries, keys, values, d_out, w_out, doc_starts):
    rows_here = queries.shape[0]
    head_size = DH
    groups = keys.shape[1] // head_size
    per_group = queries.shape[1] // keys.shape[1]
    kv_cols = keys.shape[1]
    scaling = 1.0 / math.sqrt(head_size)
    n_zh = lax.axis_size("zhi")
    n_x = lax.axis_size("xx")
    n_core = lax.axis_size("core")
    n_hi = n_zh * n_x
    me = (lax.axis_index("zhi") * n_x + lax.axis_index("xx")) * n_core + lax.axis_index("core")
    first_row = me * rows_here
    my_rows = first_row + jnp.arange(rows_here, dtype=jnp.int32)
    kv_block = lax.all_gather(
        lax.all_gather(
            lax.all_gather(jnp.concatenate([keys, values], axis=1), "zhi", axis=0),
            "xx", axis=0,
        ),
        "core", axis=0,
    )
    n_head = lax.axis_size("head")
    me_head = lax.axis_index("head")
    d_slots = peer_blocks(d_out, n_head, "head", None, False)
    head_ids = jnp.arange(n_head, dtype=jnp.int32)[:, None, None]
    d_all = jnp.where(head_ids == me_head, d_out[None], d_slots)
    attn_grad = jnp.einsum(
        "hte,che->tc",
        d_all,
        w_out.reshape(w_out.shape[0], n_head, d_out.shape[1]),
        preferred_element_type=jnp.float32,
    ).astype(jnp.bfloat16)
    query_four = queries.reshape(rows_here, groups, per_group, head_size)
    grad_four = attn_grad.reshape(rows_here, groups, per_group, head_size)
    kv_block = kv_block.reshape(n_core * n_hi * rows_here, 2 * kv_cols)
    piece_rows = kv_block.shape[0]
    slot_core = jnp.arange(piece_rows, dtype=jnp.int32) // (n_hi * rows_here)
    slot_x = (jnp.arange(piece_rows, dtype=jnp.int32) // (n_zh * rows_here)) % n_x
    slot_zh = (jnp.arange(piece_rows, dtype=jnp.int32) // rows_here) % n_zh
    slot_hi = slot_zh * n_x + slot_x
    col_ids = (slot_hi * n_core + slot_core) * rows_here + jnp.arange(piece_rows, dtype=jnp.int32) % rows_here
    allowed = allowed_pairs(doc_starts, my_rows, col_ids)
    key_three = kv_block[:, :kv_cols].reshape(piece_rows, groups, head_size)
    value_three = kv_block[:, kv_cols:].reshape(piece_rows, groups, head_size)
    scores = (
        jnp.einsum("sghd,kgd->ghsk", query_four, key_three, preferred_element_type=jnp.float32)
        * scaling
    )
    scores = jnp.where(allowed, scores, NEG_FILL)
    high = jnp.max(scores, axis=-1)
    weights = jnp.where(allowed, jnp.exp(scores - high[..., None]), 0.0)
    total = jnp.sum(weights, axis=-1)
    log_total = high + jnp.log(total)
    prob_full = jnp.where(allowed, jnp.exp(scores - log_total[..., None]), 0.0)
    grad_dots = jnp.einsum(
        "sghd,kgd->ghsk", grad_four, value_three, preferred_element_type=jnp.float32
    )
    row_delta = jnp.sum(prob_full * grad_dots, axis=-1)
    dscores = (prob_full * (grad_dots - row_delta[..., None]) * scaling).astype(jnp.bfloat16)
    prob_half = prob_full.astype(jnp.bfloat16)
    query_acc = jnp.einsum("ghsk,kgd->sghd", dscores, key_three, preferred_element_type=jnp.float32)
    key_terms = jnp.einsum(
        "ghsk,sghd->kgd", dscores, query_four, preferred_element_type=jnp.float32
    ).reshape(piece_rows, kv_cols)
    value_terms = jnp.einsum(
        "ghsk,sghd->kgd", prob_half, grad_four, preferred_element_type=jnp.float32
    ).reshape(piece_rows, kv_cols)
    kv_terms = jnp.concatenate([key_terms, value_terms], axis=1).astype(jnp.bfloat16)
    kv_grad = lax.psum_scatter(
        lax.psum_scatter(
            lax.psum_scatter(
                kv_terms.reshape(n_core, n_x, n_zh * rows_here, 2 * kv_cols), "core",
                scatter_dimension=0, tiled=False,
            ),
            "xx", scatter_dimension=0, tiled=False,
        ),
        "zhi", scatter_dimension=0, tiled=True,
    )
    query_grad = query_acc.reshape(rows_here, groups * per_group * head_size).astype(jnp.bfloat16)
    key_grad = kv_grad[:, :kv_cols]
    value_grad = kv_grad[:, kv_cols:]
    return (query_grad, key_grad, value_grad)


def solution(mesh):
    n_seq, n_head = mesh.shape["seq"], mesh.shape["head"]
    split = jax.sharding.Mesh(
        mesh.devices.reshape(n_seq // 8, 4, 2, n_head), ("zhi", "xx", "core", "head")
    )
    rows = ("zhi", "xx", "core")
    return jax.shard_map(
        shards,
        mesh=split,
        in_specs=(
            P(rows, "head"),
            P(rows, "head"),
            P(rows, "head"),
            P(rows, "head"),
            P("head", None),
            P(),
        ),
        out_specs=(P(rows, "head"), P(rows, "head"), P(rows, "head")),
        check_vma=False,
    )
```

```python
import functools
import math

import jax
import jax.numpy as jnp
from jax import lax
from jax.sharding import PartitionSpec as P
from jax.experimental import pallas as pl
from jax.experimental.pallas import tpu as pltpu

DH = 128


NEG_FILL = -1e30


def doc_index(doc_starts, places):
    return jnp.sum((places[:, None] >= doc_starts[None, :]).astype(jnp.int32), axis=1)


def allowed_pairs(doc_starts, row_ids, col_ids):
    earlier = col_ids[None, :] <= row_ids[:, None]
    same_doc = doc_index(doc_starts, row_ids)[:, None] == doc_index(doc_starts, col_ids)[None, :]
    return (earlier & same_doc)[None, None]


def _peer_kernel(n, axis, upward, per_target, src_ref, out_ref, send_sem, recv_sem):
    me = lax.axis_index(axis)
    step = -1 if upward is False else 1

    def send_desc(k):
        tgt = lax.rem(me + k, n) if upward is None else me + step * k
        src = src_ref.at[tgt] if per_target else src_ref
        return pltpu.make_async_remote_copy(
            src, out_ref.at[me], send_sem.at[k - 1], recv_sem.at[k - 1],
            device_id={axis: tgt}, device_id_type=pl.DeviceIdType.MESH)

    def recv_desc(k):
        origin = lax.rem(me + n - k, n) if upward is None else me - step * k
        src = src_ref.at[me] if per_target else src_ref
        return pltpu.make_async_remote_copy(
            src, out_ref.at[origin], send_sem.at[k - 1], recv_sem.at[k - 1],
            device_id={axis: origin}, device_id_type=pl.DeviceIdType.MESH)

    def can_send(k):
        if upward is None:
            return k > 0
        return (me + k < n) if upward else (me - k >= 0)

    def can_recv(k):
        if upward is None:
            return k > 0
        return (me - k >= 0) if upward else (me + k < n)

    def start_one(k, carry):
        @pl.when(can_send(k))
        def _():
            send_desc(k).start()
        return carry

    def finish_one(k, carry):
        @pl.when(can_send(k))
        def _():
            send_desc(k).wait_send()

        @pl.when(can_recv(k))
        def _():
            recv_desc(k).wait_recv()
        return carry

    lax.fori_loop(1, n, start_one, 0)
    lax.fori_loop(1, n, finish_one, 0)


def peer_blocks(src, n, axis, upward, per_target):
    blk = src.shape[1:] if per_target else src.shape
    return pl.pallas_call(
        functools.partial(_peer_kernel, n, axis, upward, per_target),
        out_shape=jax.ShapeDtypeStruct((n,) + tuple(blk), src.dtype),
        in_specs=[pl.BlockSpec(memory_space=pl.ANY)],
        out_specs=pl.BlockSpec(memory_space=pl.ANY),
        scratch_shapes=[pltpu.SemaphoreType.DMA((n - 1,)), pltpu.SemaphoreType.DMA((n - 1,))],
        compiler_params=pltpu.CompilerParams(has_side_effects=True),
    )(src)


KEY_TILE = 512


def _tile_mask(j, tk, rowpos_ref, rowdoc_ref, coldoc_ref):
    col = j * tk + lax.broadcasted_iota(jnp.int32, (1, tk), 1)
    return (col <= rowpos_ref[...]) & (coldoc_ref[...] == rowdoc_ref[...])


def _stats_kernel(scaling, tk, dh, bounds_ref, q_ref, g_ref, kv_ref, rowpos_ref, rowdoc_ref,
                  coldoc_ref, lt_ref, delta_ref, m_sc, l_sc, a_sc):
    j = pl.program_id(0)

    @pl.when(j == 0)
    def _():
        m_sc[...] = jnp.full(m_sc.shape, NEG_FILL, jnp.float32)
        l_sc[...] = jnp.zeros(l_sc.shape, jnp.float32)
        a_sc[...] = jnp.zeros(a_sc.shape, jnp.float32)

    @pl.when((j >= bounds_ref[0]) & (j <= bounds_ref[1]))
    def _():
        dims = (((1,), (1,)), ((), ()))
        scores = lax.dot_general(q_ref[...], kv_ref[:, :dh], dims,
                                 preferred_element_type=jnp.float32) * scaling
        allowed = _tile_mask(j, tk, rowpos_ref, rowdoc_ref, coldoc_ref)
        scores = jnp.where(allowed, scores, NEG_FILL)
        m_old = m_sc[...]
        m_new = jnp.maximum(m_old, jnp.max(scores, axis=1, keepdims=True))
        e = jnp.where(allowed, jnp.exp(scores - m_new), 0.0)
        gd = lax.dot_general(g_ref[...], kv_ref[:, dh:], dims,
                             preferred_element_type=jnp.float32)
        alpha = jnp.exp(m_old - m_new)
        l_sc[...] = alpha * l_sc[...] + jnp.sum(e, axis=1, keepdims=True)
        a_sc[...] = alpha * a_sc[...] + jnp.sum(e * gd, axis=1, keepdims=True)
        m_sc[...] = m_new

    @pl.when(j == pl.num_programs(0) - 1)
    def _():
        lt_ref[...] = m_sc[...] + jnp.log(l_sc[...])
        delta_ref[...] = a_sc[...] / l_sc[...]


def _grad_kernel(scaling, tk, dh, bounds_ref, q_ref, g_ref, kv_ref, rowpos_ref, rowdoc_ref,
                 coldoc_ref, lt_ref, delta_ref, dq_ref, dkv_ref, dq_sc):
    j = pl.program_id(0)
    active = (j >= bounds_ref[0]) & (j <= bounds_ref[1])

    @pl.when(j == 0)
    def _():
        dq_sc[...] = jnp.zeros(dq_sc.shape, jnp.float32)

    @pl.when(active)
    def _():
        dims = (((1,), (1,)), ((), ()))
        tdims = (((0,), (0,)), ((), ()))
        k_t = kv_ref[:, :dh]
        scores = lax.dot_general(q_ref[...], k_t, dims,
                                 preferred_element_type=jnp.float32) * scaling
        allowed = _tile_mask(j, tk, rowpos_ref, rowdoc_ref, coldoc_ref)
        probs = jnp.where(allowed, jnp.exp(scores - lt_ref[...]), 0.0)
        gd = lax.dot_general(g_ref[...], kv_ref[:, dh:], dims,
                             preferred_element_type=jnp.float32)
        ds = (probs * (gd - delta_ref[...]) * scaling).astype(jnp.bfloat16)
        dq_sc[...] += jnp.dot(ds, k_t, preferred_element_type=jnp.float32)
        dk = lax.dot_general(ds, q_ref[...], tdims, preferred_element_type=jnp.float32)
        dv = lax.dot_general(probs.astype(jnp.bfloat16), g_ref[...], tdims,
                             preferred_element_type=jnp.float32)
        dkv_ref[:, :dh] = dk.astype(dkv_ref.dtype)
        dkv_ref[:, dh:] = dv.astype(dkv_ref.dtype)

    @pl.when(jnp.logical_not(active))
    def _():
        dkv_ref[...] = jnp.zeros(dkv_ref.shape, dkv_ref.dtype)

    @pl.when(j == pl.num_programs(0) - 1)
    def _():
        dq_ref[...] = dq_sc[...].astype(dq_ref.dtype)


def attention_grads(q_rows, g_rows, kv_full, doc_starts, first_row, rows_here, scaling):
    n_rows, dh = q_rows.shape
    n_keys = kv_full.shape[0]
    tk = KEY_TILE
    n_tiles = n_keys // tk
    row_pos = first_row + jnp.arange(n_rows, dtype=jnp.int32) % rows_here
    row_doc = doc_index(doc_starts, row_pos)
    col_doc = doc_index(doc_starts, jnp.arange(n_keys, dtype=jnp.int32))[None, :]
    doc_first = jnp.max(jnp.where(doc_starts <= first_row, doc_starts, 0))
    bounds = jnp.stack([doc_first // tk, (first_row + rows_here - 1) // tk]).astype(jnp.int32)
    row_pos = row_pos[:, None]
    row_doc = row_doc[:, None]

    def tile_of(j, b):
        return jnp.minimum(jnp.maximum(j, b[0]), b[1])

    full = lambda shape: pl.BlockSpec(shape, lambda j, b: (0, 0))
    in_specs = [
        full((n_rows, dh)),
        full((n_rows, dh)),
        pl.BlockSpec((tk, 2 * dh), lambda j, b: (tile_of(j, b), 0)),
        full((n_rows, 1)),
        full((n_rows, 1)),
        pl.BlockSpec((1, tk), lambda j, b: (0, tile_of(j, b))),
    ]
    params = pltpu.CompilerParams(dimension_semantics=("arbitrary",))
    mm = 2 * n_rows * n_keys * dh
    log_total, delta = pl.pallas_call(
        functools.partial(_stats_kernel, scaling, tk, dh),
        grid_spec=pltpu.PrefetchScalarGridSpec(
            num_scalar_prefetch=1,
            grid=(n_tiles,),
            in_specs=in_specs,
            out_specs=[full((n_rows, 1)), full((n_rows, 1))],
            scratch_shapes=[pltpu.VMEM((n_rows, 1), jnp.float32)] * 3,
        ),
        out_shape=[jax.ShapeDtypeStruct((n_rows, 1), jnp.float32)] * 2,
        compiler_params=params,
        cost_estimate=pl.CostEstimate(flops=2 * mm, transcendentals=n_rows * n_keys,
                                      bytes_accessed=n_keys * 4 * dh),
    )(bounds, q_rows, g_rows, kv_full, row_pos, row_doc, col_doc)
    dq, dkv = pl.pallas_call(
        functools.partial(_grad_kernel, scaling, tk, dh),
        grid_spec=pltpu.PrefetchScalarGridSpec(
            num_scalar_prefetch=1,
            grid=(n_tiles,),
            in_specs=in_specs + [full((n_rows, 1)), full((n_rows, 1))],
            out_specs=[full((n_rows, dh)), pl.BlockSpec((tk, 2 * dh), lambda j, b: (j, 0))],
            scratch_shapes=[pltpu.VMEM((n_rows, dh), jnp.float32)],
        ),
        out_shape=[jax.ShapeDtypeStruct((n_rows, dh), jnp.bfloat16),
                   jax.ShapeDtypeStruct((n_keys, 2 * dh), jnp.bfloat16)],
        compiler_params=params,
        cost_estimate=pl.CostEstimate(flops=5 * mm, transcendentals=n_rows * n_keys,
                                      bytes_accessed=n_keys * 8 * dh),
    )(bounds, q_rows, g_rows, kv_full, row_pos, row_doc, col_doc, log_total, delta)
    return dq, dkv


def shards(queries, keys, values, d_out, w_out, doc_starts):
    rows_here = queries.shape[0]
    head_size = DH
    groups = keys.shape[1] // head_size
    per_group = queries.shape[1] // keys.shape[1]
    kv_cols = keys.shape[1]
    scaling = 1.0 / math.sqrt(head_size)
    first_row = lax.axis_index("seq") * rows_here
    my_rows = first_row + jnp.arange(rows_here, dtype=jnp.int32)
    kv_block = lax.all_gather(
        jnp.concatenate([keys, values], axis=1), "seq", axis=0, tiled=True
    )
    n_head = lax.axis_size("head")
    me_head = lax.axis_index("head")
    d_slots = peer_blocks(d_out, n_head, "head", None, False)
    head_ids = jnp.arange(n_head, dtype=jnp.int32)[:, None, None]
    d_all = jnp.where(head_ids == me_head, d_out[None], d_slots)
    attn_grad = jnp.einsum(
        "hte,che->tc",
        d_all,
        w_out.reshape(w_out.shape[0], n_head, d_out.shape[1]),
        preferred_element_type=jnp.float32,
    ).astype(jnp.bfloat16)
    heads = groups * per_group
    q_rows = queries.reshape(rows_here, heads, head_size).transpose(1, 0, 2).reshape(
        heads * rows_here, head_size)
    g_rows = attn_grad.reshape(rows_here, heads, head_size).transpose(1, 0, 2).reshape(
        heads * rows_here, head_size)
    dq_rows, kv_terms = attention_grads(
        q_rows, g_rows, kv_block, doc_starts, first_row, rows_here, scaling)
    query_grad = dq_rows.reshape(heads, rows_here, head_size).transpose(1, 0, 2).reshape(
        rows_here, heads * head_size)
    kv_grad = lax.psum_scatter(kv_terms, "seq", scatter_dimension=0, tiled=True)
    key_grad = kv_grad[:, :kv_cols]
    value_grad = kv_grad[:, kv_cols:]
    return (query_grad, key_grad, value_grad)


def solution(mesh):
    return jax.shard_map(
        shards,
        mesh=mesh,
        in_specs=(
            P("seq", "head"),
            P("seq", "head"),
            P("seq", "head"),
            P("seq", "head"),
            P("head", None),
            P(),
        ),
        out_specs=(P("seq", "head"), P("seq", "head"), P("seq", "head")),
        check_vma=False,
    )
```

```python
import functools
import math

import jax
import jax.numpy as jnp
from jax import lax
from jax.sharding import PartitionSpec as P
from jax.experimental import pallas as pl
from jax.experimental.pallas import tpu as pltpu

DH = 128


NEG_FILL = -1e30


def doc_index(doc_starts, places):
    return jnp.sum((places[:, None] >= doc_starts[None, :]).astype(jnp.int32), axis=1)


def allowed_pairs(doc_starts, row_ids, col_ids):
    earlier = col_ids[None, :] <= row_ids[:, None]
    same_doc = doc_index(doc_starts, row_ids)[:, None] == doc_index(doc_starts, col_ids)[None, :]
    return (earlier & same_doc)[None, None]


def _peer_kernel(n, axis, upward, per_target, src_ref, out_ref, send_sem, recv_sem):
    me = lax.axis_index(axis)
    step = -1 if upward is False else 1

    def send_desc(k):
        tgt = lax.rem(me + k, n) if upward is None else me + step * k
        src = src_ref.at[tgt] if per_target else src_ref
        return pltpu.make_async_remote_copy(
            src, out_ref.at[me], send_sem.at[k - 1], recv_sem.at[k - 1],
            device_id={axis: tgt}, device_id_type=pl.DeviceIdType.MESH)

    def recv_desc(k):
        origin = lax.rem(me + n - k, n) if upward is None else me - step * k
        src = src_ref.at[me] if per_target else src_ref
        return pltpu.make_async_remote_copy(
            src, out_ref.at[origin], send_sem.at[k - 1], recv_sem.at[k - 1],
            device_id={axis: origin}, device_id_type=pl.DeviceIdType.MESH)

    def can_send(k):
        if upward is None:
            return k > 0
        return (me + k < n) if upward else (me - k >= 0)

    def can_recv(k):
        if upward is None:
            return k > 0
        return (me - k >= 0) if upward else (me + k < n)

    def start_one(k, carry):
        @pl.when(can_send(k))
        def _():
            send_desc(k).start()
        return carry

    def finish_one(k, carry):
        @pl.when(can_send(k))
        def _():
            send_desc(k).wait_send()

        @pl.when(can_recv(k))
        def _():
            recv_desc(k).wait_recv()
        return carry

    lax.fori_loop(1, n, start_one, 0)
    lax.fori_loop(1, n, finish_one, 0)


def peer_blocks(src, n, axis, upward, per_target):
    blk = src.shape[1:] if per_target else src.shape
    return pl.pallas_call(
        functools.partial(_peer_kernel, n, axis, upward, per_target),
        out_shape=jax.ShapeDtypeStruct((n,) + tuple(blk), src.dtype),
        in_specs=[pl.BlockSpec(memory_space=pl.ANY)],
        out_specs=pl.BlockSpec(memory_space=pl.ANY),
        scratch_shapes=[pltpu.SemaphoreType.DMA((n - 1,)), pltpu.SemaphoreType.DMA((n - 1,))],
        compiler_params=pltpu.CompilerParams(has_side_effects=True),
    )(src)


def _tile_mask(j, tk, rowpos_ref, rowdoc_ref, coldoc_ref):
    col = j * tk + lax.broadcasted_iota(jnp.int32, (1, tk), 1)
    return (col <= rowpos_ref[...]) & (coldoc_ref[...] == rowdoc_ref[...])


def _stats_kernel(scaling, tk, dh, bounds_ref, q_ref, g_ref, kv_ref, rowpos_ref, rowdoc_ref,
                  coldoc_ref, lt_ref, delta_ref, m_sc, l_sc, a_sc):
    j = pl.program_id(0)

    @pl.when(j == 0)
    def _():
        m_sc[...] = jnp.full(m_sc.shape, NEG_FILL, jnp.float32)
        l_sc[...] = jnp.zeros(l_sc.shape, jnp.float32)
        a_sc[...] = jnp.zeros(a_sc.shape, jnp.float32)

    @pl.when((j >= bounds_ref[0]) & (j <= bounds_ref[1]))
    def _():
        dims = (((1,), (1,)), ((), ()))
        scores = lax.dot_general(q_ref[...], kv_ref[:, :dh], dims,
                                 preferred_element_type=jnp.float32) * scaling
        allowed = _tile_mask(j, tk, rowpos_ref, rowdoc_ref, coldoc_ref)
        scores = jnp.where(allowed, scores, NEG_FILL)
        m_old = m_sc[...]
        m_new = jnp.maximum(m_old, jnp.max(scores, axis=1, keepdims=True))
        e = jnp.where(allowed, jnp.exp(scores - m_new), 0.0)
        gd = lax.dot_general(g_ref[...], kv_ref[:, dh:], dims,
                             preferred_element_type=jnp.float32)
        alpha = jnp.exp(m_old - m_new)
        l_sc[...] = alpha * l_sc[...] + jnp.sum(e, axis=1, keepdims=True)
        a_sc[...] = alpha * a_sc[...] + jnp.sum(e * gd, axis=1, keepdims=True)
        m_sc[...] = m_new

    @pl.when(j == pl.num_programs(0) - 1)
    def _():
        lt_ref[...] = m_sc[...] + jnp.log(l_sc[...])
        delta_ref[...] = a_sc[...] / l_sc[...]


def _grad_kernel(scaling, tk, dh, bounds_ref, q_ref, g_ref, kv_ref, rowpos_ref, rowdoc_ref,
                 coldoc_ref, lt_ref, delta_ref, dq_ref, dkv_ref, dq_sc):
    j = pl.program_id(0)
    active = (j >= bounds_ref[0]) & (j <= bounds_ref[1])

    @pl.when(j == 0)
    def _():
        dq_sc[...] = jnp.zeros(dq_sc.shape, jnp.float32)

    @pl.when(active)
    def _():
        dims = (((1,), (1,)), ((), ()))
        tdims = (((0,), (0,)), ((), ()))
        k_t = kv_ref[:, :dh]
        scores = lax.dot_general(q_ref[...], k_t, dims,
                                 preferred_element_type=jnp.float32) * scaling
        allowed = _tile_mask(j, tk, rowpos_ref, rowdoc_ref, coldoc_ref)
        probs = jnp.where(allowed, jnp.exp(scores - lt_ref[...]), 0.0)
        gd = lax.dot_general(g_ref[...], kv_ref[:, dh:], dims,
                             preferred_element_type=jnp.float32)
        ds = (probs * (gd - delta_ref[...]) * scaling).astype(jnp.bfloat16)
        dq_sc[...] += jnp.dot(ds, k_t, preferred_element_type=jnp.float32)
        dk = lax.dot_general(ds, q_ref[...], tdims, preferred_element_type=jnp.float32)
        dv = lax.dot_general(probs.astype(jnp.bfloat16), g_ref[...], tdims,
                             preferred_element_type=jnp.float32)
        owner_rows = dkv_ref.shape[3]
        for c in range(dkv_ref.shape[0]):
            part = slice(c * owner_rows, (c + 1) * owner_rows)
            dkv_ref[c, 0, 0, :, :dh] = dk[part].astype(dkv_ref.dtype)
            dkv_ref[c, 0, 0, :, dh:] = dv[part].astype(dkv_ref.dtype)

    @pl.when(jnp.logical_not(active))
    def _():
        dkv_ref[...] = jnp.zeros(dkv_ref.shape, dkv_ref.dtype)

    @pl.when(j == pl.num_programs(0) - 1)
    def _():
        dq_ref[...] = dq_sc[...].astype(dq_ref.dtype)


def attention_grads(q_rows, g_rows, kv_full, doc_starts, first_row, rows_here, scaling, chips):
    n_rows, dh = q_rows.shape
    n_keys = kv_full.shape[0]
    n_zh, n_x, n_core = chips
    tk = n_core * rows_here
    n_tiles = n_keys // tk
    row_pos = first_row + jnp.arange(n_rows, dtype=jnp.int32) % rows_here
    row_doc = doc_index(doc_starts, row_pos)
    col_doc = doc_index(doc_starts, jnp.arange(n_keys, dtype=jnp.int32))[None, :]
    doc_first = jnp.max(jnp.where(doc_starts <= first_row, doc_starts, 0))
    bounds = jnp.stack([doc_first // tk, (first_row + rows_here - 1) // tk]).astype(jnp.int32)
    row_pos = row_pos[:, None]
    row_doc = row_doc[:, None]

    def tile_of(j, b):
        return jnp.minimum(jnp.maximum(j, b[0]), b[1])

    full = lambda shape: pl.BlockSpec(shape, lambda j, b: (0, 0))
    in_specs = [
        full((n_rows, dh)),
        full((n_rows, dh)),
        pl.BlockSpec((tk, 2 * dh), lambda j, b: (tile_of(j, b), 0)),
        full((n_rows, 1)),
        full((n_rows, 1)),
        pl.BlockSpec((1, tk), lambda j, b: (0, tile_of(j, b))),
    ]
    params = pltpu.CompilerParams(dimension_semantics=("arbitrary",))
    mm = 2 * n_rows * n_keys * dh
    log_total, delta = pl.pallas_call(
        functools.partial(_stats_kernel, scaling, tk, dh),
        grid_spec=pltpu.PrefetchScalarGridSpec(
            num_scalar_prefetch=1,
            grid=(n_tiles,),
            in_specs=in_specs,
            out_specs=[full((n_rows, 1)), full((n_rows, 1))],
            scratch_shapes=[pltpu.VMEM((n_rows, 1), jnp.float32)] * 3,
        ),
        out_shape=[jax.ShapeDtypeStruct((n_rows, 1), jnp.float32)] * 2,
        compiler_params=params,
        cost_estimate=pl.CostEstimate(flops=2 * mm, transcendentals=n_rows * n_keys,
                                      bytes_accessed=n_keys * 4 * dh),
    )(bounds, q_rows, g_rows, kv_full, row_pos, row_doc, col_doc)
    dq, dkv = pl.pallas_call(
        functools.partial(_grad_kernel, scaling, tk, dh),
        grid_spec=pltpu.PrefetchScalarGridSpec(
            num_scalar_prefetch=1,
            grid=(n_tiles,),
            in_specs=in_specs + [full((n_rows, 1)), full((n_rows, 1))],
            out_specs=[
                full((n_rows, dh)),
                pl.BlockSpec((n_core, 1, 1, rows_here, 2 * dh),
                             lambda j, b: (0, j % n_x, j // n_x, 0, 0)),
            ],
            scratch_shapes=[pltpu.VMEM((n_rows, dh), jnp.float32)],
        ),
        out_shape=[jax.ShapeDtypeStruct((n_rows, dh), jnp.bfloat16),
                   jax.ShapeDtypeStruct((n_core, n_x, n_zh, rows_here, 2 * dh), jnp.bfloat16)],
        compiler_params=params,
        cost_estimate=pl.CostEstimate(flops=5 * mm, transcendentals=n_rows * n_keys,
                                      bytes_accessed=n_keys * 8 * dh),
    )(bounds, q_rows, g_rows, kv_full, row_pos, row_doc, col_doc, log_total, delta)
    return dq, dkv


def stage_reduce(parts, axis):
    n = lax.axis_size(axis)
    me = lax.axis_index(axis)
    slots = peer_blocks(parts.astype(jnp.bfloat16), n, axis, None, True)
    ids = jnp.arange(n, dtype=jnp.int32).reshape((n,) + (1,) * (parts.ndim - 1))
    others = jnp.sum(jnp.where(ids == me, 0.0, slots.astype(jnp.float32)), axis=0)
    return others + lax.dynamic_index_in_dim(parts, me, 0, keepdims=False).astype(jnp.float32)


def shards(queries, keys, values, d_out, w_out, doc_starts):
    rows_here = queries.shape[0]
    head_size = DH
    groups = keys.shape[1] // head_size
    per_group = queries.shape[1] // keys.shape[1]
    kv_cols = keys.shape[1]
    scaling = 1.0 / math.sqrt(head_size)
    n_zh = lax.axis_size("zhi")
    n_x = lax.axis_size("xx")
    n_core = lax.axis_size("core")
    me = (lax.axis_index("zhi") * n_x + lax.axis_index("xx")) * n_core + lax.axis_index("core")
    first_row = me * rows_here
    my_rows = first_row + jnp.arange(rows_here, dtype=jnp.int32)
    kv_block = lax.all_gather(
        jnp.concatenate([keys, values], axis=1), ("zhi", "xx", "core"), axis=0, tiled=True
    )
    n_head = lax.axis_size("head")
    me_head = lax.axis_index("head")
    d_slots = peer_blocks(d_out, n_head, "head", None, False)
    head_ids = jnp.arange(n_head, dtype=jnp.int32)[:, None, None]
    d_all = jnp.where(head_ids == me_head, d_out[None], d_slots)
    attn_grad = jnp.einsum(
        "hte,che->tc",
        d_all,
        w_out.reshape(w_out.shape[0], n_head, d_out.shape[1]),
        preferred_element_type=jnp.float32,
    ).astype(jnp.bfloat16)
    heads = groups * per_group
    q_rows = queries.reshape(rows_here, heads, head_size).transpose(1, 0, 2).reshape(
        heads * rows_here, head_size)
    g_rows = attn_grad.reshape(rows_here, heads, head_size).transpose(1, 0, 2).reshape(
        heads * rows_here, head_size)
    dq_rows, kv_terms = attention_grads(
        q_rows, g_rows, kv_block, doc_starts, first_row, rows_here, scaling,
        (n_zh, n_x, n_core))
    query_grad = dq_rows.reshape(heads, rows_here, head_size).transpose(1, 0, 2).reshape(
        rows_here, heads * head_size)
    kv_grad = kv_terms
    for axis in ("core", "xx", "zhi"):
        kv_grad = stage_reduce(kv_grad, axis)
    kv_grad = kv_grad.astype(jnp.bfloat16)
    key_grad = kv_grad[:, :kv_cols]
    value_grad = kv_grad[:, kv_cols:]
    return (query_grad, key_grad, value_grad)


def solution(mesh):
    n_seq, n_head = mesh.shape["seq"], mesh.shape["head"]
    split = jax.sharding.Mesh(
        mesh.devices.reshape(n_seq // 8, 4, 2, n_head), ("zhi", "xx", "core", "head")
    )
    rows = ("zhi", "xx", "core")
    return jax.shard_map(
        shards,
        mesh=split,
        in_specs=(
            P(rows, "head"),
            P(rows, "head"),
            P(rows, "head"),
            P(rows, "head"),
            P("head", None),
            P(),
        ),
        out_specs=(P(rows, "head"), P(rows, "head"), P(rows, "head")),
        check_vma=False,
    )
```

```python
import functools
import math

import jax
import jax.numpy as jnp
from jax import lax
from jax.sharding import PartitionSpec as P
from jax.experimental import pallas as pl
from jax.experimental.pallas import tpu as pltpu

DH = 128


NEG_FILL = -1e30


def doc_index(doc_starts, places):
    return jnp.sum((places[:, None] >= doc_starts[None, :]).astype(jnp.int32), axis=1)


def allowed_pairs(doc_starts, row_ids, col_ids):
    earlier = col_ids[None, :] <= row_ids[:, None]
    same_doc = doc_index(doc_starts, row_ids)[:, None] == doc_index(doc_starts, col_ids)[None, :]
    return (earlier & same_doc)[None, None]


def _peer_kernel(n, axis, upward, per_target, src_ref, out_ref, send_sem, recv_sem):
    me = lax.axis_index(axis)
    barrier = pltpu.get_barrier_semaphore()

    def greet(k, carry):
        pl.semaphore_signal(barrier, 1, device_id={axis: lax.rem(me + k, n)},
                            device_id_type=pl.DeviceIdType.MESH)
        return carry

    lax.fori_loop(1, n, greet, 0)
    pl.semaphore_wait(barrier, n - 1)
    step = -1 if upward is False else 1

    def send_desc(k):
        tgt = lax.rem(me + k, n) if upward is None else me + step * k
        src = src_ref.at[tgt] if per_target else src_ref
        return pltpu.make_async_remote_copy(
            src, out_ref.at[me], send_sem.at[k - 1], recv_sem.at[k - 1],
            device_id={axis: tgt}, device_id_type=pl.DeviceIdType.MESH)

    def recv_desc(k):
        origin = lax.rem(me + n - k, n) if upward is None else me - step * k
        src = src_ref.at[me] if per_target else src_ref
        return pltpu.make_async_remote_copy(
            src, out_ref.at[origin], send_sem.at[k - 1], recv_sem.at[k - 1],
            device_id={axis: origin}, device_id_type=pl.DeviceIdType.MESH)

    def can_send(k):
        if upward is None:
            return k > 0
        return (me + k < n) if upward else (me - k >= 0)

    def can_recv(k):
        if upward is None:
            return k > 0
        return (me - k >= 0) if upward else (me + k < n)

    def start_one(k, carry):
        @pl.when(can_send(k))
        def _():
            send_desc(k).start()
        return carry

    def finish_one(k, carry):
        @pl.when(can_send(k))
        def _():
            send_desc(k).wait_send()

        @pl.when(can_recv(k))
        def _():
            recv_desc(k).wait_recv()
        return carry

    lax.fori_loop(1, n, start_one, 0)
    lax.fori_loop(1, n, finish_one, 0)


def peer_blocks(src, n, axis, upward, per_target, cid):
    blk = src.shape[1:] if per_target else src.shape
    return pl.pallas_call(
        functools.partial(_peer_kernel, n, axis, upward, per_target),
        out_shape=jax.ShapeDtypeStruct((n,) + tuple(blk), src.dtype),
        in_specs=[pl.BlockSpec(memory_space=pl.ANY)],
        out_specs=pl.BlockSpec(memory_space=pl.ANY),
        scratch_shapes=[pltpu.SemaphoreType.DMA((n - 1,)), pltpu.SemaphoreType.DMA((n - 1,))],
        compiler_params=pltpu.CompilerParams(collective_id=cid, has_side_effects=True),
    )(src)


def _tile_mask(j, tk, rowpos_ref, rowdoc_ref, coldoc_ref):
    col = j * tk + lax.broadcasted_iota(jnp.int32, (1, tk), 1)
    return (col <= rowpos_ref[...]) & (coldoc_ref[...] == rowdoc_ref[...])


def _stats_kernel(scaling, tk, dh, bounds_ref, q_ref, g_ref, kv_ref, rowpos_ref, rowdoc_ref,
                  coldoc_ref, lt_ref, delta_ref, m_sc, l_sc, a_sc):
    j = pl.program_id(0)

    @pl.when(j == 0)
    def _():
        m_sc[...] = jnp.full(m_sc.shape, NEG_FILL, jnp.float32)
        l_sc[...] = jnp.zeros(l_sc.shape, jnp.float32)
        a_sc[...] = jnp.zeros(a_sc.shape, jnp.float32)

    @pl.when((j >= bounds_ref[0]) & (j <= bounds_ref[1]))
    def _():
        dims = (((1,), (1,)), ((), ()))
        scores = lax.dot_general(q_ref[...], kv_ref[:, :dh], dims,
                                 preferred_element_type=jnp.float32) * scaling
        allowed = _tile_mask(j, tk, rowpos_ref, rowdoc_ref, coldoc_ref)
        scores = jnp.where(allowed, scores, NEG_FILL)
        m_old = m_sc[...]
        m_new = jnp.maximum(m_old, jnp.max(scores, axis=1, keepdims=True))
        e = jnp.where(allowed, jnp.exp(scores - m_new), 0.0)
        gd = lax.dot_general(g_ref[...], kv_ref[:, dh:], dims,
                             preferred_element_type=jnp.float32)
        alpha = jnp.exp(m_old - m_new)
        l_sc[...] = alpha * l_sc[...] + jnp.sum(e, axis=1, keepdims=True)
        a_sc[...] = alpha * a_sc[...] + jnp.sum(e * gd, axis=1, keepdims=True)
        m_sc[...] = m_new

    @pl.when(j == pl.num_programs(0) - 1)
    def _():
        lt_ref[...] = m_sc[...] + jnp.log(l_sc[...])
        delta_ref[...] = a_sc[...] / l_sc[...]


def _grad_kernel(scaling, tk, dh, bounds_ref, q_ref, g_ref, kv_ref, rowpos_ref, rowdoc_ref,
                 coldoc_ref, lt_ref, delta_ref, dq_ref, dkv_ref, dq_sc):
    j = pl.program_id(0)
    active = (j >= bounds_ref[0]) & (j <= bounds_ref[1])

    @pl.when(j == 0)
    def _():
        dq_sc[...] = jnp.zeros(dq_sc.shape, jnp.float32)

    @pl.when(active)
    def _():
        dims = (((1,), (1,)), ((), ()))
        tdims = (((0,), (0,)), ((), ()))
        k_t = kv_ref[:, :dh]
        scores = lax.dot_general(q_ref[...], k_t, dims,
                                 preferred_element_type=jnp.float32) * scaling
        allowed = _tile_mask(j, tk, rowpos_ref, rowdoc_ref, coldoc_ref)
        probs = jnp.where(allowed, jnp.exp(scores - lt_ref[...]), 0.0)
        gd = lax.dot_general(g_ref[...], kv_ref[:, dh:], dims,
                             preferred_element_type=jnp.float32)
        ds = (probs * (gd - delta_ref[...]) * scaling).astype(jnp.bfloat16)
        dq_sc[...] += jnp.dot(ds, k_t, preferred_element_type=jnp.float32)
        dk = lax.dot_general(ds, q_ref[...], tdims, preferred_element_type=jnp.float32)
        dv = lax.dot_general(probs.astype(jnp.bfloat16), g_ref[...], tdims,
                             preferred_element_type=jnp.float32)
        owner_rows = dkv_ref.shape[3]
        for c in range(dkv_ref.shape[0]):
            part = slice(c * owner_rows, (c + 1) * owner_rows)
            dkv_ref[c, 0, 0, :, :dh] = dk[part].astype(dkv_ref.dtype)
            dkv_ref[c, 0, 0, :, dh:] = dv[part].astype(dkv_ref.dtype)

    @pl.when(jnp.logical_not(active))
    def _():
        dkv_ref[...] = jnp.zeros(dkv_ref.shape, dkv_ref.dtype)

    @pl.when(j == pl.num_programs(0) - 1)
    def _():
        dq_ref[...] = dq_sc[...].astype(dq_ref.dtype)


def attention_grads(q_rows, g_rows, kv_full, doc_starts, first_row, rows_here, scaling, chips):
    n_rows, dh = q_rows.shape
    n_keys = kv_full.shape[0]
    n_zh, n_x, n_core = chips
    tk = n_core * rows_here
    n_tiles = n_keys // tk
    row_pos = first_row + jnp.arange(n_rows, dtype=jnp.int32) % rows_here
    row_doc = doc_index(doc_starts, row_pos)
    col_doc = doc_index(doc_starts, jnp.arange(n_keys, dtype=jnp.int32))[None, :]
    doc_first = jnp.max(jnp.where(doc_starts <= first_row, doc_starts, 0))
    bounds = jnp.stack([doc_first // tk, (first_row + rows_here - 1) // tk]).astype(jnp.int32)
    row_pos = row_pos[:, None]
    row_doc = row_doc[:, None]

    def tile_of(j, b):
        return jnp.minimum(jnp.maximum(j, b[0]), b[1])

    full = lambda shape: pl.BlockSpec(shape, lambda j, b: (0, 0))
    in_specs = [
        full((n_rows, dh)),
        full((n_rows, dh)),
        pl.BlockSpec((tk, 2 * dh), lambda j, b: (tile_of(j, b), 0)),
        full((n_rows, 1)),
        full((n_rows, 1)),
        pl.BlockSpec((1, tk), lambda j, b: (0, tile_of(j, b))),
    ]
    params = pltpu.CompilerParams(dimension_semantics=("arbitrary",))
    mm = 2 * n_rows * n_keys * dh
    log_total, delta = pl.pallas_call(
        functools.partial(_stats_kernel, scaling, tk, dh),
        grid_spec=pltpu.PrefetchScalarGridSpec(
            num_scalar_prefetch=1,
            grid=(n_tiles,),
            in_specs=in_specs,
            out_specs=[full((n_rows, 1)), full((n_rows, 1))],
            scratch_shapes=[pltpu.VMEM((n_rows, 1), jnp.float32)] * 3,
        ),
        out_shape=[jax.ShapeDtypeStruct((n_rows, 1), jnp.float32)] * 2,
        compiler_params=params,
        cost_estimate=pl.CostEstimate(flops=2 * mm, transcendentals=n_rows * n_keys,
                                      bytes_accessed=n_keys * 4 * dh),
    )(bounds, q_rows, g_rows, kv_full, row_pos, row_doc, col_doc)
    dq, dkv = pl.pallas_call(
        functools.partial(_grad_kernel, scaling, tk, dh),
        grid_spec=pltpu.PrefetchScalarGridSpec(
            num_scalar_prefetch=1,
            grid=(n_tiles,),
            in_specs=in_specs + [full((n_rows, 1)), full((n_rows, 1))],
            out_specs=[
                full((n_rows, dh)),
                pl.BlockSpec((n_core, 1, 1, rows_here, 2 * dh),
                             lambda j, b: (0, j % n_x, j // n_x, 0, 0)),
            ],
            scratch_shapes=[pltpu.VMEM((n_rows, dh), jnp.float32)],
        ),
        out_shape=[jax.ShapeDtypeStruct((n_rows, dh), jnp.bfloat16),
                   jax.ShapeDtypeStruct((n_core, n_x, n_zh, rows_here, 2 * dh), jnp.bfloat16)],
        compiler_params=params,
        cost_estimate=pl.CostEstimate(flops=5 * mm, transcendentals=n_rows * n_keys,
                                      bytes_accessed=n_keys * 8 * dh),
    )(bounds, q_rows, g_rows, kv_full, row_pos, row_doc, col_doc, log_total, delta)
    return dq, dkv


def stage_reduce(parts, axis, cid):
    n = lax.axis_size(axis)
    me = lax.axis_index(axis)
    slots = peer_blocks(parts.astype(jnp.bfloat16), n, axis, None, True, cid)
    ids = jnp.arange(n, dtype=jnp.int32).reshape((n,) + (1,) * (parts.ndim - 1))
    others = jnp.sum(jnp.where(ids == me, 0.0, slots.astype(jnp.float32)), axis=0)
    return others + lax.dynamic_index_in_dim(parts, me, 0, keepdims=False).astype(jnp.float32)


def shards(queries, keys, values, d_out, w_out, doc_starts):
    rows_here = queries.shape[0]
    head_size = DH
    groups = keys.shape[1] // head_size
    per_group = queries.shape[1] // keys.shape[1]
    kv_cols = keys.shape[1]
    scaling = 1.0 / math.sqrt(head_size)
    n_zh = lax.axis_size("zhi")
    n_x = lax.axis_size("xx")
    n_core = lax.axis_size("core")
    me = (lax.axis_index("zhi") * n_x + lax.axis_index("xx")) * n_core + lax.axis_index("core")
    first_row = me * rows_here
    my_rows = first_row + jnp.arange(rows_here, dtype=jnp.int32)
    kv_block = lax.all_gather(
        jnp.concatenate([keys, values], axis=1), ("zhi", "xx", "core"), axis=0, tiled=True
    )
    n_head = lax.axis_size("head")
    me_head = lax.axis_index("head")
    d_slots = peer_blocks(d_out, n_head, "head", None, False, 0)
    head_ids = jnp.arange(n_head, dtype=jnp.int32)[:, None, None]
    d_all = jnp.where(head_ids == me_head, d_out[None], d_slots)
    attn_grad = jnp.einsum(
        "hte,che->tc",
        d_all,
        w_out.reshape(w_out.shape[0], n_head, d_out.shape[1]),
        preferred_element_type=jnp.float32,
    ).astype(jnp.bfloat16)
    heads = groups * per_group
    q_rows = queries.reshape(rows_here, heads, head_size).transpose(1, 0, 2).reshape(
        heads * rows_here, head_size)
    g_rows = attn_grad.reshape(rows_here, heads, head_size).transpose(1, 0, 2).reshape(
        heads * rows_here, head_size)
    dq_rows, kv_terms = attention_grads(
        q_rows, g_rows, kv_block, doc_starts, first_row, rows_here, scaling,
        (n_zh, n_x, n_core))
    query_grad = dq_rows.reshape(heads, rows_here, head_size).transpose(1, 0, 2).reshape(
        rows_here, heads * head_size)
    kv_grad = kv_terms
    for cid, axis in enumerate(("core", "xx", "zhi")):
        kv_grad = stage_reduce(kv_grad, axis, cid + 1)
    kv_grad = kv_grad.astype(jnp.bfloat16)
    key_grad = kv_grad[:, :kv_cols]
    value_grad = kv_grad[:, kv_cols:]
    return (query_grad, key_grad, value_grad)


def solution(mesh):
    n_seq, n_head = mesh.shape["seq"], mesh.shape["head"]
    split = jax.sharding.Mesh(
        mesh.devices.reshape(n_seq // 8, 4, 2, n_head), ("zhi", "xx", "core", "head")
    )
    rows = ("zhi", "xx", "core")
    return jax.shard_map(
        shards,
        mesh=split,
        in_specs=(
            P(rows, "head"),
            P(rows, "head"),
            P(rows, "head"),
            P(rows, "head"),
            P("head", None),
            P(),
        ),
        out_specs=(P(rows, "head"), P(rows, "head"), P(rows, "head")),
        check_vma=False,
    )
```

```python
import functools
import math

import jax
import jax.numpy as jnp
from jax import lax
from jax.sharding import PartitionSpec as P
from jax.experimental import pallas as pl
from jax.experimental.pallas import tpu as pltpu

DH = 128


NEG_FILL = -1e30


def doc_index(doc_starts, places):
    return jnp.sum((places[:, None] >= doc_starts[None, :]).astype(jnp.int32), axis=1)


def allowed_pairs(doc_starts, row_ids, col_ids):
    earlier = col_ids[None, :] <= row_ids[:, None]
    same_doc = doc_index(doc_starts, row_ids)[:, None] == doc_index(doc_starts, col_ids)[None, :]
    return (earlier & same_doc)[None, None]


def _peer_kernel(n, axis, upward, per_target, src_ref, out_ref, send_sem, recv_sem):
    me = lax.axis_index(axis)
    barrier = pltpu.get_barrier_semaphore()

    def greet(k, carry):
        pl.semaphore_signal(barrier, 1, device_id={axis: lax.rem(me + k, n)},
                            device_id_type=pl.DeviceIdType.MESH)
        return carry

    lax.fori_loop(1, n, greet, 0)
    pl.semaphore_wait(barrier, n - 1)
    step = -1 if upward is False else 1

    def send_desc(k):
        tgt = lax.rem(me + k, n) if upward is None else me + step * k
        src = src_ref.at[tgt] if per_target else src_ref
        return pltpu.make_async_remote_copy(
            src, out_ref.at[me], send_sem.at[k - 1], recv_sem.at[k - 1],
            device_id={axis: tgt}, device_id_type=pl.DeviceIdType.MESH)

    def recv_desc(k):
        origin = lax.rem(me + n - k, n) if upward is None else me - step * k
        src = src_ref.at[me] if per_target else src_ref
        return pltpu.make_async_remote_copy(
            src, out_ref.at[origin], send_sem.at[k - 1], recv_sem.at[k - 1],
            device_id={axis: origin}, device_id_type=pl.DeviceIdType.MESH)

    def can_send(k):
        if upward is None:
            return k > 0
        return (me + k < n) if upward else (me - k >= 0)

    def can_recv(k):
        if upward is None:
            return k > 0
        return (me - k >= 0) if upward else (me + k < n)

    def start_one(k, carry):
        @pl.when(can_send(k))
        def _():
            send_desc(k).start()
        return carry

    def finish_one(k, carry):
        @pl.when(can_send(k))
        def _():
            send_desc(k).wait_send()

        @pl.when(can_recv(k))
        def _():
            recv_desc(k).wait_recv()
        return carry

    lax.fori_loop(1, n, start_one, 0)
    lax.fori_loop(1, n, finish_one, 0)


def peer_blocks(src, n, axis, upward, per_target, cid):
    blk = src.shape[1:] if per_target else src.shape
    return pl.pallas_call(
        functools.partial(_peer_kernel, n, axis, upward, per_target),
        out_shape=jax.ShapeDtypeStruct((n,) + tuple(blk), src.dtype),
        in_specs=[pl.BlockSpec(memory_space=pl.ANY)],
        out_specs=pl.BlockSpec(memory_space=pl.ANY),
        scratch_shapes=[pltpu.SemaphoreType.DMA((n - 1,)), pltpu.SemaphoreType.DMA((n - 1,))],
        compiler_params=pltpu.CompilerParams(collective_id=cid, has_side_effects=True),
    )(src)


def _tile_mask(j, tk, rowpos_ref, rowdoc_ref, coldoc_ref):
    col = j * tk + lax.broadcasted_iota(jnp.int32, (1, tk), 1)
    return (col <= rowpos_ref[...]) & (coldoc_ref[...] == rowdoc_ref[...])


def _key_tile(kv_ref):
    return jnp.concatenate([kv_ref[c, 0, 0] for c in range(kv_ref.shape[0])], axis=0)


def _stats_kernel(scaling, tk, dh, bounds_ref, q_ref, g_ref, kv_ref, rowpos_ref, rowdoc_ref,
                  coldoc_ref, lt_ref, delta_ref, m_sc, l_sc, a_sc):
    j = pl.program_id(0)

    @pl.when(j == 0)
    def _():
        m_sc[...] = jnp.full(m_sc.shape, NEG_FILL, jnp.float32)
        l_sc[...] = jnp.zeros(l_sc.shape, jnp.float32)
        a_sc[...] = jnp.zeros(a_sc.shape, jnp.float32)

    @pl.when((j >= bounds_ref[0]) & (j <= bounds_ref[1]))
    def _():
        dims = (((1,), (1,)), ((), ()))
        kv = _key_tile(kv_ref)
        scores = lax.dot_general(q_ref[...], kv[:, :dh], dims,
                                 preferred_element_type=jnp.float32) * scaling
        allowed = _tile_mask(j, tk, rowpos_ref, rowdoc_ref, coldoc_ref)
        scores = jnp.where(allowed, scores, NEG_FILL)
        m_old = m_sc[...]
        m_new = jnp.maximum(m_old, jnp.max(scores, axis=1, keepdims=True))
        e = jnp.where(allowed, jnp.exp(scores - m_new), 0.0)
        gd = lax.dot_general(g_ref[...], kv[:, dh:], dims,
                             preferred_element_type=jnp.float32)
        alpha = jnp.exp(m_old - m_new)
        l_sc[...] = alpha * l_sc[...] + jnp.sum(e, axis=1, keepdims=True)
        a_sc[...] = alpha * a_sc[...] + jnp.sum(e * gd, axis=1, keepdims=True)
        m_sc[...] = m_new

    @pl.when(j == pl.num_programs(0) - 1)
    def _():
        lt_ref[...] = m_sc[...] + jnp.log(l_sc[...])
        delta_ref[...] = a_sc[...] / l_sc[...]


def _grad_kernel(scaling, tk, dh, bounds_ref, q_ref, g_ref, kv_ref, rowpos_ref, rowdoc_ref,
                 coldoc_ref, lt_ref, delta_ref, dq_ref, dkv_ref, dq_sc):
    j = pl.program_id(0)
    active = (j >= bounds_ref[0]) & (j <= bounds_ref[1])

    @pl.when(j == 0)
    def _():
        dq_sc[...] = jnp.zeros(dq_sc.shape, jnp.float32)

    @pl.when(active)
    def _():
        dims = (((1,), (1,)), ((), ()))
        tdims = (((0,), (0,)), ((), ()))
        kv = _key_tile(kv_ref)
        k_t = kv[:, :dh]
        scores = lax.dot_general(q_ref[...], k_t, dims,
                                 preferred_element_type=jnp.float32) * scaling
        allowed = _tile_mask(j, tk, rowpos_ref, rowdoc_ref, coldoc_ref)
        probs = jnp.where(allowed, jnp.exp(scores - lt_ref[...]), 0.0)
        gd = lax.dot_general(g_ref[...], kv[:, dh:], dims,
                             preferred_element_type=jnp.float32)
        ds = (probs * (gd - delta_ref[...]) * scaling).astype(jnp.bfloat16)
        dq_sc[...] += jnp.dot(ds, k_t, preferred_element_type=jnp.float32)
        dk = lax.dot_general(ds, q_ref[...], tdims, preferred_element_type=jnp.float32)
        dv = lax.dot_general(probs.astype(jnp.bfloat16), g_ref[...], tdims,
                             preferred_element_type=jnp.float32)
        owner_rows = dkv_ref.shape[3]
        for c in range(dkv_ref.shape[0]):
            part = slice(c * owner_rows, (c + 1) * owner_rows)
            dkv_ref[c, 0, 0, :, :dh] = dk[part].astype(dkv_ref.dtype)
            dkv_ref[c, 0, 0, :, dh:] = dv[part].astype(dkv_ref.dtype)

    @pl.when(jnp.logical_not(active))
    def _():
        dkv_ref[...] = jnp.zeros(dkv_ref.shape, dkv_ref.dtype)

    @pl.when(j == pl.num_programs(0) - 1)
    def _():
        dq_ref[...] = dq_sc[...].astype(dq_ref.dtype)


def attention_grads(q_rows, g_rows, kv_full, doc_starts, first_row, rows_here, scaling, chips):
    n_rows, dh = q_rows.shape
    n_keys = kv_full.shape[0] * kv_full.shape[1] * kv_full.shape[2] * kv_full.shape[3]
    n_zh, n_x, n_core = chips
    tk = n_core * rows_here
    n_tiles = n_keys // tk
    row_pos = first_row + jnp.arange(n_rows, dtype=jnp.int32) % rows_here
    row_doc = doc_index(doc_starts, row_pos)
    col_doc = doc_index(doc_starts, jnp.arange(n_keys, dtype=jnp.int32))[None, :]
    doc_first = jnp.max(jnp.where(doc_starts <= first_row, doc_starts, 0))
    bounds = jnp.stack([doc_first // tk, (first_row + rows_here - 1) // tk]).astype(jnp.int32)
    row_pos = row_pos[:, None]
    row_doc = row_doc[:, None]

    def tile_of(j, b):
        return jnp.minimum(jnp.maximum(j, b[0]), b[1])

    full = lambda shape: pl.BlockSpec(shape, lambda j, b: (0, 0))
    in_specs = [
        full((n_rows, dh)),
        full((n_rows, dh)),
        pl.BlockSpec((n_core, 1, 1, rows_here, 2 * dh),
                     lambda j, b: (0, tile_of(j, b) % n_x, tile_of(j, b) // n_x, 0, 0)),
        full((n_rows, 1)),
        full((n_rows, 1)),
        pl.BlockSpec((1, tk), lambda j, b: (0, tile_of(j, b))),
    ]
    params = pltpu.CompilerParams(dimension_semantics=("arbitrary",))
    mm = 2 * n_rows * n_keys * dh
    log_total, delta = pl.pallas_call(
        functools.partial(_stats_kernel, scaling, tk, dh),
        grid_spec=pltpu.PrefetchScalarGridSpec(
            num_scalar_prefetch=1,
            grid=(n_tiles,),
            in_specs=in_specs,
            out_specs=[full((n_rows, 1)), full((n_rows, 1))],
            scratch_shapes=[pltpu.VMEM((n_rows, 1), jnp.float32)] * 3,
        ),
        out_shape=[jax.ShapeDtypeStruct((n_rows, 1), jnp.float32)] * 2,
        compiler_params=params,
        cost_estimate=pl.CostEstimate(flops=2 * mm, transcendentals=n_rows * n_keys,
                                      bytes_accessed=n_keys * 4 * dh),
    )(bounds, q_rows, g_rows, kv_full, row_pos, row_doc, col_doc)
    dq, dkv = pl.pallas_call(
        functools.partial(_grad_kernel, scaling, tk, dh),
        grid_spec=pltpu.PrefetchScalarGridSpec(
            num_scalar_prefetch=1,
            grid=(n_tiles,),
            in_specs=in_specs + [full((n_rows, 1)), full((n_rows, 1))],
            out_specs=[
                full((n_rows, dh)),
                pl.BlockSpec((n_core, 1, 1, rows_here, 2 * dh),
                             lambda j, b: (0, j % n_x, j // n_x, 0, 0)),
            ],
            scratch_shapes=[pltpu.VMEM((n_rows, dh), jnp.float32)],
        ),
        out_shape=[jax.ShapeDtypeStruct((n_rows, dh), jnp.bfloat16),
                   jax.ShapeDtypeStruct((n_core, n_x, n_zh, rows_here, 2 * dh), jnp.bfloat16)],
        compiler_params=params,
        cost_estimate=pl.CostEstimate(flops=5 * mm, transcendentals=n_rows * n_keys,
                                      bytes_accessed=n_keys * 8 * dh),
    )(bounds, q_rows, g_rows, kv_full, row_pos, row_doc, col_doc, log_total, delta)
    return dq, dkv


def stage_reduce(parts, axis, cid):
    n = lax.axis_size(axis)
    me = lax.axis_index(axis)
    slots = peer_blocks(parts.astype(jnp.bfloat16), n, axis, None, True, cid)
    ids = jnp.arange(n, dtype=jnp.int32).reshape((n,) + (1,) * (parts.ndim - 1))
    others = jnp.sum(jnp.where(ids == me, 0.0, slots.astype(jnp.float32)), axis=0)
    return others + lax.dynamic_index_in_dim(parts, me, 0, keepdims=False).astype(jnp.float32)


def stage_gather(block, axis, cid):
    n = lax.axis_size(axis)
    me = lax.axis_index(axis)
    slots = peer_blocks(block, n, axis, None, False, cid)
    ids = jnp.arange(n, dtype=jnp.int32).reshape((n,) + (1,) * block.ndim)
    return jnp.where(ids == me, block[None], slots)


def shards(queries, keys, values, d_out, w_out, doc_starts):
    rows_here = queries.shape[0]
    head_size = DH
    groups = keys.shape[1] // head_size
    per_group = queries.shape[1] // keys.shape[1]
    kv_cols = keys.shape[1]
    scaling = 1.0 / math.sqrt(head_size)
    n_zh = lax.axis_size("zhi")
    n_x = lax.axis_size("xx")
    n_core = lax.axis_size("core")
    me = (lax.axis_index("zhi") * n_x + lax.axis_index("xx")) * n_core + lax.axis_index("core")
    first_row = me * rows_here
    my_rows = first_row + jnp.arange(rows_here, dtype=jnp.int32)
    kv_block = jnp.concatenate([keys, values], axis=1)
    for cid, axis in enumerate(("zhi", "xx", "core")):
        kv_block = stage_gather(kv_block, axis, cid + 4)
    n_head = lax.axis_size("head")
    me_head = lax.axis_index("head")
    d_slots = peer_blocks(d_out, n_head, "head", None, False, 0)
    head_ids = jnp.arange(n_head, dtype=jnp.int32)[:, None, None]
    d_all = jnp.where(head_ids == me_head, d_out[None], d_slots)
    attn_grad = jnp.einsum(
        "hte,che->tc",
        d_all,
        w_out.reshape(w_out.shape[0], n_head, d_out.shape[1]),
        preferred_element_type=jnp.float32,
    ).astype(jnp.bfloat16)
    heads = groups * per_group
    q_rows = queries.reshape(rows_here, heads, head_size).transpose(1, 0, 2).reshape(
        heads * rows_here, head_size)
    g_rows = attn_grad.reshape(rows_here, heads, head_size).transpose(1, 0, 2).reshape(
        heads * rows_here, head_size)
    dq_rows, kv_terms = attention_grads(
        q_rows, g_rows, kv_block, doc_starts, first_row, rows_here, scaling,
        (n_zh, n_x, n_core))
    query_grad = dq_rows.reshape(heads, rows_here, head_size).transpose(1, 0, 2).reshape(
        rows_here, heads * head_size)
    kv_grad = kv_terms
    for cid, axis in enumerate(("core", "xx", "zhi")):
        kv_grad = stage_reduce(kv_grad, axis, cid + 1)
    kv_grad = kv_grad.astype(jnp.bfloat16)
    key_grad = kv_grad[:, :kv_cols]
    value_grad = kv_grad[:, kv_cols:]
    return (query_grad, key_grad, value_grad)


def solution(mesh):
    n_seq, n_head = mesh.shape["seq"], mesh.shape["head"]
    split = jax.sharding.Mesh(
        mesh.devices.reshape(n_seq // 8, 4, 2, n_head), ("zhi", "xx", "core", "head")
    )
    rows = ("zhi", "xx", "core")
    return jax.shard_map(
        shards,
        mesh=split,
        in_specs=(
            P(rows, "head"),
            P(rows, "head"),
            P(rows, "head"),
            P(rows, "head"),
            P("head", None),
            P(),
        ),
        out_specs=(P(rows, "head"), P(rows, "head"), P(rows, "head")),
        check_vma=False,
    )
```

```python
import functools
import math

import jax
import jax.numpy as jnp
from jax import lax
from jax.sharding import PartitionSpec as P
from jax.experimental import pallas as pl
from jax.experimental.pallas import tpu as pltpu

DH = 128


NEG_FILL = -1e30


def doc_index(doc_starts, places):
    return jnp.sum((places[:, None] >= doc_starts[None, :]).astype(jnp.int32), axis=1)


def allowed_pairs(doc_starts, row_ids, col_ids):
    earlier = col_ids[None, :] <= row_ids[:, None]
    same_doc = doc_index(doc_starts, row_ids)[:, None] == doc_index(doc_starts, col_ids)[None, :]
    return (earlier & same_doc)[None, None]


def _peer_kernel(n, axis, upward, per_target, src_ref, out_ref, send_sem, recv_sem):
    me = lax.axis_index(axis)
    barrier = pltpu.get_barrier_semaphore()

    def greet(k, carry):
        pl.semaphore_signal(barrier, 1, device_id={axis: lax.rem(me + k, n)},
                            device_id_type=pl.DeviceIdType.MESH)
        return carry

    lax.fori_loop(1, n, greet, 0)
    pl.semaphore_wait(barrier, n - 1)
    step = -1 if upward is False else 1

    def send_desc(k):
        tgt = lax.rem(me + k, n) if upward is None else me + step * k
        src = src_ref.at[tgt] if per_target else src_ref
        return pltpu.make_async_remote_copy(
            src, out_ref.at[me], send_sem.at[k - 1], recv_sem.at[k - 1],
            device_id={axis: tgt}, device_id_type=pl.DeviceIdType.MESH)

    def recv_desc(k):
        origin = lax.rem(me + n - k, n) if upward is None else me - step * k
        src = src_ref.at[me] if per_target else src_ref
        return pltpu.make_async_remote_copy(
            src, out_ref.at[origin], send_sem.at[k - 1], recv_sem.at[k - 1],
            device_id={axis: origin}, device_id_type=pl.DeviceIdType.MESH)

    def can_send(k):
        if upward is None:
            return k > 0
        return (me + k < n) if upward else (me - k >= 0)

    def can_recv(k):
        if upward is None:
            return k > 0
        return (me - k >= 0) if upward else (me + k < n)

    def start_one(k, carry):
        @pl.when(can_send(k))
        def _():
            send_desc(k).start()
        return carry

    def finish_one(k, carry):
        @pl.when(can_send(k))
        def _():
            send_desc(k).wait_send()

        @pl.when(can_recv(k))
        def _():
            recv_desc(k).wait_recv()
        return carry

    lax.fori_loop(1, n, start_one, 0)
    lax.fori_loop(1, n, finish_one, 0)


def peer_blocks(src, n, axis, upward, per_target, cid):
    blk = src.shape[1:] if per_target else src.shape
    return pl.pallas_call(
        functools.partial(_peer_kernel, n, axis, upward, per_target),
        out_shape=jax.ShapeDtypeStruct((n,) + tuple(blk), src.dtype),
        in_specs=[pl.BlockSpec(memory_space=pl.ANY)],
        out_specs=pl.BlockSpec(memory_space=pl.ANY),
        scratch_shapes=[pltpu.SemaphoreType.DMA((n - 1,)), pltpu.SemaphoreType.DMA((n - 1,))],
        compiler_params=pltpu.CompilerParams(collective_id=cid, has_side_effects=True),
    )(src)


def _tile_mask(j, tk, rowpos_ref, rowdoc_ref, coldoc_ref):
    col = j * tk + lax.broadcasted_iota(jnp.int32, (1, tk), 1)
    return (col <= rowpos_ref[...]) & (coldoc_ref[...] == rowdoc_ref[...])


def _key_tile(kv_ref):
    return jnp.concatenate([kv_ref[c, 0, 0] for c in range(kv_ref.shape[0])], axis=0)


def _stats_kernel(scaling, tk, dh, bounds_ref, q_ref, g_ref, kv_ref, rowpos_ref, rowdoc_ref,
                  coldoc_ref, lt_ref, delta_ref, m_sc, l_sc, a_sc):
    j = pl.program_id(0)

    @pl.when(j == 0)
    def _():
        m_sc[...] = jnp.full(m_sc.shape, NEG_FILL, jnp.float32)
        l_sc[...] = jnp.zeros(l_sc.shape, jnp.float32)
        a_sc[...] = jnp.zeros(a_sc.shape, jnp.float32)

    @pl.when((j >= bounds_ref[0]) & (j <= bounds_ref[1]))
    def _():
        dims = (((1,), (1,)), ((), ()))
        kv = _key_tile(kv_ref)
        scores = lax.dot_general(q_ref[...], kv[:, :dh], dims,
                                 preferred_element_type=jnp.float32) * scaling
        allowed = _tile_mask(j, tk, rowpos_ref, rowdoc_ref, coldoc_ref)
        scores = jnp.where(allowed, scores, NEG_FILL)
        m_old = m_sc[...]
        m_new = jnp.maximum(m_old, jnp.max(scores, axis=1, keepdims=True))
        e = jnp.where(allowed, jnp.exp(scores - m_new), 0.0)
        gd = lax.dot_general(g_ref[...], kv[:, dh:], dims,
                             preferred_element_type=jnp.float32)
        alpha = jnp.exp(m_old - m_new)
        l_sc[...] = alpha * l_sc[...] + jnp.sum(e, axis=1, keepdims=True)
        a_sc[...] = alpha * a_sc[...] + jnp.sum(e * gd, axis=1, keepdims=True)
        m_sc[...] = m_new

    @pl.when(j == pl.num_programs(0) - 1)
    def _():
        lt_ref[...] = m_sc[...] + jnp.log(l_sc[...])
        delta_ref[...] = a_sc[...] / l_sc[...]


def _grad_kernel(scaling, tk, dh, bounds_ref, q_ref, g_ref, kv_ref, rowpos_ref, rowdoc_ref,
                 coldoc_ref, lt_ref, delta_ref, dq_ref, dkv_ref, dq_sc):
    j = pl.program_id(0)
    active = (j >= bounds_ref[0]) & (j <= bounds_ref[1])

    @pl.when(j == 0)
    def _():
        dq_sc[...] = jnp.zeros(dq_sc.shape, jnp.float32)

    @pl.when(active)
    def _():
        dims = (((1,), (1,)), ((), ()))
        tdims = (((0,), (0,)), ((), ()))
        kv = _key_tile(kv_ref)
        k_t = kv[:, :dh]
        scores = lax.dot_general(q_ref[...], k_t, dims,
                                 preferred_element_type=jnp.float32) * scaling
        allowed = _tile_mask(j, tk, rowpos_ref, rowdoc_ref, coldoc_ref)
        probs = jnp.where(allowed, jnp.exp(scores - lt_ref[...]), 0.0)
        gd = lax.dot_general(g_ref[...], kv[:, dh:], dims,
                             preferred_element_type=jnp.float32)
        ds = (probs * (gd - delta_ref[...]) * scaling).astype(jnp.bfloat16)
        dq_sc[...] += jnp.dot(ds, k_t, preferred_element_type=jnp.float32)
        dk = lax.dot_general(ds, q_ref[...], tdims, preferred_element_type=jnp.float32)
        dv = lax.dot_general(probs.astype(jnp.bfloat16), g_ref[...], tdims,
                             preferred_element_type=jnp.float32)
        owner_rows = dkv_ref.shape[3]
        for c in range(dkv_ref.shape[0]):
            part = slice(c * owner_rows, (c + 1) * owner_rows)
            dkv_ref[c, 0, 0, :, :dh] = dk[part].astype(dkv_ref.dtype)
            dkv_ref[c, 0, 0, :, dh:] = dv[part].astype(dkv_ref.dtype)

    @pl.when(jnp.logical_not(active))
    def _():
        dkv_ref[...] = jnp.zeros(dkv_ref.shape, dkv_ref.dtype)

    @pl.when(j == pl.num_programs(0) - 1)
    def _():
        dq_ref[...] = dq_sc[...].astype(dq_ref.dtype)


def attention_grads(q_rows, g_rows, kv_full, doc_starts, first_row, rows_here, scaling, chips):
    n_rows, dh = q_rows.shape
    n_keys = kv_full.shape[0] * kv_full.shape[1] * kv_full.shape[2] * kv_full.shape[3]
    n_zh, n_x, n_core = chips
    tk = n_core * rows_here
    n_tiles = n_keys // tk
    row_pos = first_row + jnp.arange(n_rows, dtype=jnp.int32) % rows_here
    row_doc = doc_index(doc_starts, row_pos)
    col_doc = doc_index(doc_starts, jnp.arange(n_keys, dtype=jnp.int32))[None, :]
    doc_first = jnp.max(jnp.where(doc_starts <= first_row, doc_starts, 0))
    bounds = jnp.stack([doc_first // tk, (first_row + rows_here - 1) // tk]).astype(jnp.int32)
    row_pos = row_pos[:, None]
    row_doc = row_doc[:, None]

    def tile_of(j, b):
        return jnp.minimum(jnp.maximum(j, b[0]), b[1])

    full = lambda shape: pl.BlockSpec(shape, lambda j, b: (0, 0))
    in_specs = [
        full((n_rows, dh)),
        full((n_rows, dh)),
        pl.BlockSpec((n_core, 1, 1, rows_here, 2 * dh),
                     lambda j, b: (0, tile_of(j, b) % n_x, tile_of(j, b) // n_x, 0, 0)),
        full((n_rows, 1)),
        full((n_rows, 1)),
        pl.BlockSpec((1, tk), lambda j, b: (0, tile_of(j, b))),
    ]
    params = pltpu.CompilerParams(dimension_semantics=("arbitrary",))
    mm = 2 * n_rows * n_keys * dh
    log_total, delta = pl.pallas_call(
        functools.partial(_stats_kernel, scaling, tk, dh),
        grid_spec=pltpu.PrefetchScalarGridSpec(
            num_scalar_prefetch=1,
            grid=(n_tiles,),
            in_specs=in_specs,
            out_specs=[full((n_rows, 1)), full((n_rows, 1))],
            scratch_shapes=[pltpu.VMEM((n_rows, 1), jnp.float32)] * 3,
        ),
        out_shape=[jax.ShapeDtypeStruct((n_rows, 1), jnp.float32)] * 2,
        compiler_params=params,
        cost_estimate=pl.CostEstimate(flops=2 * mm, transcendentals=n_rows * n_keys,
                                      bytes_accessed=n_keys * 4 * dh),
    )(bounds, q_rows, g_rows, kv_full, row_pos, row_doc, col_doc)
    dq, dkv = pl.pallas_call(
        functools.partial(_grad_kernel, scaling, tk, dh),
        grid_spec=pltpu.PrefetchScalarGridSpec(
            num_scalar_prefetch=1,
            grid=(n_tiles,),
            in_specs=in_specs + [full((n_rows, 1)), full((n_rows, 1))],
            out_specs=[
                full((n_rows, dh)),
                pl.BlockSpec((n_core, 1, 1, rows_here, 2 * dh),
                             lambda j, b: (0, j % n_x, j // n_x, 0, 0)),
            ],
            scratch_shapes=[pltpu.VMEM((n_rows, dh), jnp.float32)],
        ),
        out_shape=[jax.ShapeDtypeStruct((n_rows, dh), jnp.bfloat16),
                   jax.ShapeDtypeStruct((n_core, n_x, n_zh, rows_here, 2 * dh), jnp.bfloat16)],
        compiler_params=params,
        cost_estimate=pl.CostEstimate(flops=5 * mm, transcendentals=n_rows * n_keys,
                                      bytes_accessed=n_keys * 8 * dh),
    )(bounds, q_rows, g_rows, kv_full, row_pos, row_doc, col_doc, log_total, delta)
    return dq, dkv


def stage_reduce(parts, axis, cid):
    n = lax.axis_size(axis)
    me = lax.axis_index(axis)
    slots = peer_blocks(parts.astype(jnp.bfloat16), n, axis, None, True, cid)
    ids = jnp.arange(n, dtype=jnp.int32).reshape((n,) + (1,) * (parts.ndim - 1))
    others = jnp.sum(jnp.where(ids == me, 0.0, slots.astype(jnp.float32)), axis=0)
    return others + lax.dynamic_index_in_dim(parts, me, 0, keepdims=False).astype(jnp.float32)


def stage_gather(block, axis, cid):
    n = lax.axis_size(axis)
    me = lax.axis_index(axis)
    slots = peer_blocks(block, n, axis, None, False, cid)
    ids = jnp.arange(n, dtype=jnp.int32).reshape((n,) + (1,) * block.ndim)
    return jnp.where(ids == me, block[None], slots)


def _multi_kernel(groups, *refs):
    n_groups = len(groups)
    srcs, outs = refs[:n_groups], refs[n_groups:2 * n_groups]
    send_sems, recv_sems = refs[2 * n_groups:3 * n_groups], refs[3 * n_groups:]
    barrier = pltpu.get_barrier_semaphore()
    for n, axis in groups:
        me = lax.axis_index(axis)

        def greet(k, carry, n=n, axis=axis, me=me):
            pl.semaphore_signal(barrier, 1, device_id={axis: lax.rem(me + k, n)},
                                device_id_type=pl.DeviceIdType.MESH)
            return carry

        lax.fori_loop(1, n, greet, 0)
    pl.semaphore_wait(barrier, sum(n - 1 for n, _ in groups))

    def desc(g, k, sending):
        n, axis = groups[g]
        me = lax.axis_index(axis)
        peer = lax.rem(me + k, n) if sending else lax.rem(me + n - k, n)
        slot = me if sending else peer
        return pltpu.make_async_remote_copy(
            srcs[g], outs[g].at[slot], send_sems[g].at[k - 1], recv_sems[g].at[k - 1],
            device_id={axis: peer}, device_id_type=pl.DeviceIdType.MESH)

    for g, (n, _) in enumerate(groups):
        def start_one(k, carry, g=g):
            desc(g, k, True).start()
            return carry

        lax.fori_loop(1, n, start_one, 0)
    for g, (n, _) in enumerate(groups):
        def finish_one(k, carry, g=g):
            desc(g, k, True).wait_send()
            desc(g, k, False).wait_recv()
            return carry

        lax.fori_loop(1, n, finish_one, 0)


def gather_many(blocks, cid):
    groups = tuple((lax.axis_size(axis), axis) for _, axis in blocks)
    srcs = [b for b, _ in blocks]
    slots = pl.pallas_call(
        functools.partial(_multi_kernel, groups),
        out_shape=[jax.ShapeDtypeStruct((n,) + b.shape, b.dtype) for b, (n, _) in zip(srcs, groups)],
        in_specs=[pl.BlockSpec(memory_space=pl.ANY)] * len(srcs),
        out_specs=[pl.BlockSpec(memory_space=pl.ANY)] * len(srcs),
        scratch_shapes=[pltpu.SemaphoreType.DMA((n - 1,)) for n, _ in groups] * 2,
        compiler_params=pltpu.CompilerParams(collective_id=cid, has_side_effects=True),
    )(*srcs)
    result = []
    for b, (n, axis), s in zip(srcs, groups, slots):
        ids = jnp.arange(n, dtype=jnp.int32).reshape((n,) + (1,) * b.ndim)
        result.append(jnp.where(ids == lax.axis_index(axis), b[None], s))
    return result


def shards(queries, keys, values, d_out, w_out, doc_starts):
    rows_here = queries.shape[0]
    head_size = DH
    groups = keys.shape[1] // head_size
    per_group = queries.shape[1] // keys.shape[1]
    kv_cols = keys.shape[1]
    scaling = 1.0 / math.sqrt(head_size)
    n_zh = lax.axis_size("zhi")
    n_x = lax.axis_size("xx")
    n_core = lax.axis_size("core")
    me = (lax.axis_index("zhi") * n_x + lax.axis_index("xx")) * n_core + lax.axis_index("core")
    first_row = me * rows_here
    my_rows = first_row + jnp.arange(rows_here, dtype=jnp.int32)
    n_head = lax.axis_size("head")
    d_all, kv_block = gather_many(
        [(d_out, "head"), (jnp.concatenate([keys, values], axis=1), "zhi")], 0)
    for cid, axis in enumerate(("xx", "core")):
        kv_block = stage_gather(kv_block, axis, cid + 4)
    attn_grad = jnp.einsum(
        "hte,che->tc",
        d_all,
        w_out.reshape(w_out.shape[0], n_head, d_out.shape[1]),
        preferred_element_type=jnp.float32,
    ).astype(jnp.bfloat16)
    heads = groups * per_group
    q_rows = queries.reshape(rows_here, heads, head_size).transpose(1, 0, 2).reshape(
        heads * rows_here, head_size)
    g_rows = attn_grad.reshape(rows_here, heads, head_size).transpose(1, 0, 2).reshape(
        heads * rows_here, head_size)
    dq_rows, kv_terms = attention_grads(
        q_rows, g_rows, kv_block, doc_starts, first_row, rows_here, scaling,
        (n_zh, n_x, n_core))
    query_grad = dq_rows.reshape(heads, rows_here, head_size).transpose(1, 0, 2).reshape(
        rows_here, heads * head_size)
    kv_grad = kv_terms
    for cid, axis in enumerate(("core", "xx", "zhi")):
        kv_grad = stage_reduce(kv_grad, axis, cid + 1)
    kv_grad = kv_grad.astype(jnp.bfloat16)
    key_grad = kv_grad[:, :kv_cols]
    value_grad = kv_grad[:, kv_cols:]
    return (query_grad, key_grad, value_grad)


def solution(mesh):
    n_seq, n_head = mesh.shape["seq"], mesh.shape["head"]
    split = jax.sharding.Mesh(
        mesh.devices.reshape(n_seq // 8, 4, 2, n_head), ("zhi", "xx", "core", "head")
    )
    rows = ("zhi", "xx", "core")
    return jax.shard_map(
        shards,
        mesh=split,
        in_specs=(
            P(rows, "head"),
            P(rows, "head"),
            P(rows, "head"),
            P(rows, "head"),
            P("head", None),
            P(),
        ),
        out_specs=(P(rows, "head"), P(rows, "head"), P(rows, "head")),
        check_vma=False,
    )
```

```python
import functools
import math

import jax
import jax.numpy as jnp
from jax import lax
from jax.sharding import PartitionSpec as P
from jax.experimental import pallas as pl
from jax.experimental.pallas import tpu as pltpu

DH = 128


NEG_FILL = -1e30


def doc_index(doc_starts, places):
    return jnp.sum((places[:, None] >= doc_starts[None, :]).astype(jnp.int32), axis=1)


def allowed_pairs(doc_starts, row_ids, col_ids):
    earlier = col_ids[None, :] <= row_ids[:, None]
    same_doc = doc_index(doc_starts, row_ids)[:, None] == doc_index(doc_starts, col_ids)[None, :]
    return (earlier & same_doc)[None, None]


def _peer_kernel(n, axis, upward, per_target, src_ref, out_ref, send_sem, recv_sem):
    me = lax.axis_index(axis)
    barrier = pltpu.get_barrier_semaphore()

    def greet(k, carry):
        pl.semaphore_signal(barrier, 1, device_id={axis: lax.rem(me + k, n)},
                            device_id_type=pl.DeviceIdType.MESH)
        return carry

    lax.fori_loop(1, n, greet, 0)
    pl.semaphore_wait(barrier, n - 1)
    step = -1 if upward is False else 1

    def send_desc(k):
        tgt = lax.rem(me + k, n) if upward is None else me + step * k
        src = src_ref.at[tgt] if per_target else src_ref
        return pltpu.make_async_remote_copy(
            src, out_ref.at[me], send_sem.at[k - 1], recv_sem.at[k - 1],
            device_id={axis: tgt}, device_id_type=pl.DeviceIdType.MESH)

    def recv_desc(k):
        origin = lax.rem(me + n - k, n) if upward is None else me - step * k
        src = src_ref.at[me] if per_target else src_ref
        return pltpu.make_async_remote_copy(
            src, out_ref.at[origin], send_sem.at[k - 1], recv_sem.at[k - 1],
            device_id={axis: origin}, device_id_type=pl.DeviceIdType.MESH)

    def can_send(k):
        if upward is None:
            return k > 0
        return (me + k < n) if upward else (me - k >= 0)

    def can_recv(k):
        if upward is None:
            return k > 0
        return (me - k >= 0) if upward else (me + k < n)

    def start_one(k, carry):
        @pl.when(can_send(k))
        def _():
            send_desc(k).start()
        return carry

    def finish_one(k, carry):
        @pl.when(can_send(k))
        def _():
            send_desc(k).wait_send()

        @pl.when(can_recv(k))
        def _():
            recv_desc(k).wait_recv()
        return carry

    lax.fori_loop(1, n, start_one, 0)
    lax.fori_loop(1, n, finish_one, 0)


def peer_blocks(src, n, axis, upward, per_target, cid):
    blk = src.shape[1:] if per_target else src.shape
    return pl.pallas_call(
        functools.partial(_peer_kernel, n, axis, upward, per_target),
        out_shape=jax.ShapeDtypeStruct((n,) + tuple(blk), src.dtype),
        in_specs=[pl.BlockSpec(memory_space=pl.ANY)],
        out_specs=pl.BlockSpec(memory_space=pl.ANY),
        scratch_shapes=[pltpu.SemaphoreType.DMA((n - 1,)), pltpu.SemaphoreType.DMA((n - 1,))],
        compiler_params=pltpu.CompilerParams(collective_id=cid, has_side_effects=True),
    )(src)


def _tile_mask(j, tk, rowpos_ref, rowdoc_ref, coldoc_ref):
    col = j * tk + lax.broadcasted_iota(jnp.int32, (1, tk), 1)
    return (col <= rowpos_ref[...]) & (coldoc_ref[...] == rowdoc_ref[...])


def _key_tile(kv_ref):
    return jnp.concatenate([kv_ref[c, 0, 0] for c in range(kv_ref.shape[0])], axis=0)


def _stats_kernel(scaling, tk, dh, bounds_ref, q_ref, g_ref, kv_ref, rowpos_ref, rowdoc_ref,
                  coldoc_ref, lt_ref, delta_ref, m_sc, l_sc, a_sc):
    j = pl.program_id(0)

    @pl.when(j == 0)
    def _():
        m_sc[...] = jnp.full(m_sc.shape, NEG_FILL, jnp.float32)
        l_sc[...] = jnp.zeros(l_sc.shape, jnp.float32)
        a_sc[...] = jnp.zeros(a_sc.shape, jnp.float32)

    @pl.when((j >= bounds_ref[0]) & (j <= bounds_ref[1]))
    def _():
        dims = (((1,), (1,)), ((), ()))
        kv = _key_tile(kv_ref)
        scores = lax.dot_general(q_ref[...], kv[:, :dh], dims,
                                 preferred_element_type=jnp.float32) * scaling
        allowed = _tile_mask(j, tk, rowpos_ref, rowdoc_ref, coldoc_ref)
        scores = jnp.where(allowed, scores, NEG_FILL)
        m_old = m_sc[...]
        m_new = jnp.maximum(m_old, jnp.max(scores, axis=1, keepdims=True))
        e = jnp.where(allowed, jnp.exp(scores - m_new), 0.0)
        gd = lax.dot_general(g_ref[...], kv[:, dh:], dims,
                             preferred_element_type=jnp.float32)
        alpha = jnp.exp(m_old - m_new)
        l_sc[...] = alpha * l_sc[...] + jnp.sum(e, axis=1, keepdims=True)
        a_sc[...] = alpha * a_sc[...] + jnp.sum(e * gd, axis=1, keepdims=True)
        m_sc[...] = m_new

    @pl.when(j == pl.num_programs(0) - 1)
    def _():
        lt_ref[...] = m_sc[...] + jnp.log(l_sc[...])
        delta_ref[...] = a_sc[...] / l_sc[...]


def _grad_kernel(scaling, tk, dh, bounds_ref, q_ref, g_ref, kv_ref, rowpos_ref, rowdoc_ref,
                 coldoc_ref, lt_ref, delta_ref, dq_ref, dkv_ref, dq_sc):
    j = pl.program_id(0)
    active = (j >= bounds_ref[0]) & (j <= bounds_ref[1])

    @pl.when(j == 0)
    def _():
        dq_sc[...] = jnp.zeros(dq_sc.shape, jnp.float32)

    @pl.when(active)
    def _():
        dims = (((1,), (1,)), ((), ()))
        tdims = (((0,), (0,)), ((), ()))
        kv = _key_tile(kv_ref)
        k_t = kv[:, :dh]
        scores = lax.dot_general(q_ref[...], k_t, dims,
                                 preferred_element_type=jnp.float32) * scaling
        allowed = _tile_mask(j, tk, rowpos_ref, rowdoc_ref, coldoc_ref)
        probs = jnp.where(allowed, jnp.exp(scores - lt_ref[...]), 0.0)
        gd = lax.dot_general(g_ref[...], kv[:, dh:], dims,
                             preferred_element_type=jnp.float32)
        ds = (probs * (gd - delta_ref[...]) * scaling).astype(jnp.bfloat16)
        dq_sc[...] += jnp.dot(ds, k_t, preferred_element_type=jnp.float32)
        dk = lax.dot_general(ds, q_ref[...], tdims, preferred_element_type=jnp.float32)
        dv = lax.dot_general(probs.astype(jnp.bfloat16), g_ref[...], tdims,
                             preferred_element_type=jnp.float32)
        owner_rows = dkv_ref.shape[3]
        for c in range(dkv_ref.shape[0]):
            part = slice(c * owner_rows, (c + 1) * owner_rows)
            dkv_ref[c, 0, 0, :, :dh] = dk[part].astype(dkv_ref.dtype)
            dkv_ref[c, 0, 0, :, dh:] = dv[part].astype(dkv_ref.dtype)

    @pl.when(jnp.logical_not(active))
    def _():
        dkv_ref[...] = jnp.zeros(dkv_ref.shape, dkv_ref.dtype)

    @pl.when(j == pl.num_programs(0) - 1)
    def _():
        dq_ref[...] = dq_sc[...].astype(dq_ref.dtype)


def attention_grads(q_rows, g_rows, kv_full, doc_starts, first_row, rows_here, scaling, chips):
    n_rows, dh = q_rows.shape
    n_keys = kv_full.shape[0] * kv_full.shape[1] * kv_full.shape[2] * kv_full.shape[3]
    n_zh, n_x, n_core = chips
    tk = n_core * rows_here
    n_tiles = n_keys // tk
    row_pos = first_row + jnp.arange(n_rows, dtype=jnp.int32) % rows_here
    row_doc = doc_index(doc_starts, row_pos)
    col_doc = doc_index(doc_starts, jnp.arange(n_keys, dtype=jnp.int32))[None, :]
    doc_first = jnp.max(jnp.where(doc_starts <= first_row, doc_starts, 0))
    bounds = jnp.stack([doc_first // tk, (first_row + rows_here - 1) // tk]).astype(jnp.int32)
    row_pos = row_pos[:, None]
    row_doc = row_doc[:, None]

    def tile_of(j, b):
        return jnp.minimum(jnp.maximum(j, b[0]), b[1])

    full = lambda shape: pl.BlockSpec(shape, lambda j, b: (0, 0))
    in_specs = [
        full((n_rows, dh)),
        full((n_rows, dh)),
        pl.BlockSpec((n_core, 1, 1, rows_here, 2 * dh),
                     lambda j, b: (0, tile_of(j, b) % n_x, tile_of(j, b) // n_x, 0, 0)),
        full((n_rows, 1)),
        full((n_rows, 1)),
        pl.BlockSpec((1, tk), lambda j, b: (0, tile_of(j, b))),
    ]
    params = pltpu.CompilerParams(dimension_semantics=("arbitrary",))
    mm = 2 * n_rows * n_keys * dh
    log_total, delta = pl.pallas_call(
        functools.partial(_stats_kernel, scaling, tk, dh),
        grid_spec=pltpu.PrefetchScalarGridSpec(
            num_scalar_prefetch=1,
            grid=(n_tiles,),
            in_specs=in_specs,
            out_specs=[full((n_rows, 1)), full((n_rows, 1))],
            scratch_shapes=[pltpu.VMEM((n_rows, 1), jnp.float32)] * 3,
        ),
        out_shape=[jax.ShapeDtypeStruct((n_rows, 1), jnp.float32)] * 2,
        compiler_params=params,
        cost_estimate=pl.CostEstimate(flops=2 * mm, transcendentals=n_rows * n_keys,
                                      bytes_accessed=n_keys * 4 * dh),
    )(bounds, q_rows, g_rows, kv_full, row_pos, row_doc, col_doc)
    dq, dkv = pl.pallas_call(
        functools.partial(_grad_kernel, scaling, tk, dh),
        grid_spec=pltpu.PrefetchScalarGridSpec(
            num_scalar_prefetch=1,
            grid=(n_tiles,),
            in_specs=in_specs + [full((n_rows, 1)), full((n_rows, 1))],
            out_specs=[
                full((n_rows, dh)),
                pl.BlockSpec((n_core, 1, 1, rows_here, 2 * dh),
                             lambda j, b: (0, j % n_x, j // n_x, 0, 0)),
            ],
            scratch_shapes=[pltpu.VMEM((n_rows, dh), jnp.float32)],
        ),
        out_shape=[jax.ShapeDtypeStruct((n_rows, dh), jnp.bfloat16),
                   jax.ShapeDtypeStruct((n_core, n_x, n_zh, rows_here, 2 * dh), jnp.bfloat16)],
        compiler_params=params,
        cost_estimate=pl.CostEstimate(flops=5 * mm, transcendentals=n_rows * n_keys,
                                      bytes_accessed=n_keys * 8 * dh),
    )(bounds, q_rows, g_rows, kv_full, row_pos, row_doc, col_doc, log_total, delta)
    return dq, dkv


def stage_reduce(parts, axis, cid):
    n = lax.axis_size(axis)
    me = lax.axis_index(axis)
    slots = peer_blocks(parts.astype(jnp.bfloat16), n, axis, None, True, cid)
    ids = jnp.arange(n, dtype=jnp.int32).reshape((n,) + (1,) * (parts.ndim - 1))
    others = jnp.sum(jnp.where(ids == me, 0.0, slots.astype(jnp.float32)), axis=0)
    return others + lax.dynamic_index_in_dim(parts, me, 0, keepdims=False).astype(jnp.float32)


def stage_gather(block, axis, cid):
    n = lax.axis_size(axis)
    me = lax.axis_index(axis)
    slots = peer_blocks(block, n, axis, None, False, cid)
    ids = jnp.arange(n, dtype=jnp.int32).reshape((n,) + (1,) * block.ndim)
    return jnp.where(ids == me, block[None], slots)


def shards(queries, keys, values, d_out, w_out, doc_starts):
    rows_here = queries.shape[0]
    head_size = DH
    groups = keys.shape[1] // head_size
    per_group = queries.shape[1] // keys.shape[1]
    kv_cols = keys.shape[1]
    scaling = 1.0 / math.sqrt(head_size)
    n_zh = lax.axis_size("zhi")
    n_x = lax.axis_size("xx")
    n_core = lax.axis_size("core")
    me = (lax.axis_index("zhi") * n_x + lax.axis_index("xx")) * n_core + lax.axis_index("core")
    first_row = me * rows_here
    my_rows = first_row + jnp.arange(rows_here, dtype=jnp.int32)
    kv_block = jnp.concatenate([keys, values], axis=1)
    for cid, axis in enumerate(("zhi", "xx", "core")):
        kv_block = stage_gather(kv_block, axis, cid + 4)
    attn_grad = lax.dot_general(
        lax.all_gather(d_out, "head", axis=1, tiled=True),
        w_out,
        (((1,), (1,)), ((), ())),
        preferred_element_type=jnp.float32,
    ).astype(jnp.bfloat16)
    heads = groups * per_group
    q_rows = queries.reshape(rows_here, heads, head_size).transpose(1, 0, 2).reshape(
        heads * rows_here, head_size)
    g_rows = attn_grad.reshape(rows_here, heads, head_size).transpose(1, 0, 2).reshape(
        heads * rows_here, head_size)
    dq_rows, kv_terms = attention_grads(
        q_rows, g_rows, kv_block, doc_starts, first_row, rows_here, scaling,
        (n_zh, n_x, n_core))
    query_grad = dq_rows.reshape(heads, rows_here, head_size).transpose(1, 0, 2).reshape(
        rows_here, heads * head_size)
    kv_grad = kv_terms
    for cid, axis in enumerate(("core", "xx", "zhi")):
        kv_grad = stage_reduce(kv_grad, axis, cid + 1)
    kv_grad = kv_grad.astype(jnp.bfloat16)
    key_grad = kv_grad[:, :kv_cols]
    value_grad = kv_grad[:, kv_cols:]
    return (query_grad, key_grad, value_grad)


def solution(mesh):
    n_seq, n_head = mesh.shape["seq"], mesh.shape["head"]
    split = jax.sharding.Mesh(
        mesh.devices.reshape(n_seq // 8, 4, 2, n_head), ("zhi", "xx", "core", "head")
    )
    rows = ("zhi", "xx", "core")
    return jax.shard_map(
        shards,
        mesh=split,
        in_specs=(
            P(rows, "head"),
            P(rows, "head"),
            P(rows, "head"),
            P(rows, "head"),
            P("head", None),
            P(),
        ),
        out_specs=(P(rows, "head"), P(rows, "head"), P(rows, "head")),
        check_vma=False,
    )
```

```python
import functools
import math

import jax
import jax.numpy as jnp
from jax import lax
from jax.sharding import PartitionSpec as P
from jax.experimental import pallas as pl
from jax.experimental.pallas import tpu as pltpu

DH = 128


NEG_FILL = -1e30


def doc_index(doc_starts, places):
    return jnp.sum((places[:, None] >= doc_starts[None, :]).astype(jnp.int32), axis=1)


def allowed_pairs(doc_starts, row_ids, col_ids):
    earlier = col_ids[None, :] <= row_ids[:, None]
    same_doc = doc_index(doc_starts, row_ids)[:, None] == doc_index(doc_starts, col_ids)[None, :]
    return (earlier & same_doc)[None, None]


def _peer_kernel(n, axis, upward, per_target, src_ref, out_ref, send_sem, recv_sem, own_sem):
    me = lax.axis_index(axis)
    own = None
    if not per_target:
        own = pltpu.make_async_copy(src_ref, out_ref.at[me], own_sem)
        own.start()
    barrier = pltpu.get_barrier_semaphore()

    def greet(k, carry):
        pl.semaphore_signal(barrier, 1, device_id={axis: lax.rem(me + k, n)},
                            device_id_type=pl.DeviceIdType.MESH)
        return carry

    lax.fori_loop(1, n, greet, 0)
    pl.semaphore_wait(barrier, n - 1)
    step = -1 if upward is False else 1

    def send_desc(k):
        tgt = lax.rem(me + k, n) if upward is None else me + step * k
        src = src_ref.at[tgt] if per_target else src_ref
        return pltpu.make_async_remote_copy(
            src, out_ref.at[me], send_sem.at[k - 1], recv_sem.at[k - 1],
            device_id={axis: tgt}, device_id_type=pl.DeviceIdType.MESH)

    def recv_desc(k):
        origin = lax.rem(me + n - k, n) if upward is None else me - step * k
        src = src_ref.at[me] if per_target else src_ref
        return pltpu.make_async_remote_copy(
            src, out_ref.at[origin], send_sem.at[k - 1], recv_sem.at[k - 1],
            device_id={axis: origin}, device_id_type=pl.DeviceIdType.MESH)

    def can_send(k):
        if upward is None:
            return k > 0
        return (me + k < n) if upward else (me - k >= 0)

    def can_recv(k):
        if upward is None:
            return k > 0
        return (me - k >= 0) if upward else (me + k < n)

    def start_one(k, carry):
        @pl.when(can_send(k))
        def _():
            send_desc(k).start()
        return carry

    def finish_one(k, carry):
        @pl.when(can_send(k))
        def _():
            send_desc(k).wait_send()

        @pl.when(can_recv(k))
        def _():
            recv_desc(k).wait_recv()
        return carry

    lax.fori_loop(1, n, start_one, 0)
    lax.fori_loop(1, n, finish_one, 0)
    if own is not None:
        own.wait()


def peer_blocks(src, n, axis, upward, per_target, cid):
    blk = src.shape[1:] if per_target else src.shape
    return pl.pallas_call(
        functools.partial(_peer_kernel, n, axis, upward, per_target),
        out_shape=jax.ShapeDtypeStruct((n,) + tuple(blk), src.dtype),
        in_specs=[pl.BlockSpec(memory_space=pl.ANY)],
        out_specs=pl.BlockSpec(memory_space=pl.ANY),
        scratch_shapes=[pltpu.SemaphoreType.DMA((n - 1,)), pltpu.SemaphoreType.DMA((n - 1,)),
                        pltpu.SemaphoreType.DMA(())],
        compiler_params=pltpu.CompilerParams(collective_id=cid, has_side_effects=True),
    )(src)


def _tile_mask(j, tk, rowpos_ref, rowdoc_ref, coldoc_ref):
    col = j * tk + lax.broadcasted_iota(jnp.int32, (1, tk), 1)
    return (col <= rowpos_ref[...]) & (coldoc_ref[...] == rowdoc_ref[...])


def _key_tile(kv_ref):
    return jnp.concatenate([kv_ref[c, 0, 0] for c in range(kv_ref.shape[0])], axis=0)


def _stats_kernel(scaling, tk, dh, bounds_ref, q_ref, g_ref, kv_ref, rowpos_ref, rowdoc_ref,
                  coldoc_ref, lt_ref, delta_ref, m_sc, l_sc, a_sc):
    j = pl.program_id(0)

    @pl.when(j == 0)
    def _():
        m_sc[...] = jnp.full(m_sc.shape, NEG_FILL, jnp.float32)
        l_sc[...] = jnp.zeros(l_sc.shape, jnp.float32)
        a_sc[...] = jnp.zeros(a_sc.shape, jnp.float32)

    @pl.when((j >= bounds_ref[0]) & (j <= bounds_ref[1]))
    def _():
        dims = (((1,), (1,)), ((), ()))
        kv = _key_tile(kv_ref)
        scores = lax.dot_general(q_ref[...], kv[:, :dh], dims,
                                 preferred_element_type=jnp.float32) * scaling
        allowed = _tile_mask(j, tk, rowpos_ref, rowdoc_ref, coldoc_ref)
        scores = jnp.where(allowed, scores, NEG_FILL)
        m_old = m_sc[...]
        m_new = jnp.maximum(m_old, jnp.max(scores, axis=1, keepdims=True))
        e = jnp.where(allowed, jnp.exp(scores - m_new), 0.0)
        gd = lax.dot_general(g_ref[...], kv[:, dh:], dims,
                             preferred_element_type=jnp.float32)
        alpha = jnp.exp(m_old - m_new)
        l_sc[...] = alpha * l_sc[...] + jnp.sum(e, axis=1, keepdims=True)
        a_sc[...] = alpha * a_sc[...] + jnp.sum(e * gd, axis=1, keepdims=True)
        m_sc[...] = m_new

    @pl.when(j == pl.num_programs(0) - 1)
    def _():
        lt_ref[...] = m_sc[...] + jnp.log(l_sc[...])
        delta_ref[...] = a_sc[...] / l_sc[...]


def _grad_kernel(scaling, tk, dh, bounds_ref, q_ref, g_ref, kv_ref, rowpos_ref, rowdoc_ref,
                 coldoc_ref, lt_ref, delta_ref, dq_ref, dkv_ref, dq_sc):
    j = pl.program_id(0)
    active = (j >= bounds_ref[0]) & (j <= bounds_ref[1])

    @pl.when(j == 0)
    def _():
        dq_sc[...] = jnp.zeros(dq_sc.shape, jnp.float32)

    @pl.when(active)
    def _():
        dims = (((1,), (1,)), ((), ()))
        tdims = (((0,), (0,)), ((), ()))
        kv = _key_tile(kv_ref)
        k_t = kv[:, :dh]
        scores = lax.dot_general(q_ref[...], k_t, dims,
                                 preferred_element_type=jnp.float32) * scaling
        allowed = _tile_mask(j, tk, rowpos_ref, rowdoc_ref, coldoc_ref)
        probs = jnp.where(allowed, jnp.exp(scores - lt_ref[...]), 0.0)
        gd = lax.dot_general(g_ref[...], kv[:, dh:], dims,
                             preferred_element_type=jnp.float32)
        ds = (probs * (gd - delta_ref[...]) * scaling).astype(jnp.bfloat16)
        dq_sc[...] += jnp.dot(ds, k_t, preferred_element_type=jnp.float32)
        dk = lax.dot_general(ds, q_ref[...], tdims, preferred_element_type=jnp.float32)
        dv = lax.dot_general(probs.astype(jnp.bfloat16), g_ref[...], tdims,
                             preferred_element_type=jnp.float32)
        owner_rows = dkv_ref.shape[3]
        for c in range(dkv_ref.shape[0]):
            part = slice(c * owner_rows, (c + 1) * owner_rows)
            dkv_ref[c, 0, 0, :, :dh] = dk[part].astype(dkv_ref.dtype)
            dkv_ref[c, 0, 0, :, dh:] = dv[part].astype(dkv_ref.dtype)

    @pl.when(jnp.logical_not(active))
    def _():
        dkv_ref[...] = jnp.zeros(dkv_ref.shape, dkv_ref.dtype)

    @pl.when(j == pl.num_programs(0) - 1)
    def _():
        dq_ref[...] = dq_sc[...].astype(dq_ref.dtype)


def attention_grads(q_rows, g_rows, kv_full, doc_starts, first_row, rows_here, scaling, chips):
    n_rows, dh = q_rows.shape
    n_keys = kv_full.shape[0] * kv_full.shape[1] * kv_full.shape[2] * kv_full.shape[3]
    n_zh, n_x, n_core = chips
    tk = n_core * rows_here
    n_tiles = n_keys // tk
    row_pos = first_row + jnp.arange(n_rows, dtype=jnp.int32) % rows_here
    row_doc = doc_index(doc_starts, row_pos)
    col_doc = doc_index(doc_starts, jnp.arange(n_keys, dtype=jnp.int32))[None, :]
    doc_first = jnp.max(jnp.where(doc_starts <= first_row, doc_starts, 0))
    bounds = jnp.stack([doc_first // tk, (first_row + rows_here - 1) // tk]).astype(jnp.int32)
    row_pos = row_pos[:, None]
    row_doc = row_doc[:, None]

    def tile_of(j, b):
        return jnp.minimum(jnp.maximum(j, b[0]), b[1])

    full = lambda shape: pl.BlockSpec(shape, lambda j, b: (0, 0))
    in_specs = [
        full((n_rows, dh)),
        full((n_rows, dh)),
        pl.BlockSpec((n_core, 1, 1, rows_here, 2 * dh),
                     lambda j, b: (0, tile_of(j, b) % n_x, tile_of(j, b) // n_x, 0, 0)),
        full((n_rows, 1)),
        full((n_rows, 1)),
        pl.BlockSpec((1, tk), lambda j, b: (0, tile_of(j, b))),
    ]
    params = pltpu.CompilerParams(dimension_semantics=("arbitrary",))
    mm = 2 * n_rows * n_keys * dh
    log_total, delta = pl.pallas_call(
        functools.partial(_stats_kernel, scaling, tk, dh),
        grid_spec=pltpu.PrefetchScalarGridSpec(
            num_scalar_prefetch=1,
            grid=(n_tiles,),
            in_specs=in_specs,
            out_specs=[full((n_rows, 1)), full((n_rows, 1))],
            scratch_shapes=[pltpu.VMEM((n_rows, 1), jnp.float32)] * 3,
        ),
        out_shape=[jax.ShapeDtypeStruct((n_rows, 1), jnp.float32)] * 2,
        compiler_params=params,
        cost_estimate=pl.CostEstimate(flops=2 * mm, transcendentals=n_rows * n_keys,
                                      bytes_accessed=n_keys * 4 * dh),
    )(bounds, q_rows, g_rows, kv_full, row_pos, row_doc, col_doc)
    dq, dkv = pl.pallas_call(
        functools.partial(_grad_kernel, scaling, tk, dh),
        grid_spec=pltpu.PrefetchScalarGridSpec(
            num_scalar_prefetch=1,
            grid=(n_tiles,),
            in_specs=in_specs + [full((n_rows, 1)), full((n_rows, 1))],
            out_specs=[
                full((n_rows, dh)),
                pl.BlockSpec((n_core, 1, 1, rows_here, 2 * dh),
                             lambda j, b: (0, j % n_x, j // n_x, 0, 0)),
            ],
            scratch_shapes=[pltpu.VMEM((n_rows, dh), jnp.float32)],
        ),
        out_shape=[jax.ShapeDtypeStruct((n_rows, dh), jnp.bfloat16),
                   jax.ShapeDtypeStruct((n_core, n_x, n_zh, rows_here, 2 * dh), jnp.bfloat16)],
        compiler_params=params,
        cost_estimate=pl.CostEstimate(flops=5 * mm, transcendentals=n_rows * n_keys,
                                      bytes_accessed=n_keys * 8 * dh),
    )(bounds, q_rows, g_rows, kv_full, row_pos, row_doc, col_doc, log_total, delta)
    return dq, dkv


def stage_reduce(parts, axis, cid):
    n = lax.axis_size(axis)
    me = lax.axis_index(axis)
    slots = peer_blocks(parts.astype(jnp.bfloat16), n, axis, None, True, cid)
    ids = jnp.arange(n, dtype=jnp.int32).reshape((n,) + (1,) * (parts.ndim - 1))
    others = jnp.sum(jnp.where(ids == me, 0.0, slots.astype(jnp.float32)), axis=0)
    return others + lax.dynamic_index_in_dim(parts, me, 0, keepdims=False).astype(jnp.float32)


def stage_gather(block, axis, cid):
    n = lax.axis_size(axis)
    return peer_blocks(block, n, axis, None, False, cid)


def shards(queries, keys, values, d_out, w_out, doc_starts):
    rows_here = queries.shape[0]
    head_size = DH
    groups = keys.shape[1] // head_size
    per_group = queries.shape[1] // keys.shape[1]
    kv_cols = keys.shape[1]
    scaling = 1.0 / math.sqrt(head_size)
    n_zh = lax.axis_size("zhi")
    n_x = lax.axis_size("xx")
    n_core = lax.axis_size("core")
    me = (lax.axis_index("zhi") * n_x + lax.axis_index("xx")) * n_core + lax.axis_index("core")
    first_row = me * rows_here
    my_rows = first_row + jnp.arange(rows_here, dtype=jnp.int32)
    kv_block = jnp.concatenate([keys, values], axis=1)
    for cid, axis in enumerate(("zhi", "xx", "core")):
        kv_block = stage_gather(kv_block, axis, cid + 4)
    attn_grad = lax.dot_general(
        lax.all_gather(d_out, "head", axis=1, tiled=True),
        w_out,
        (((1,), (1,)), ((), ())),
        preferred_element_type=jnp.float32,
    ).astype(jnp.bfloat16)
    heads = groups * per_group
    q_rows = queries.reshape(rows_here, heads, head_size).transpose(1, 0, 2).reshape(
        heads * rows_here, head_size)
    g_rows = attn_grad.reshape(rows_here, heads, head_size).transpose(1, 0, 2).reshape(
        heads * rows_here, head_size)
    dq_rows, kv_terms = attention_grads(
        q_rows, g_rows, kv_block, doc_starts, first_row, rows_here, scaling,
        (n_zh, n_x, n_core))
    query_grad = dq_rows.reshape(heads, rows_here, head_size).transpose(1, 0, 2).reshape(
        rows_here, heads * head_size)
    kv_grad = kv_terms
    for cid, axis in enumerate(("core", "xx", "zhi")):
        kv_grad = stage_reduce(kv_grad, axis, cid + 1)
    kv_grad = kv_grad.astype(jnp.bfloat16)
    key_grad = kv_grad[:, :kv_cols]
    value_grad = kv_grad[:, kv_cols:]
    return (query_grad, key_grad, value_grad)


def solution(mesh):
    n_seq, n_head = mesh.shape["seq"], mesh.shape["head"]
    split = jax.sharding.Mesh(
        mesh.devices.reshape(n_seq // 8, 4, 2, n_head), ("zhi", "xx", "core", "head")
    )
    rows = ("zhi", "xx", "core")
    return jax.shard_map(
        shards,
        mesh=split,
        in_specs=(
            P(rows, "head"),
            P(rows, "head"),
            P(rows, "head"),
            P(rows, "head"),
            P("head", None),
            P(),
        ),
        out_specs=(P(rows, "head"), P(rows, "head"), P(rows, "head")),
        check_vma=False,
    )
```

```python
import functools
import math

import jax
import jax.numpy as jnp
from jax import lax
from jax.sharding import PartitionSpec as P
from jax.experimental import pallas as pl
from jax.experimental.pallas import tpu as pltpu

DH = 128


NEG_FILL = -1e30


def doc_index(doc_starts, places):
    return jnp.sum((places[:, None] >= doc_starts[None, :]).astype(jnp.int32), axis=1)


def allowed_pairs(doc_starts, row_ids, col_ids):
    earlier = col_ids[None, :] <= row_ids[:, None]
    same_doc = doc_index(doc_starts, row_ids)[:, None] == doc_index(doc_starts, col_ids)[None, :]
    return (earlier & same_doc)[None, None]


def _peer_kernel(n, axis, upward, per_target, own_copy, src_ref, out_ref, send_sem, recv_sem,
                 own_sem):
    me = lax.axis_index(axis)
    own = None
    if own_copy:
        own = pltpu.make_async_copy(src_ref, out_ref.at[me], own_sem)
        own.start()
    barrier = pltpu.get_barrier_semaphore()

    def greet(k, carry):
        pl.semaphore_signal(barrier, 1, device_id={axis: lax.rem(me + k, n)},
                            device_id_type=pl.DeviceIdType.MESH)
        return carry

    lax.fori_loop(1, n, greet, 0)
    pl.semaphore_wait(barrier, n - 1)
    step = -1 if upward is False else 1

    def send_desc(k):
        tgt = lax.rem(me + k, n) if upward is None else me + step * k
        src = src_ref.at[tgt] if per_target else src_ref
        return pltpu.make_async_remote_copy(
            src, out_ref.at[me], send_sem.at[k - 1], recv_sem.at[k - 1],
            device_id={axis: tgt}, device_id_type=pl.DeviceIdType.MESH)

    def recv_desc(k):
        origin = lax.rem(me + n - k, n) if upward is None else me - step * k
        src = src_ref.at[me] if per_target else src_ref
        return pltpu.make_async_remote_copy(
            src, out_ref.at[origin], send_sem.at[k - 1], recv_sem.at[k - 1],
            device_id={axis: origin}, device_id_type=pl.DeviceIdType.MESH)

    def can_send(k):
        if upward is None:
            return k > 0
        return (me + k < n) if upward else (me - k >= 0)

    def can_recv(k):
        if upward is None:
            return k > 0
        return (me - k >= 0) if upward else (me + k < n)

    def start_one(k, carry):
        @pl.when(can_send(k))
        def _():
            send_desc(k).start()
        return carry

    def finish_one(k, carry):
        @pl.when(can_send(k))
        def _():
            send_desc(k).wait_send()

        @pl.when(can_recv(k))
        def _():
            recv_desc(k).wait_recv()
        return carry

    lax.fori_loop(1, n, start_one, 0)
    lax.fori_loop(1, n, finish_one, 0)
    if own is not None:
        own.wait()


def peer_blocks(src, n, axis, upward, per_target, cid, own_copy=False):
    blk = src.shape[1:] if per_target else src.shape
    return pl.pallas_call(
        functools.partial(_peer_kernel, n, axis, upward, per_target, own_copy),
        out_shape=jax.ShapeDtypeStruct((n,) + tuple(blk), src.dtype),
        in_specs=[pl.BlockSpec(memory_space=pl.ANY)],
        out_specs=pl.BlockSpec(memory_space=pl.ANY),
        scratch_shapes=[pltpu.SemaphoreType.DMA((n - 1,)), pltpu.SemaphoreType.DMA((n - 1,)),
                        pltpu.SemaphoreType.DMA(())],
        compiler_params=pltpu.CompilerParams(collective_id=cid, has_side_effects=True),
    )(src)


def _tile_mask(j, tk, rowpos_ref, rowdoc_ref, coldoc_ref):
    col = j * tk + lax.broadcasted_iota(jnp.int32, (1, tk), 1)
    return (col <= rowpos_ref[...]) & (coldoc_ref[...] == rowdoc_ref[...])


def _key_tile(kv_ref):
    return jnp.concatenate([kv_ref[c, 0, 0] for c in range(kv_ref.shape[0])], axis=0)


def _stats_kernel(scaling, tk, dh, bounds_ref, q_ref, g_ref, kv_ref, rowpos_ref, rowdoc_ref,
                  coldoc_ref, lt_ref, delta_ref, m_sc, l_sc, a_sc):
    j = pl.program_id(0)

    @pl.when(j == 0)
    def _():
        m_sc[...] = jnp.full(m_sc.shape, NEG_FILL, jnp.float32)
        l_sc[...] = jnp.zeros(l_sc.shape, jnp.float32)
        a_sc[...] = jnp.zeros(a_sc.shape, jnp.float32)

    @pl.when((j >= bounds_ref[0]) & (j <= bounds_ref[1]))
    def _():
        dims = (((1,), (1,)), ((), ()))
        kv = _key_tile(kv_ref)
        scores = lax.dot_general(q_ref[...], kv[:, :dh], dims,
                                 preferred_element_type=jnp.float32) * scaling
        allowed = _tile_mask(j, tk, rowpos_ref, rowdoc_ref, coldoc_ref)
        scores = jnp.where(allowed, scores, NEG_FILL)
        m_old = m_sc[...]
        m_new = jnp.maximum(m_old, jnp.max(scores, axis=1, keepdims=True))
        e = jnp.where(allowed, jnp.exp(scores - m_new), 0.0)
        gd = lax.dot_general(g_ref[...], kv[:, dh:], dims,
                             preferred_element_type=jnp.float32)
        alpha = jnp.exp(m_old - m_new)
        l_sc[...] = alpha * l_sc[...] + jnp.sum(e, axis=1, keepdims=True)
        a_sc[...] = alpha * a_sc[...] + jnp.sum(e * gd, axis=1, keepdims=True)
        m_sc[...] = m_new

    @pl.when(j == pl.num_programs(0) - 1)
    def _():
        lt_ref[...] = m_sc[...] + jnp.log(l_sc[...])
        delta_ref[...] = a_sc[...] / l_sc[...]


def _grad_kernel(scaling, tk, dh, bounds_ref, q_ref, g_ref, kv_ref, rowpos_ref, rowdoc_ref,
                 coldoc_ref, lt_ref, delta_ref, dq_ref, dkv_ref, dq_sc):
    j = pl.program_id(0)
    active = (j >= bounds_ref[0]) & (j <= bounds_ref[1])

    @pl.when(j == 0)
    def _():
        dq_sc[...] = jnp.zeros(dq_sc.shape, jnp.float32)

    @pl.when(active)
    def _():
        dims = (((1,), (1,)), ((), ()))
        tdims = (((0,), (0,)), ((), ()))
        kv = _key_tile(kv_ref)
        k_t = kv[:, :dh]
        scores = lax.dot_general(q_ref[...], k_t, dims,
                                 preferred_element_type=jnp.float32) * scaling
        allowed = _tile_mask(j, tk, rowpos_ref, rowdoc_ref, coldoc_ref)
        probs = jnp.where(allowed, jnp.exp(scores - lt_ref[...]), 0.0)
        gd = lax.dot_general(g_ref[...], kv[:, dh:], dims,
                             preferred_element_type=jnp.float32)
        ds = (probs * (gd - delta_ref[...]) * scaling).astype(jnp.bfloat16)
        dq_sc[...] += jnp.dot(ds, k_t, preferred_element_type=jnp.float32)
        dk = lax.dot_general(ds, q_ref[...], tdims, preferred_element_type=jnp.float32)
        dv = lax.dot_general(probs.astype(jnp.bfloat16), g_ref[...], tdims,
                             preferred_element_type=jnp.float32)
        owner_rows = dkv_ref.shape[3]
        for c in range(dkv_ref.shape[0]):
            part = slice(c * owner_rows, (c + 1) * owner_rows)
            dkv_ref[c, 0, 0, :, :dh] = dk[part].astype(dkv_ref.dtype)
            dkv_ref[c, 0, 0, :, dh:] = dv[part].astype(dkv_ref.dtype)

    @pl.when(jnp.logical_not(active))
    def _():
        dkv_ref[...] = jnp.zeros(dkv_ref.shape, dkv_ref.dtype)

    @pl.when(j == pl.num_programs(0) - 1)
    def _():
        dq_ref[...] = dq_sc[...].astype(dq_ref.dtype)


def attention_grads(q_rows, g_rows, kv_full, doc_starts, first_row, rows_here, scaling, chips):
    n_rows, dh = q_rows.shape
    n_keys = kv_full.shape[0] * kv_full.shape[1] * kv_full.shape[2] * kv_full.shape[3]
    n_zh, n_x, n_core = chips
    tk = n_core * rows_here
    n_tiles = n_keys // tk
    row_pos = first_row + jnp.arange(n_rows, dtype=jnp.int32) % rows_here
    row_doc = doc_index(doc_starts, row_pos)
    col_doc = doc_index(doc_starts, jnp.arange(n_keys, dtype=jnp.int32))[None, :]
    doc_first = jnp.max(jnp.where(doc_starts <= first_row, doc_starts, 0))
    bounds = jnp.stack([doc_first // tk, (first_row + rows_here - 1) // tk]).astype(jnp.int32)
    row_pos = row_pos[:, None]
    row_doc = row_doc[:, None]

    def tile_of(j, b):
        return jnp.minimum(jnp.maximum(j, b[0]), b[1])

    full = lambda shape: pl.BlockSpec(shape, lambda j, b: (0, 0))
    in_specs = [
        full((n_rows, dh)),
        full((n_rows, dh)),
        pl.BlockSpec((n_core, 1, 1, rows_here, 2 * dh),
                     lambda j, b: (0, tile_of(j, b) % n_x, tile_of(j, b) // n_x, 0, 0)),
        full((n_rows, 1)),
        full((n_rows, 1)),
        pl.BlockSpec((1, tk), lambda j, b: (0, tile_of(j, b))),
    ]
    params = pltpu.CompilerParams(dimension_semantics=("arbitrary",))
    mm = 2 * n_rows * n_keys * dh
    log_total, delta = pl.pallas_call(
        functools.partial(_stats_kernel, scaling, tk, dh),
        grid_spec=pltpu.PrefetchScalarGridSpec(
            num_scalar_prefetch=1,
            grid=(n_tiles,),
            in_specs=in_specs,
            out_specs=[full((n_rows, 1)), full((n_rows, 1))],
            scratch_shapes=[pltpu.VMEM((n_rows, 1), jnp.float32)] * 3,
        ),
        out_shape=[jax.ShapeDtypeStruct((n_rows, 1), jnp.float32)] * 2,
        compiler_params=params,
        cost_estimate=pl.CostEstimate(flops=2 * mm, transcendentals=n_rows * n_keys,
                                      bytes_accessed=n_keys * 4 * dh),
    )(bounds, q_rows, g_rows, kv_full, row_pos, row_doc, col_doc)
    dq, dkv = pl.pallas_call(
        functools.partial(_grad_kernel, scaling, tk, dh),
        grid_spec=pltpu.PrefetchScalarGridSpec(
            num_scalar_prefetch=1,
            grid=(n_tiles,),
            in_specs=in_specs + [full((n_rows, 1)), full((n_rows, 1))],
            out_specs=[
                full((n_rows, dh)),
                pl.BlockSpec((n_core, 1, 1, rows_here, 2 * dh),
                             lambda j, b: (0, j % n_x, j // n_x, 0, 0)),
            ],
            scratch_shapes=[pltpu.VMEM((n_rows, dh), jnp.float32)],
        ),
        out_shape=[jax.ShapeDtypeStruct((n_rows, dh), jnp.bfloat16),
                   jax.ShapeDtypeStruct((n_core, n_x, n_zh, rows_here, 2 * dh), jnp.bfloat16)],
        compiler_params=params,
        cost_estimate=pl.CostEstimate(flops=5 * mm, transcendentals=n_rows * n_keys,
                                      bytes_accessed=n_keys * 8 * dh),
    )(bounds, q_rows, g_rows, kv_full, row_pos, row_doc, col_doc, log_total, delta)
    return dq, dkv


def stage_reduce(parts, axis, cid):
    n = lax.axis_size(axis)
    me = lax.axis_index(axis)
    slots = peer_blocks(parts.astype(jnp.bfloat16), n, axis, None, True, cid)
    ids = jnp.arange(n, dtype=jnp.int32).reshape((n,) + (1,) * (parts.ndim - 1))
    others = jnp.sum(jnp.where(ids == me, 0.0, slots.astype(jnp.float32)), axis=0)
    return others + lax.dynamic_index_in_dim(parts, me, 0, keepdims=False).astype(jnp.float32)


def stage_gather(block, axis, cid):
    n = lax.axis_size(axis)
    if block.size * n * block.dtype.itemsize <= (1 << 21):
        return peer_blocks(block, n, axis, None, False, cid, own_copy=True)
    slots = peer_blocks(block, n, axis, None, False, cid)
    ids = jnp.arange(n, dtype=jnp.int32).reshape((n,) + (1,) * block.ndim)
    return jnp.where(ids == lax.axis_index(axis), block[None], slots)


def shards(queries, keys, values, d_out, w_out, doc_starts):
    rows_here = queries.shape[0]
    head_size = DH
    groups = keys.shape[1] // head_size
    per_group = queries.shape[1] // keys.shape[1]
    kv_cols = keys.shape[1]
    scaling = 1.0 / math.sqrt(head_size)
    n_zh = lax.axis_size("zhi")
    n_x = lax.axis_size("xx")
    n_core = lax.axis_size("core")
    me = (lax.axis_index("zhi") * n_x + lax.axis_index("xx")) * n_core + lax.axis_index("core")
    first_row = me * rows_here
    my_rows = first_row + jnp.arange(rows_here, dtype=jnp.int32)
    kv_block = jnp.concatenate([keys, values], axis=1)
    for cid, axis in enumerate(("zhi", "xx", "core")):
        kv_block = stage_gather(kv_block, axis, cid + 4)
    attn_grad = lax.dot_general(
        lax.all_gather(d_out, "head", axis=1, tiled=True),
        w_out,
        (((1,), (1,)), ((), ())),
        preferred_element_type=jnp.float32,
    ).astype(jnp.bfloat16)
    heads = groups * per_group
    q_rows = queries.reshape(rows_here, heads, head_size).transpose(1, 0, 2).reshape(
        heads * rows_here, head_size)
    g_rows = attn_grad.reshape(rows_here, heads, head_size).transpose(1, 0, 2).reshape(
        heads * rows_here, head_size)
    dq_rows, kv_terms = attention_grads(
        q_rows, g_rows, kv_block, doc_starts, first_row, rows_here, scaling,
        (n_zh, n_x, n_core))
    query_grad = dq_rows.reshape(heads, rows_here, head_size).transpose(1, 0, 2).reshape(
        rows_here, heads * head_size)
    kv_grad = kv_terms
    for cid, axis in enumerate(("core", "xx", "zhi")):
        kv_grad = stage_reduce(kv_grad, axis, cid + 1)
    kv_grad = kv_grad.astype(jnp.bfloat16)
    key_grad = kv_grad[:, :kv_cols]
    value_grad = kv_grad[:, kv_cols:]
    return (query_grad, key_grad, value_grad)


def solution(mesh):
    n_seq, n_head = mesh.shape["seq"], mesh.shape["head"]
    split = jax.sharding.Mesh(
        mesh.devices.reshape(n_seq // 8, 4, 2, n_head), ("zhi", "xx", "core", "head")
    )
    rows = ("zhi", "xx", "core")
    return jax.shard_map(
        shards,
        mesh=split,
        in_specs=(
            P(rows, "head"),
            P(rows, "head"),
            P(rows, "head"),
            P(rows, "head"),
            P("head", None),
            P(),
        ),
        out_specs=(P(rows, "head"), P(rows, "head"), P(rows, "head")),
        check_vma=False,
    )
```

```python
import functools
import math

import jax
import jax.numpy as jnp
from jax import lax
from jax.sharding import PartitionSpec as P
from jax.experimental import pallas as pl
from jax.experimental.pallas import tpu as pltpu

DH = 128


NEG_FILL = -1e30


def doc_index(doc_starts, places):
    return jnp.sum((places[:, None] >= doc_starts[None, :]).astype(jnp.int32), axis=1)


def allowed_pairs(doc_starts, row_ids, col_ids):
    earlier = col_ids[None, :] <= row_ids[:, None]
    same_doc = doc_index(doc_starts, row_ids)[:, None] == doc_index(doc_starts, col_ids)[None, :]
    return (earlier & same_doc)[None, None]


def _peer_kernel(n, axis, upward, per_target, own_copy, src_ref, out_ref, send_sem, recv_sem,
                 own_sem):
    me = lax.axis_index(axis)
    own = None
    if own_copy:
        own = pltpu.make_async_copy(src_ref, out_ref.at[me], own_sem)
        own.start()
    barrier = pltpu.get_barrier_semaphore()

    def greet(k, carry):
        pl.semaphore_signal(barrier, 1, device_id={axis: lax.rem(me + k, n)},
                            device_id_type=pl.DeviceIdType.MESH)
        return carry

    lax.fori_loop(1, n, greet, 0)
    pl.semaphore_wait(barrier, n - 1)
    step = -1 if upward is False else 1

    def send_desc(k):
        tgt = lax.rem(me + k, n) if upward is None else me + step * k
        src = src_ref.at[tgt] if per_target else src_ref
        return pltpu.make_async_remote_copy(
            src, out_ref.at[me], send_sem.at[k - 1], recv_sem.at[k - 1],
            device_id={axis: tgt}, device_id_type=pl.DeviceIdType.MESH)

    def recv_desc(k):
        origin = lax.rem(me + n - k, n) if upward is None else me - step * k
        src = src_ref.at[me] if per_target else src_ref
        return pltpu.make_async_remote_copy(
            src, out_ref.at[origin], send_sem.at[k - 1], recv_sem.at[k - 1],
            device_id={axis: origin}, device_id_type=pl.DeviceIdType.MESH)

    def can_send(k):
        if upward is None:
            return k > 0
        return (me + k < n) if upward else (me - k >= 0)

    def can_recv(k):
        if upward is None:
            return k > 0
        return (me - k >= 0) if upward else (me + k < n)

    def start_one(k, carry):
        @pl.when(can_send(k))
        def _():
            send_desc(k).start()
        return carry

    def finish_one(k, carry):
        @pl.when(can_send(k))
        def _():
            send_desc(k).wait_send()

        @pl.when(can_recv(k))
        def _():
            recv_desc(k).wait_recv()
        return carry

    lax.fori_loop(1, n, start_one, 0)
    lax.fori_loop(1, n, finish_one, 0)
    if own is not None:
        own.wait()


def peer_blocks(src, n, axis, upward, per_target, cid, own_copy=False):
    blk = src.shape[1:] if per_target else src.shape
    return pl.pallas_call(
        functools.partial(_peer_kernel, n, axis, upward, per_target, own_copy),
        out_shape=jax.ShapeDtypeStruct((n,) + tuple(blk), src.dtype),
        in_specs=[pl.BlockSpec(memory_space=pl.ANY)],
        out_specs=pl.BlockSpec(memory_space=pl.ANY),
        scratch_shapes=[pltpu.SemaphoreType.DMA((n - 1,)), pltpu.SemaphoreType.DMA((n - 1,)),
                        pltpu.SemaphoreType.DMA(())],
        compiler_params=pltpu.CompilerParams(collective_id=cid, has_side_effects=True),
    )(src)


def _tile_mask(j, tk, rowpos_ref, rowdoc_ref, coldoc_ref):
    col = j * tk + lax.broadcasted_iota(jnp.int32, (1, tk), 1)
    return (col <= rowpos_ref[...]) & (coldoc_ref[...] == rowdoc_ref[...])


def _key_tile(kv_ref):
    return jnp.concatenate([kv_ref[c, 0, 0] for c in range(kv_ref.shape[0])], axis=0)


def _stats_kernel(scaling, tk, dh, bounds_ref, q_ref, g_ref, kv_ref, rowpos_ref, rowdoc_ref,
                  coldoc_ref, lt_ref, delta_ref, m_sc, l_sc, a_sc):
    j = pl.program_id(0)

    @pl.when(j == 0)
    def _():
        m_sc[...] = jnp.full(m_sc.shape, NEG_FILL, jnp.float32)
        l_sc[...] = jnp.zeros(l_sc.shape, jnp.float32)
        a_sc[...] = jnp.zeros(a_sc.shape, jnp.float32)

    @pl.when((j >= bounds_ref[0]) & (j <= bounds_ref[1]))
    def _():
        dims = (((1,), (1,)), ((), ()))
        kv = _key_tile(kv_ref)
        scores = lax.dot_general(q_ref[...], kv[:, :dh], dims,
                                 preferred_element_type=jnp.float32) * scaling
        allowed = _tile_mask(j, tk, rowpos_ref, rowdoc_ref, coldoc_ref)
        scores = jnp.where(allowed, scores, NEG_FILL)
        m_old = m_sc[...]
        m_new = jnp.maximum(m_old, jnp.max(scores, axis=1, keepdims=True))
        e = jnp.where(allowed, jnp.exp(scores - m_new), 0.0)
        gd = lax.dot_general(g_ref[...], kv[:, dh:], dims,
                             preferred_element_type=jnp.float32)
        alpha = jnp.exp(m_old - m_new)
        l_sc[...] = alpha * l_sc[...] + jnp.sum(e, axis=1, keepdims=True)
        a_sc[...] = alpha * a_sc[...] + jnp.sum(e * gd, axis=1, keepdims=True)
        m_sc[...] = m_new

    @pl.when(j == pl.num_programs(0) - 1)
    def _():
        lt_ref[...] = m_sc[...] + jnp.log(l_sc[...])
        delta_ref[...] = a_sc[...] / l_sc[...]


def _grad_kernel(scaling, tk, dh, bounds_ref, q_ref, g_ref, kv_ref, rowpos_ref, rowdoc_ref,
                 coldoc_ref, lt_ref, delta_ref, dq_ref, dkv_ref, dq_sc):
    j = pl.program_id(0)
    active = (j >= bounds_ref[0]) & (j <= bounds_ref[1])

    @pl.when(j == 0)
    def _():
        dq_sc[...] = jnp.zeros(dq_sc.shape, jnp.float32)

    @pl.when(active)
    def _():
        dims = (((1,), (1,)), ((), ()))
        tdims = (((0,), (0,)), ((), ()))
        kv = _key_tile(kv_ref)
        k_t = kv[:, :dh]
        scores = lax.dot_general(q_ref[...], k_t, dims,
                                 preferred_element_type=jnp.float32) * scaling
        allowed = _tile_mask(j, tk, rowpos_ref, rowdoc_ref, coldoc_ref)
        probs = jnp.where(allowed, jnp.exp(scores - lt_ref[...]), 0.0)
        gd = lax.dot_general(g_ref[...], kv[:, dh:], dims,
                             preferred_element_type=jnp.float32)
        ds = (probs * (gd - delta_ref[...]) * scaling).astype(jnp.bfloat16)
        dq_sc[...] += jnp.dot(ds, k_t, preferred_element_type=jnp.float32)
        dk = lax.dot_general(ds, q_ref[...], tdims, preferred_element_type=jnp.float32)
        dv = lax.dot_general(probs.astype(jnp.bfloat16), g_ref[...], tdims,
                             preferred_element_type=jnp.float32)
        owner_rows = dkv_ref.shape[3]
        for c in range(dkv_ref.shape[0]):
            part = slice(c * owner_rows, (c + 1) * owner_rows)
            dkv_ref[c, 0, 0, :, :dh] = dk[part].astype(dkv_ref.dtype)
            dkv_ref[c, 0, 0, :, dh:] = dv[part].astype(dkv_ref.dtype)

    @pl.when(jnp.logical_not(active))
    def _():
        dkv_ref[...] = jnp.zeros(dkv_ref.shape, dkv_ref.dtype)

    @pl.when(j == pl.num_programs(0) - 1)
    def _():
        dq_ref[...] = dq_sc[...].astype(dq_ref.dtype)


def attention_grads(q_rows, g_rows, kv_full, doc_starts, first_row, rows_here, scaling, chips):
    n_rows, dh = q_rows.shape
    n_keys = kv_full.shape[0] * kv_full.shape[1] * kv_full.shape[2] * kv_full.shape[3]
    n_zh, n_x, n_core = chips
    tk = n_core * rows_here
    n_tiles = n_keys // tk
    row_pos = first_row + jnp.arange(n_rows, dtype=jnp.int32) % rows_here
    row_doc = doc_index(doc_starts, row_pos)
    col_doc = doc_index(doc_starts, jnp.arange(n_keys, dtype=jnp.int32))[None, :]
    doc_first = jnp.max(jnp.where(doc_starts <= first_row, doc_starts, 0))
    bounds = jnp.stack([doc_first // tk, (first_row + rows_here - 1) // tk]).astype(jnp.int32)
    row_pos = row_pos[:, None]
    row_doc = row_doc[:, None]

    def tile_of(j, b):
        return jnp.minimum(jnp.maximum(j, b[0]), b[1])

    full = lambda shape: pl.BlockSpec(shape, lambda j, b: (0, 0))
    in_specs = [
        full((n_rows, dh)),
        full((n_rows, dh)),
        pl.BlockSpec((n_core, 1, 1, rows_here, 2 * dh),
                     lambda j, b: (0, tile_of(j, b) // n_x, tile_of(j, b) % n_x, 0, 0)),
        full((n_rows, 1)),
        full((n_rows, 1)),
        pl.BlockSpec((1, tk), lambda j, b: (0, tile_of(j, b))),
    ]
    params = pltpu.CompilerParams(dimension_semantics=("arbitrary",))
    mm = 2 * n_rows * n_keys * dh
    log_total, delta = pl.pallas_call(
        functools.partial(_stats_kernel, scaling, tk, dh),
        grid_spec=pltpu.PrefetchScalarGridSpec(
            num_scalar_prefetch=1,
            grid=(n_tiles,),
            in_specs=in_specs,
            out_specs=[full((n_rows, 1)), full((n_rows, 1))],
            scratch_shapes=[pltpu.VMEM((n_rows, 1), jnp.float32)] * 3,
        ),
        out_shape=[jax.ShapeDtypeStruct((n_rows, 1), jnp.float32)] * 2,
        compiler_params=params,
        cost_estimate=pl.CostEstimate(flops=2 * mm, transcendentals=n_rows * n_keys,
                                      bytes_accessed=n_keys * 4 * dh),
    )(bounds, q_rows, g_rows, kv_full, row_pos, row_doc, col_doc)
    dq, dkv = pl.pallas_call(
        functools.partial(_grad_kernel, scaling, tk, dh),
        grid_spec=pltpu.PrefetchScalarGridSpec(
            num_scalar_prefetch=1,
            grid=(n_tiles,),
            in_specs=in_specs + [full((n_rows, 1)), full((n_rows, 1))],
            out_specs=[
                full((n_rows, dh)),
                pl.BlockSpec((n_core, 1, 1, rows_here, 2 * dh),
                             lambda j, b: (0, j % n_x, j // n_x, 0, 0)),
            ],
            scratch_shapes=[pltpu.VMEM((n_rows, dh), jnp.float32)],
        ),
        out_shape=[jax.ShapeDtypeStruct((n_rows, dh), jnp.bfloat16),
                   jax.ShapeDtypeStruct((n_core, n_x, n_zh, rows_here, 2 * dh), jnp.bfloat16)],
        compiler_params=params,
        cost_estimate=pl.CostEstimate(flops=5 * mm, transcendentals=n_rows * n_keys,
                                      bytes_accessed=n_keys * 8 * dh),
    )(bounds, q_rows, g_rows, kv_full, row_pos, row_doc, col_doc, log_total, delta)
    return dq, dkv


def stage_reduce(parts, axis, cid):
    n = lax.axis_size(axis)
    me = lax.axis_index(axis)
    slots = peer_blocks(parts.astype(jnp.bfloat16), n, axis, None, True, cid)
    ids = jnp.arange(n, dtype=jnp.int32).reshape((n,) + (1,) * (parts.ndim - 1))
    others = jnp.sum(jnp.where(ids == me, 0.0, slots.astype(jnp.float32)), axis=0)
    return others + lax.dynamic_index_in_dim(parts, me, 0, keepdims=False).astype(jnp.float32)


def stage_gather(block, axis, cid):
    n = lax.axis_size(axis)
    if block.size * n * block.dtype.itemsize <= (1 << 21):
        return peer_blocks(block, n, axis, None, False, cid, own_copy=True)
    slots = peer_blocks(block, n, axis, None, False, cid)
    ids = jnp.arange(n, dtype=jnp.int32).reshape((n,) + (1,) * block.ndim)
    return jnp.where(ids == lax.axis_index(axis), block[None], slots)


def shards(queries, keys, values, d_out, w_out, doc_starts):
    rows_here = queries.shape[0]
    head_size = DH
    groups = keys.shape[1] // head_size
    per_group = queries.shape[1] // keys.shape[1]
    kv_cols = keys.shape[1]
    scaling = 1.0 / math.sqrt(head_size)
    n_zh = lax.axis_size("zhi")
    n_x = lax.axis_size("xx")
    n_core = lax.axis_size("core")
    me = (lax.axis_index("zhi") * n_x + lax.axis_index("xx")) * n_core + lax.axis_index("core")
    first_row = me * rows_here
    my_rows = first_row + jnp.arange(rows_here, dtype=jnp.int32)
    kv_block = jnp.concatenate([keys, values], axis=1)
    for cid, axis in enumerate(("xx", "zhi", "core")):
        kv_block = stage_gather(kv_block, axis, cid + 4)
    attn_grad = lax.dot_general(
        lax.all_gather(d_out, "head", axis=1, tiled=True),
        w_out,
        (((1,), (1,)), ((), ())),
        preferred_element_type=jnp.float32,
    ).astype(jnp.bfloat16)
    heads = groups * per_group
    q_rows = queries.reshape(rows_here, heads, head_size).transpose(1, 0, 2).reshape(
        heads * rows_here, head_size)
    g_rows = attn_grad.reshape(rows_here, heads, head_size).transpose(1, 0, 2).reshape(
        heads * rows_here, head_size)
    dq_rows, kv_terms = attention_grads(
        q_rows, g_rows, kv_block, doc_starts, first_row, rows_here, scaling,
        (n_zh, n_x, n_core))
    query_grad = dq_rows.reshape(heads, rows_here, head_size).transpose(1, 0, 2).reshape(
        rows_here, heads * head_size)
    kv_grad = kv_terms
    for cid, axis in enumerate(("core", "xx", "zhi")):
        kv_grad = stage_reduce(kv_grad, axis, cid + 1)
    kv_grad = kv_grad.astype(jnp.bfloat16)
    key_grad = kv_grad[:, :kv_cols]
    value_grad = kv_grad[:, kv_cols:]
    return (query_grad, key_grad, value_grad)


def solution(mesh):
    n_seq, n_head = mesh.shape["seq"], mesh.shape["head"]
    split = jax.sharding.Mesh(
        mesh.devices.reshape(n_seq // 8, 4, 2, n_head), ("zhi", "xx", "core", "head")
    )
    rows = ("zhi", "xx", "core")
    return jax.shard_map(
        shards,
        mesh=split,
        in_specs=(
            P(rows, "head"),
            P(rows, "head"),
            P(rows, "head"),
            P(rows, "head"),
            P("head", None),
            P(),
        ),
        out_specs=(P(rows, "head"), P(rows, "head"), P(rows, "head")),
        check_vma=False,
    )
```

```python
import functools
import math

import jax
import jax.numpy as jnp
from jax import lax
from jax.sharding import PartitionSpec as P
from jax.experimental import pallas as pl
from jax.experimental.pallas import tpu as pltpu

DH = 128


NEG_FILL = -1e30


def doc_index(doc_starts, places):
    return jnp.sum((places[:, None] >= doc_starts[None, :]).astype(jnp.int32), axis=1)


def allowed_pairs(doc_starts, row_ids, col_ids):
    earlier = col_ids[None, :] <= row_ids[:, None]
    same_doc = doc_index(doc_starts, row_ids)[:, None] == doc_index(doc_starts, col_ids)[None, :]
    return (earlier & same_doc)[None, None]


def _peer_kernel(n, axis, upward, per_target, own_copy, src_ref, out_ref, send_sem, recv_sem,
                 own_sem):
    me = lax.axis_index(axis)
    own = None
    if own_copy:
        own = pltpu.make_async_copy(src_ref, out_ref.at[me], own_sem)
        own.start()
    barrier = pltpu.get_barrier_semaphore()

    def greet(k, carry):
        pl.semaphore_signal(barrier, 1, device_id={axis: lax.rem(me + k, n)},
                            device_id_type=pl.DeviceIdType.MESH)
        return carry

    lax.fori_loop(1, n, greet, 0)
    pl.semaphore_wait(barrier, n - 1)
    step = -1 if upward is False else 1

    def send_desc(k):
        tgt = lax.rem(me + k, n) if upward is None else me + step * k
        src = src_ref.at[tgt] if per_target else src_ref
        return pltpu.make_async_remote_copy(
            src, out_ref.at[me], send_sem.at[k - 1], recv_sem.at[k - 1],
            device_id={axis: tgt}, device_id_type=pl.DeviceIdType.MESH)

    def recv_desc(k):
        origin = lax.rem(me + n - k, n) if upward is None else me - step * k
        src = src_ref.at[me] if per_target else src_ref
        return pltpu.make_async_remote_copy(
            src, out_ref.at[origin], send_sem.at[k - 1], recv_sem.at[k - 1],
            device_id={axis: origin}, device_id_type=pl.DeviceIdType.MESH)

    def can_send(k):
        if upward is None:
            return k > 0
        return (me + k < n) if upward else (me - k >= 0)

    def can_recv(k):
        if upward is None:
            return k > 0
        return (me - k >= 0) if upward else (me + k < n)

    def start_one(k, carry):
        @pl.when(can_send(k))
        def _():
            send_desc(k).start()
        return carry

    def finish_one(k, carry):
        @pl.when(can_send(k))
        def _():
            send_desc(k).wait_send()

        @pl.when(can_recv(k))
        def _():
            recv_desc(k).wait_recv()
        return carry

    lax.fori_loop(1, n, start_one, 0)
    lax.fori_loop(1, n, finish_one, 0)
    if own is not None:
        own.wait()


def peer_blocks(src, n, axis, upward, per_target, cid, own_copy=False):
    blk = src.shape[1:] if per_target else src.shape
    return pl.pallas_call(
        functools.partial(_peer_kernel, n, axis, upward, per_target, own_copy),
        out_shape=jax.ShapeDtypeStruct((n,) + tuple(blk), src.dtype),
        in_specs=[pl.BlockSpec(memory_space=pl.ANY)],
        out_specs=pl.BlockSpec(memory_space=pl.ANY),
        scratch_shapes=[pltpu.SemaphoreType.DMA((n - 1,)), pltpu.SemaphoreType.DMA((n - 1,)),
                        pltpu.SemaphoreType.DMA(())],
        compiler_params=pltpu.CompilerParams(collective_id=cid, has_side_effects=True),
    )(src)


def _tile_mask(j, tk, rowpos_ref, rowdoc_ref, coldoc_ref):
    col = j * tk + lax.broadcasted_iota(jnp.int32, (1, tk), 1)
    return (col <= rowpos_ref[...]) & (coldoc_ref[...] == rowdoc_ref[...])


def _key_tile(kv_ref):
    return jnp.concatenate([kv_ref[c, 0, 0] for c in range(kv_ref.shape[0])], axis=0)


def _stats_kernel(scaling, tk, dh, bounds_ref, q_ref, g_ref, kv_ref, rowpos_ref, rowdoc_ref,
                  coldoc_ref, lt_ref, delta_ref, m_sc, l_sc, a_sc):
    j = pl.program_id(0)

    @pl.when(j == 0)
    def _():
        m_sc[...] = jnp.full(m_sc.shape, NEG_FILL, jnp.float32)
        l_sc[...] = jnp.zeros(l_sc.shape, jnp.float32)
        a_sc[...] = jnp.zeros(a_sc.shape, jnp.float32)

    @pl.when((j >= bounds_ref[0]) & (j <= bounds_ref[1]))
    def _():
        dims = (((1,), (1,)), ((), ()))
        kv = _key_tile(kv_ref)
        scores = lax.dot_general(q_ref[...], kv[:, :dh], dims,
                                 preferred_element_type=jnp.float32) * scaling
        allowed = _tile_mask(j, tk, rowpos_ref, rowdoc_ref, coldoc_ref)
        scores = jnp.where(allowed, scores, NEG_FILL)
        m_old = m_sc[...]
        m_new = jnp.maximum(m_old, jnp.max(scores, axis=1, keepdims=True))
        e = jnp.where(allowed, jnp.exp(scores - m_new), 0.0)
        gd = lax.dot_general(g_ref[...], kv[:, dh:], dims,
                             preferred_element_type=jnp.float32)
        alpha = jnp.exp(m_old - m_new)
        l_sc[...] = alpha * l_sc[...] + jnp.sum(e, axis=1, keepdims=True)
        a_sc[...] = alpha * a_sc[...] + jnp.sum(e * gd, axis=1, keepdims=True)
        m_sc[...] = m_new

    @pl.when(j == pl.num_programs(0) - 1)
    def _():
        lt_ref[...] = m_sc[...] + jnp.log(l_sc[...])
        delta_ref[...] = a_sc[...] / l_sc[...]


def _grad_kernel(scaling, tk, dh, bounds_ref, q_ref, g_ref, kv_ref, rowpos_ref, rowdoc_ref,
                 coldoc_ref, lt_ref, delta_ref, dq_ref, dkv_ref, dq_sc):
    j = pl.program_id(0)
    active = (j >= bounds_ref[0]) & (j <= bounds_ref[1])

    @pl.when(j == 0)
    def _():
        dq_sc[...] = jnp.zeros(dq_sc.shape, jnp.float32)

    @pl.when(active)
    def _():
        dims = (((1,), (1,)), ((), ()))
        tdims = (((0,), (0,)), ((), ()))
        kv = _key_tile(kv_ref)
        k_t = kv[:, :dh]
        scores = lax.dot_general(q_ref[...], k_t, dims,
                                 preferred_element_type=jnp.float32) * scaling
        allowed = _tile_mask(j, tk, rowpos_ref, rowdoc_ref, coldoc_ref)
        probs = jnp.where(allowed, jnp.exp(scores - lt_ref[...]), 0.0)
        gd = lax.dot_general(g_ref[...], kv[:, dh:], dims,
                             preferred_element_type=jnp.float32)
        ds = (probs * (gd - delta_ref[...]) * scaling).astype(jnp.bfloat16)
        dq_sc[...] += jnp.dot(ds, k_t, preferred_element_type=jnp.float32)
        dk = lax.dot_general(ds, q_ref[...], tdims, preferred_element_type=jnp.float32)
        dv = lax.dot_general(probs.astype(jnp.bfloat16), g_ref[...], tdims,
                             preferred_element_type=jnp.float32)
        owner_rows = dkv_ref.shape[3]
        for c in range(dkv_ref.shape[0]):
            part = slice(c * owner_rows, (c + 1) * owner_rows)
            dkv_ref[c, 0, 0, :, :dh] = dk[part].astype(dkv_ref.dtype)
            dkv_ref[c, 0, 0, :, dh:] = dv[part].astype(dkv_ref.dtype)

    @pl.when(jnp.logical_not(active))
    def _():
        dkv_ref[...] = jnp.zeros(dkv_ref.shape, dkv_ref.dtype)

    @pl.when(j == pl.num_programs(0) - 1)
    def _():
        dq_ref[...] = dq_sc[...].astype(dq_ref.dtype)


def attention_grads(q_rows, g_rows, kv_full, doc_starts, first_row, rows_here, scaling, chips):
    n_rows, dh = q_rows.shape
    n_keys = kv_full.shape[0] * kv_full.shape[1] * kv_full.shape[2] * kv_full.shape[3]
    n_zh, n_x, n_core = chips
    tk = n_core * rows_here
    n_tiles = n_keys // tk
    row_pos = first_row + jnp.arange(n_rows, dtype=jnp.int32) % rows_here
    row_doc = doc_index(doc_starts, row_pos)
    col_doc = doc_index(doc_starts, jnp.arange(n_keys, dtype=jnp.int32))[None, :]
    doc_first = jnp.max(jnp.where(doc_starts <= first_row, doc_starts, 0))
    bounds = jnp.stack([doc_first // tk, (first_row + rows_here - 1) // tk]).astype(jnp.int32)
    row_pos = row_pos[:, None]
    row_doc = row_doc[:, None]

    def tile_of(j, b):
        return jnp.minimum(jnp.maximum(j, b[0]), b[1])

    full = lambda shape: pl.BlockSpec(shape, lambda j, b: (0, 0))
    in_specs = [
        full((n_rows, dh)),
        full((n_rows, dh)),
        pl.BlockSpec((n_core, 1, 1, rows_here, 2 * dh),
                     lambda j, b: (0, tile_of(j, b) % n_x, tile_of(j, b) // n_x, 0, 0)),
        full((n_rows, 1)),
        full((n_rows, 1)),
        pl.BlockSpec((1, tk), lambda j, b: (0, tile_of(j, b))),
    ]
    params = pltpu.CompilerParams(dimension_semantics=("arbitrary",))
    mm = 2 * n_rows * n_keys * dh
    log_total, delta = pl.pallas_call(
        functools.partial(_stats_kernel, scaling, tk, dh),
        grid_spec=pltpu.PrefetchScalarGridSpec(
            num_scalar_prefetch=1,
            grid=(n_tiles,),
            in_specs=in_specs,
            out_specs=[full((n_rows, 1)), full((n_rows, 1))],
            scratch_shapes=[pltpu.VMEM((n_rows, 1), jnp.float32)] * 3,
        ),
        out_shape=[jax.ShapeDtypeStruct((n_rows, 1), jnp.float32)] * 2,
        compiler_params=params,
        cost_estimate=pl.CostEstimate(flops=2 * mm, transcendentals=n_rows * n_keys,
                                      bytes_accessed=n_keys * 4 * dh),
    )(bounds, q_rows, g_rows, kv_full, row_pos, row_doc, col_doc)
    dq, dkv = pl.pallas_call(
        functools.partial(_grad_kernel, scaling, tk, dh),
        grid_spec=pltpu.PrefetchScalarGridSpec(
            num_scalar_prefetch=1,
            grid=(n_tiles,),
            in_specs=in_specs + [full((n_rows, 1)), full((n_rows, 1))],
            out_specs=[
                full((n_rows, dh)),
                pl.BlockSpec((n_core, 1, 1, rows_here, 2 * dh),
                             lambda j, b: (0, j % n_x, j // n_x, 0, 0)),
            ],
            scratch_shapes=[pltpu.VMEM((n_rows, dh), jnp.float32)],
        ),
        out_shape=[jax.ShapeDtypeStruct((n_rows, dh), jnp.bfloat16),
                   jax.ShapeDtypeStruct((n_core, n_x, n_zh, rows_here, 2 * dh), jnp.bfloat16)],
        compiler_params=params,
        cost_estimate=pl.CostEstimate(flops=5 * mm, transcendentals=n_rows * n_keys,
                                      bytes_accessed=n_keys * 8 * dh),
    )(bounds, q_rows, g_rows, kv_full, row_pos, row_doc, col_doc, log_total, delta)
    return dq, dkv


def stage_reduce(parts, axis, cid):
    n = lax.axis_size(axis)
    me = lax.axis_index(axis)
    slots = peer_blocks(parts.astype(jnp.bfloat16), n, axis, None, True, cid)
    ids = jnp.arange(n, dtype=jnp.int32).reshape((n,) + (1,) * (parts.ndim - 1))
    total = lax.dynamic_index_in_dim(parts, me, 0, keepdims=False).astype(jnp.float32)
    for i in range(n):
        total = total + jnp.where(me == i, 0.0, slots[i].astype(jnp.float32))
    return total.astype(jnp.bfloat16)


def stage_gather(block, axis, cid):
    n = lax.axis_size(axis)
    if block.size * n * block.dtype.itemsize <= (1 << 21):
        return peer_blocks(block, n, axis, None, False, cid, own_copy=True)
    slots = peer_blocks(block, n, axis, None, False, cid)
    ids = jnp.arange(n, dtype=jnp.int32).reshape((n,) + (1,) * block.ndim)
    return jnp.where(ids == lax.axis_index(axis), block[None], slots)


def shards(queries, keys, values, d_out, w_out, doc_starts):
    rows_here = queries.shape[0]
    head_size = DH
    groups = keys.shape[1] // head_size
    per_group = queries.shape[1] // keys.shape[1]
    kv_cols = keys.shape[1]
    scaling = 1.0 / math.sqrt(head_size)
    n_zh = lax.axis_size("zhi")
    n_x = lax.axis_size("xx")
    n_core = lax.axis_size("core")
    me = (lax.axis_index("zhi") * n_x + lax.axis_index("xx")) * n_core + lax.axis_index("core")
    first_row = me * rows_here
    my_rows = first_row + jnp.arange(rows_here, dtype=jnp.int32)
    kv_block = jnp.concatenate([keys, values], axis=1)
    for cid, axis in enumerate(("zhi", "xx", "core")):
        kv_block = stage_gather(kv_block, axis, cid + 4)
    attn_grad = lax.dot_general(
        lax.all_gather(d_out, "head", axis=1, tiled=True),
        w_out,
        (((1,), (1,)), ((), ())),
        preferred_element_type=jnp.float32,
    ).astype(jnp.bfloat16)
    heads = groups * per_group
    q_rows = queries.reshape(rows_here, heads, head_size).transpose(1, 0, 2).reshape(
        heads * rows_here, head_size)
    g_rows = attn_grad.reshape(rows_here, heads, head_size).transpose(1, 0, 2).reshape(
        heads * rows_here, head_size)
    dq_rows, kv_terms = attention_grads(
        q_rows, g_rows, kv_block, doc_starts, first_row, rows_here, scaling,
        (n_zh, n_x, n_core))
    query_grad = dq_rows.reshape(heads, rows_here, head_size).transpose(1, 0, 2).reshape(
        rows_here, heads * head_size)
    kv_grad = kv_terms
    for cid, axis in enumerate(("core", "xx", "zhi")):
        kv_grad = stage_reduce(kv_grad, axis, cid + 1)
    kv_grad = kv_grad.astype(jnp.bfloat16)
    key_grad = kv_grad[:, :kv_cols]
    value_grad = kv_grad[:, kv_cols:]
    return (query_grad, key_grad, value_grad)


def solution(mesh):
    n_seq, n_head = mesh.shape["seq"], mesh.shape["head"]
    split = jax.sharding.Mesh(
        mesh.devices.reshape(n_seq // 8, 4, 2, n_head), ("zhi", "xx", "core", "head")
    )
    rows = ("zhi", "xx", "core")
    return jax.shard_map(
        shards,
        mesh=split,
        in_specs=(
            P(rows, "head"),
            P(rows, "head"),
            P(rows, "head"),
            P(rows, "head"),
            P("head", None),
            P(),
        ),
        out_specs=(P(rows, "head"), P(rows, "head"), P(rows, "head")),
        check_vma=False,
    )
```

```python
import functools
import math

import jax
import jax.numpy as jnp
from jax import lax
from jax.sharding import PartitionSpec as P
from jax.experimental import pallas as pl
from jax.experimental.pallas import tpu as pltpu

DH = 128


NEG_FILL = -1e30


def doc_index(doc_starts, places):
    return jnp.sum((places[:, None] >= doc_starts[None, :]).astype(jnp.int32), axis=1)


def allowed_pairs(doc_starts, row_ids, col_ids):
    earlier = col_ids[None, :] <= row_ids[:, None]
    same_doc = doc_index(doc_starts, row_ids)[:, None] == doc_index(doc_starts, col_ids)[None, :]
    return (earlier & same_doc)[None, None]


def _peer_kernel(n, axis, upward, per_target, own_copy, src_ref, out_ref, send_sem, recv_sem,
                 own_sem):
    me = lax.axis_index(axis)
    own = None
    if own_copy:
        own = pltpu.make_async_copy(src_ref, out_ref.at[me], own_sem)
        own.start()
    barrier = pltpu.get_barrier_semaphore()

    def greet(k, carry):
        pl.semaphore_signal(barrier, 1, device_id={axis: lax.rem(me + k, n)},
                            device_id_type=pl.DeviceIdType.MESH)
        return carry

    lax.fori_loop(1, n, greet, 0)
    pl.semaphore_wait(barrier, n - 1)
    step = -1 if upward is False else 1

    def send_desc(k):
        tgt = lax.rem(me + k, n) if upward is None else me + step * k
        src = src_ref.at[tgt] if per_target else src_ref
        return pltpu.make_async_remote_copy(
            src, out_ref.at[me], send_sem.at[k - 1], recv_sem.at[k - 1],
            device_id={axis: tgt}, device_id_type=pl.DeviceIdType.MESH)

    def recv_desc(k):
        origin = lax.rem(me + n - k, n) if upward is None else me - step * k
        src = src_ref.at[me] if per_target else src_ref
        return pltpu.make_async_remote_copy(
            src, out_ref.at[origin], send_sem.at[k - 1], recv_sem.at[k - 1],
            device_id={axis: origin}, device_id_type=pl.DeviceIdType.MESH)

    def can_send(k):
        if upward is None:
            return k > 0
        return (me + k < n) if upward else (me - k >= 0)

    def can_recv(k):
        if upward is None:
            return k > 0
        return (me - k >= 0) if upward else (me + k < n)

    def start_one(k, carry):
        @pl.when(can_send(k))
        def _():
            send_desc(k).start()
        return carry

    def finish_one(k, carry):
        @pl.when(can_send(k))
        def _():
            send_desc(k).wait_send()

        @pl.when(can_recv(k))
        def _():
            recv_desc(k).wait_recv()
        return carry

    lax.fori_loop(1, n, start_one, 0)
    lax.fori_loop(1, n, finish_one, 0)
    if own is not None:
        own.wait()


def peer_blocks(src, n, axis, upward, per_target, cid, own_copy=False):
    blk = src.shape[1:] if per_target else src.shape
    return pl.pallas_call(
        functools.partial(_peer_kernel, n, axis, upward, per_target, own_copy),
        out_shape=jax.ShapeDtypeStruct((n,) + tuple(blk), src.dtype),
        in_specs=[pl.BlockSpec(memory_space=pl.ANY)],
        out_specs=pl.BlockSpec(memory_space=pl.ANY),
        scratch_shapes=[pltpu.SemaphoreType.DMA((n - 1,)), pltpu.SemaphoreType.DMA((n - 1,)),
                        pltpu.SemaphoreType.DMA(())],
        compiler_params=pltpu.CompilerParams(collective_id=cid, has_side_effects=True),
    )(src)


def _tile_mask(j, tk, meta_ref, n_rows, rows_here, n_docs):
    col = j * tk + lax.broadcasted_iota(jnp.int32, (1, tk), 1)
    row = meta_ref[2] + lax.broadcasted_iota(jnp.int32, (n_rows, 1), 0) % rows_here
    col_doc = jnp.zeros((1, tk), jnp.int32)
    row_doc = jnp.zeros((n_rows, 1), jnp.int32)
    for k in range(n_docs):
        start = meta_ref[3 + k]
        col_doc = col_doc + (col >= start).astype(jnp.int32)
        row_doc = row_doc + (row >= start).astype(jnp.int32)
    return (col <= row) & (col_doc == row_doc)


def _key_tile(kv_ref):
    return jnp.concatenate([kv_ref[c, 0, 0] for c in range(kv_ref.shape[0])], axis=0)


def _stats_kernel(scaling, tk, dh, rows_here, n_docs, bounds_ref, q_ref, g_ref, kv_ref,
                  lt_ref, delta_ref, m_sc, l_sc, a_sc):
    j = pl.program_id(0)

    @pl.when(j == 0)
    def _():
        m_sc[...] = jnp.full(m_sc.shape, NEG_FILL, jnp.float32)
        l_sc[...] = jnp.zeros(l_sc.shape, jnp.float32)
        a_sc[...] = jnp.zeros(a_sc.shape, jnp.float32)

    @pl.when((j >= bounds_ref[0]) & (j <= bounds_ref[1]))
    def _():
        dims = (((1,), (1,)), ((), ()))
        kv = _key_tile(kv_ref)
        scores = lax.dot_general(q_ref[...], kv[:, :dh], dims,
                                 preferred_element_type=jnp.float32) * scaling
        allowed = _tile_mask(j, tk, bounds_ref, q_ref.shape[0], rows_here, n_docs)
        scores = jnp.where(allowed, scores, NEG_FILL)
        m_old = m_sc[...]
        m_new = jnp.maximum(m_old, jnp.max(scores, axis=1, keepdims=True))
        e = jnp.where(allowed, jnp.exp(scores - m_new), 0.0)
        gd = lax.dot_general(g_ref[...], kv[:, dh:], dims,
                             preferred_element_type=jnp.float32)
        alpha = jnp.exp(m_old - m_new)
        l_sc[...] = alpha * l_sc[...] + jnp.sum(e, axis=1, keepdims=True)
        a_sc[...] = alpha * a_sc[...] + jnp.sum(e * gd, axis=1, keepdims=True)
        m_sc[...] = m_new

    @pl.when(j == pl.num_programs(0) - 1)
    def _():
        lt_ref[...] = m_sc[...] + jnp.log(l_sc[...])
        delta_ref[...] = a_sc[...] / l_sc[...]


def _grad_kernel(scaling, tk, dh, rows_here, n_docs, bounds_ref, q_ref, g_ref, kv_ref,
                 lt_ref, delta_ref, dq_ref, dkv_ref, dq_sc):
    j = pl.program_id(0)
    active = (j >= bounds_ref[0]) & (j <= bounds_ref[1])

    @pl.when(j == 0)
    def _():
        dq_sc[...] = jnp.zeros(dq_sc.shape, jnp.float32)

    @pl.when(active)
    def _():
        dims = (((1,), (1,)), ((), ()))
        tdims = (((0,), (0,)), ((), ()))
        kv = _key_tile(kv_ref)
        k_t = kv[:, :dh]
        scores = lax.dot_general(q_ref[...], k_t, dims,
                                 preferred_element_type=jnp.float32) * scaling
        allowed = _tile_mask(j, tk, bounds_ref, q_ref.shape[0], rows_here, n_docs)
        probs = jnp.where(allowed, jnp.exp(scores - lt_ref[...]), 0.0)
        gd = lax.dot_general(g_ref[...], kv[:, dh:], dims,
                             preferred_element_type=jnp.float32)
        ds = (probs * (gd - delta_ref[...]) * scaling).astype(jnp.bfloat16)
        dq_sc[...] += jnp.dot(ds, k_t, preferred_element_type=jnp.float32)
        dk = lax.dot_general(ds, q_ref[...], tdims, preferred_element_type=jnp.float32)
        dv = lax.dot_general(probs.astype(jnp.bfloat16), g_ref[...], tdims,
                             preferred_element_type=jnp.float32)
        owner_rows = dkv_ref.shape[3]
        for c in range(dkv_ref.shape[0]):
            part = slice(c * owner_rows, (c + 1) * owner_rows)
            dkv_ref[c, 0, 0, :, :dh] = dk[part].astype(dkv_ref.dtype)
            dkv_ref[c, 0, 0, :, dh:] = dv[part].astype(dkv_ref.dtype)

    @pl.when(jnp.logical_not(active))
    def _():
        dkv_ref[...] = jnp.zeros(dkv_ref.shape, dkv_ref.dtype)

    @pl.when(j == pl.num_programs(0) - 1)
    def _():
        dq_ref[...] = dq_sc[...].astype(dq_ref.dtype)


def attention_grads(q_rows, g_rows, kv_full, doc_starts, first_row, rows_here, scaling, chips):
    n_rows, dh = q_rows.shape
    n_keys = kv_full.shape[0] * kv_full.shape[1] * kv_full.shape[2] * kv_full.shape[3]
    n_zh, n_x, n_core = chips
    tk = n_core * rows_here
    n_tiles = n_keys // tk
    n_docs = doc_starts.shape[0]
    doc_first = jnp.max(jnp.where(doc_starts <= first_row, doc_starts, 0))
    bounds = jnp.concatenate([
        jnp.stack([doc_first // tk, (first_row + rows_here - 1) // tk, first_row]),
        doc_starts,
    ]).astype(jnp.int32)

    def tile_of(j, b):
        return jnp.minimum(jnp.maximum(j, b[0]), b[1])

    full = lambda shape: pl.BlockSpec(shape, lambda j, b: (0, 0))
    in_specs = [
        full((n_rows, dh)),
        full((n_rows, dh)),
        pl.BlockSpec((n_core, 1, 1, rows_here, 2 * dh),
                     lambda j, b: (0, tile_of(j, b) % n_x, tile_of(j, b) // n_x, 0, 0)),
    ]
    params = pltpu.CompilerParams(dimension_semantics=("arbitrary",))
    mm = 2 * n_rows * n_keys * dh
    log_total, delta = pl.pallas_call(
        functools.partial(_stats_kernel, scaling, tk, dh, rows_here, n_docs),
        grid_spec=pltpu.PrefetchScalarGridSpec(
            num_scalar_prefetch=1,
            grid=(n_tiles,),
            in_specs=in_specs,
            out_specs=[full((n_rows, 1)), full((n_rows, 1))],
            scratch_shapes=[pltpu.VMEM((n_rows, 1), jnp.float32)] * 3,
        ),
        out_shape=[jax.ShapeDtypeStruct((n_rows, 1), jnp.float32)] * 2,
        compiler_params=params,
        cost_estimate=pl.CostEstimate(flops=2 * mm, transcendentals=n_rows * n_keys,
                                      bytes_accessed=n_keys * 4 * dh),
    )(bounds, q_rows, g_rows, kv_full)
    dq, dkv = pl.pallas_call(
        functools.partial(_grad_kernel, scaling, tk, dh, rows_here, n_docs),
        grid_spec=pltpu.PrefetchScalarGridSpec(
            num_scalar_prefetch=1,
            grid=(n_tiles,),
            in_specs=in_specs + [full((n_rows, 1)), full((n_rows, 1))],
            out_specs=[
                full((n_rows, dh)),
                pl.BlockSpec((n_core, 1, 1, rows_here, 2 * dh),
                             lambda j, b: (0, j % n_x, j // n_x, 0, 0)),
            ],
            scratch_shapes=[pltpu.VMEM((n_rows, dh), jnp.float32)],
        ),
        out_shape=[jax.ShapeDtypeStruct((n_rows, dh), jnp.bfloat16),
                   jax.ShapeDtypeStruct((n_core, n_x, n_zh, rows_here, 2 * dh), jnp.bfloat16)],
        compiler_params=params,
        cost_estimate=pl.CostEstimate(flops=5 * mm, transcendentals=n_rows * n_keys,
                                      bytes_accessed=n_keys * 8 * dh),
    )(bounds, q_rows, g_rows, kv_full, log_total, delta)
    return dq, dkv


def stage_reduce(parts, axis, cid):
    n = lax.axis_size(axis)
    me = lax.axis_index(axis)
    slots = peer_blocks(parts.astype(jnp.bfloat16), n, axis, None, True, cid)
    ids = jnp.arange(n, dtype=jnp.int32).reshape((n,) + (1,) * (parts.ndim - 1))
    others = jnp.sum(jnp.where(ids == me, 0.0, slots.astype(jnp.float32)), axis=0)
    return others + lax.dynamic_index_in_dim(parts, me, 0, keepdims=False).astype(jnp.float32)


def stage_gather(block, axis, cid):
    n = lax.axis_size(axis)
    if block.size * n * block.dtype.itemsize <= (1 << 21):
        return peer_blocks(block, n, axis, None, False, cid, own_copy=True)
    slots = peer_blocks(block, n, axis, None, False, cid)
    ids = jnp.arange(n, dtype=jnp.int32).reshape((n,) + (1,) * block.ndim)
    return jnp.where(ids == lax.axis_index(axis), block[None], slots)


def shards(queries, keys, values, d_out, w_out, doc_starts):
    rows_here = queries.shape[0]
    head_size = DH
    groups = keys.shape[1] // head_size
    per_group = queries.shape[1] // keys.shape[1]
    kv_cols = keys.shape[1]
    scaling = 1.0 / math.sqrt(head_size)
    n_zh = lax.axis_size("zhi")
    n_x = lax.axis_size("xx")
    n_core = lax.axis_size("core")
    me = (lax.axis_index("zhi") * n_x + lax.axis_index("xx")) * n_core + lax.axis_index("core")
    first_row = me * rows_here
    my_rows = first_row + jnp.arange(rows_here, dtype=jnp.int32)
    kv_block = jnp.concatenate([keys, values], axis=1)
    for cid, axis in enumerate(("zhi", "xx", "core")):
        kv_block = stage_gather(kv_block, axis, cid + 4)
    attn_grad = lax.dot_general(
        lax.all_gather(d_out, "head", axis=1, tiled=True),
        w_out,
        (((1,), (1,)), ((), ())),
        preferred_element_type=jnp.float32,
    ).astype(jnp.bfloat16)
    heads = groups * per_group
    q_rows = queries.reshape(rows_here, heads, head_size).transpose(1, 0, 2).reshape(
        heads * rows_here, head_size)
    g_rows = attn_grad.reshape(rows_here, heads, head_size).transpose(1, 0, 2).reshape(
        heads * rows_here, head_size)
    dq_rows, kv_terms = attention_grads(
        q_rows, g_rows, kv_block, doc_starts, first_row, rows_here, scaling,
        (n_zh, n_x, n_core))
    query_grad = dq_rows.reshape(heads, rows_here, head_size).transpose(1, 0, 2).reshape(
        rows_here, heads * head_size)
    kv_grad = kv_terms
    for cid, axis in enumerate(("core", "xx", "zhi")):
        kv_grad = stage_reduce(kv_grad, axis, cid + 1)
    kv_grad = kv_grad.astype(jnp.bfloat16)
    key_grad = kv_grad[:, :kv_cols]
    value_grad = kv_grad[:, kv_cols:]
    return (query_grad, key_grad, value_grad)


def solution(mesh):
    n_seq, n_head = mesh.shape["seq"], mesh.shape["head"]
    split = jax.sharding.Mesh(
        mesh.devices.reshape(n_seq // 8, 4, 2, n_head), ("zhi", "xx", "core", "head")
    )
    rows = ("zhi", "xx", "core")
    return jax.shard_map(
        shards,
        mesh=split,
        in_specs=(
            P(rows, "head"),
            P(rows, "head"),
            P(rows, "head"),
            P(rows, "head"),
            P("head", None),
            P(),
        ),
        out_specs=(P(rows, "head"), P(rows, "head"), P(rows, "head")),
        check_vma=False,
    )
```

```python
import functools
import math

import jax
import jax.numpy as jnp
from jax import lax
from jax.sharding import PartitionSpec as P
from jax.experimental import pallas as pl
from jax.experimental.pallas import tpu as pltpu

DH = 128


NEG_FILL = -1e30


def doc_index(doc_starts, places):
    return jnp.sum((places[:, None] >= doc_starts[None, :]).astype(jnp.int32), axis=1)


def allowed_pairs(doc_starts, row_ids, col_ids):
    earlier = col_ids[None, :] <= row_ids[:, None]
    same_doc = doc_index(doc_starts, row_ids)[:, None] == doc_index(doc_starts, col_ids)[None, :]
    return (earlier & same_doc)[None, None]


def _peer_kernel(n, axis, upward, per_target, own_copy, src_ref, out_ref, send_sem, recv_sem,
                 own_sem):
    me = lax.axis_index(axis)
    own = None
    if own_copy:
        own = pltpu.make_async_copy(src_ref, out_ref.at[me], own_sem)
        own.start()
    barrier = pltpu.get_barrier_semaphore()

    def greet(k, carry):
        pl.semaphore_signal(barrier, 1, device_id={axis: lax.rem(me + k, n)},
                            device_id_type=pl.DeviceIdType.MESH)
        return carry

    lax.fori_loop(1, n, greet, 0)
    pl.semaphore_wait(barrier, n - 1)
    step = -1 if upward is False else 1

    def send_desc(k):
        tgt = lax.rem(me + k, n) if upward is None else me + step * k
        src = src_ref.at[tgt] if per_target else src_ref
        return pltpu.make_async_remote_copy(
            src, out_ref.at[me], send_sem.at[k - 1], recv_sem.at[k - 1],
            device_id={axis: tgt}, device_id_type=pl.DeviceIdType.MESH)

    def recv_desc(k):
        origin = lax.rem(me + n - k, n) if upward is None else me - step * k
        src = src_ref.at[me] if per_target else src_ref
        return pltpu.make_async_remote_copy(
            src, out_ref.at[origin], send_sem.at[k - 1], recv_sem.at[k - 1],
            device_id={axis: origin}, device_id_type=pl.DeviceIdType.MESH)

    def can_send(k):
        if upward is None:
            return k > 0
        return (me + k < n) if upward else (me - k >= 0)

    def can_recv(k):
        if upward is None:
            return k > 0
        return (me - k >= 0) if upward else (me + k < n)

    def start_one(k, carry):
        @pl.when(can_send(k))
        def _():
            send_desc(k).start()
        return carry

    def finish_one(k, carry):
        @pl.when(can_send(k))
        def _():
            send_desc(k).wait_send()

        @pl.when(can_recv(k))
        def _():
            recv_desc(k).wait_recv()
        return carry

    lax.fori_loop(1, n, start_one, 0)
    lax.fori_loop(1, n, finish_one, 0)
    if own is not None:
        own.wait()


def peer_blocks(src, n, axis, upward, per_target, cid, own_copy=False):
    blk = src.shape[1:] if per_target else src.shape
    return pl.pallas_call(
        functools.partial(_peer_kernel, n, axis, upward, per_target, own_copy),
        out_shape=jax.ShapeDtypeStruct((n,) + tuple(blk), src.dtype),
        in_specs=[pl.BlockSpec(memory_space=pl.ANY)],
        out_specs=pl.BlockSpec(memory_space=pl.ANY),
        scratch_shapes=[pltpu.SemaphoreType.DMA((n - 1,)), pltpu.SemaphoreType.DMA((n - 1,)),
                        pltpu.SemaphoreType.DMA(())],
        compiler_params=pltpu.CompilerParams(collective_id=cid, has_side_effects=True),
    )(src)


def _tile_mask(j, tk, meta_ref, n_rows, rows_here, n_docs):
    col = j * tk + lax.broadcasted_iota(jnp.int32, (1, tk), 1)
    row = meta_ref[2] + lax.broadcasted_iota(jnp.int32, (n_rows, 1), 0) % rows_here
    col_doc = jnp.zeros((1, tk), jnp.int32)
    row_doc = jnp.zeros((n_rows, 1), jnp.int32)
    for k in range(n_docs):
        start = meta_ref[3 + k]
        col_doc = col_doc + (col >= start).astype(jnp.int32)
        row_doc = row_doc + (row >= start).astype(jnp.int32)
    return (col <= row) & (col_doc == row_doc)


def _key_tile(kv_ref):
    return jnp.concatenate([kv_ref[c, 0, 0] for c in range(kv_ref.shape[0])], axis=0)


def _attn_kernel(scaling, dh, rows_here, n_docs, n_x, meta_ref, q_ref, g_ref, kv_ref,
                 dq_ref, dkv_ref, m_sc, l_sc, a_sc, dq_sc):
    n_core = kv_ref.shape[0]
    tk = n_core * rows_here
    n_rows = q_ref.shape[0]
    lo, hi = meta_ref[0], meta_ref[1]
    dims = (((1,), (1,)), ((), ()))
    tdims = (((0,), (0,)), ((), ()))

    def key_tile(t):
        x, zh = t % n_x, t // n_x
        return jnp.concatenate([kv_ref[c, x, zh] for c in range(n_core)], axis=0)

    m_sc[...] = jnp.full(m_sc.shape, NEG_FILL, jnp.float32)
    l_sc[...] = jnp.zeros(l_sc.shape, jnp.float32)
    a_sc[...] = jnp.zeros(a_sc.shape, jnp.float32)

    def stats_body(t, carry):
        kv = key_tile(t)
        scores = lax.dot_general(q_ref[...], kv[:, :dh], dims,
                                 preferred_element_type=jnp.float32) * scaling
        allowed = _tile_mask(t, tk, meta_ref, n_rows, rows_here, n_docs)
        scores = jnp.where(allowed, scores, NEG_FILL)
        m_old = m_sc[...]
        m_new = jnp.maximum(m_old, jnp.max(scores, axis=1, keepdims=True))
        e = jnp.where(allowed, jnp.exp(scores - m_new), 0.0)
        gd = lax.dot_general(g_ref[...], kv[:, dh:], dims,
                             preferred_element_type=jnp.float32)
        alpha = jnp.exp(m_old - m_new)
        l_sc[...] = alpha * l_sc[...] + jnp.sum(e, axis=1, keepdims=True)
        a_sc[...] = alpha * a_sc[...] + jnp.sum(e * gd, axis=1, keepdims=True)
        m_sc[...] = m_new
        return carry

    lax.fori_loop(lo, hi + 1, stats_body, 0)
    m_sc[...] = m_sc[...] + jnp.log(l_sc[...])
    a_sc[...] = a_sc[...] / l_sc[...]
    dq_sc[...] = jnp.zeros(dq_sc.shape, jnp.float32)
    dkv_ref[...] = jnp.zeros(dkv_ref.shape, dkv_ref.dtype)

    def grad_body(t, carry):
        kv = key_tile(t)
        k_t = kv[:, :dh]
        scores = lax.dot_general(q_ref[...], k_t, dims,
                                 preferred_element_type=jnp.float32) * scaling
        allowed = _tile_mask(t, tk, meta_ref, n_rows, rows_here, n_docs)
        probs = jnp.where(allowed, jnp.exp(scores - m_sc[...]), 0.0)
        gd = lax.dot_general(g_ref[...], kv[:, dh:], dims,
                             preferred_element_type=jnp.float32)
        ds = (probs * (gd - a_sc[...]) * scaling).astype(jnp.bfloat16)
        dq_sc[...] += jnp.dot(ds, k_t, preferred_element_type=jnp.float32)
        dk = lax.dot_general(ds, q_ref[...], tdims, preferred_element_type=jnp.float32)
        dv = lax.dot_general(probs.astype(jnp.bfloat16), g_ref[...], tdims,
                             preferred_element_type=jnp.float32)
        x, zh = t % n_x, t // n_x
        for c in range(n_core):
            part = slice(c * rows_here, (c + 1) * rows_here)
            dkv_ref[c, x, zh, :, :dh] = dk[part].astype(dkv_ref.dtype)
            dkv_ref[c, x, zh, :, dh:] = dv[part].astype(dkv_ref.dtype)
        return carry

    lax.fori_loop(lo, hi + 1, grad_body, 0)
    dq_ref[...] = dq_sc[...].astype(dq_ref.dtype)


def attention_grads(q_rows, g_rows, kv_full, doc_starts, first_row, rows_here, scaling, chips):
    n_rows, dh = q_rows.shape
    n_zh, n_x, n_core = chips
    n_keys = n_core * n_x * n_zh * rows_here
    tk = n_core * rows_here
    n_docs = doc_starts.shape[0]
    doc_first = jnp.max(jnp.where(doc_starts <= first_row, doc_starts, 0))
    meta = jnp.concatenate([
        jnp.stack([doc_first // tk, (first_row + rows_here - 1) // tk, first_row]),
        doc_starts,
    ]).astype(jnp.int32)
    vmem = pl.BlockSpec(memory_space=pltpu.VMEM)
    mm = 2 * n_rows * n_keys * dh
    dq, dkv = pl.pallas_call(
        functools.partial(_attn_kernel, scaling, dh, rows_here, n_docs, n_x),
        in_specs=[pl.BlockSpec(memory_space=pltpu.SMEM), vmem, vmem, vmem],
        out_specs=[vmem, vmem],
        out_shape=[jax.ShapeDtypeStruct((n_rows, dh), jnp.bfloat16),
                   jax.ShapeDtypeStruct((n_core, n_x, n_zh, rows_here, 2 * dh), jnp.bfloat16)],
        scratch_shapes=[pltpu.VMEM((n_rows, 1), jnp.float32)] * 3
        + [pltpu.VMEM((n_rows, dh), jnp.float32)],
        cost_estimate=pl.CostEstimate(flops=7 * mm, transcendentals=2 * n_rows * n_keys,
                                      bytes_accessed=n_keys * 8 * dh),
    )(meta, q_rows, g_rows, kv_full)
    return dq, dkv

def stage_reduce(parts, axis, cid):
    n = lax.axis_size(axis)
    me = lax.axis_index(axis)
    slots = peer_blocks(parts.astype(jnp.bfloat16), n, axis, None, True, cid)
    ids = jnp.arange(n, dtype=jnp.int32).reshape((n,) + (1,) * (parts.ndim - 1))
    others = jnp.sum(jnp.where(ids == me, 0.0, slots.astype(jnp.float32)), axis=0)
    return others + lax.dynamic_index_in_dim(parts, me, 0, keepdims=False).astype(jnp.float32)


def stage_gather(block, axis, cid):
    n = lax.axis_size(axis)
    if block.size * n * block.dtype.itemsize <= (1 << 21):
        return peer_blocks(block, n, axis, None, False, cid, own_copy=True)
    slots = peer_blocks(block, n, axis, None, False, cid)
    ids = jnp.arange(n, dtype=jnp.int32).reshape((n,) + (1,) * block.ndim)
    return jnp.where(ids == lax.axis_index(axis), block[None], slots)


def shards(queries, keys, values, d_out, w_out, doc_starts):
    rows_here = queries.shape[0]
    head_size = DH
    groups = keys.shape[1] // head_size
    per_group = queries.shape[1] // keys.shape[1]
    kv_cols = keys.shape[1]
    scaling = 1.0 / math.sqrt(head_size)
    n_zh = lax.axis_size("zhi")
    n_x = lax.axis_size("xx")
    n_core = lax.axis_size("core")
    me = (lax.axis_index("zhi") * n_x + lax.axis_index("xx")) * n_core + lax.axis_index("core")
    first_row = me * rows_here
    my_rows = first_row + jnp.arange(rows_here, dtype=jnp.int32)
    kv_block = jnp.concatenate([keys, values], axis=1)
    for cid, axis in enumerate(("zhi", "xx", "core")):
        kv_block = stage_gather(kv_block, axis, cid + 4)
    attn_grad = lax.dot_general(
        lax.all_gather(d_out, "head", axis=1, tiled=True),
        w_out,
        (((1,), (1,)), ((), ())),
        preferred_element_type=jnp.float32,
    ).astype(jnp.bfloat16)
    heads = groups * per_group
    q_rows = queries.reshape(rows_here, heads, head_size).transpose(1, 0, 2).reshape(
        heads * rows_here, head_size)
    g_rows = attn_grad.reshape(rows_here, heads, head_size).transpose(1, 0, 2).reshape(
        heads * rows_here, head_size)
    dq_rows, kv_terms = attention_grads(
        q_rows, g_rows, kv_block, doc_starts, first_row, rows_here, scaling,
        (n_zh, n_x, n_core))
    query_grad = dq_rows.reshape(heads, rows_here, head_size).transpose(1, 0, 2).reshape(
        rows_here, heads * head_size)
    kv_grad = kv_terms
    for cid, axis in enumerate(("core", "xx", "zhi")):
        kv_grad = stage_reduce(kv_grad, axis, cid + 1)
    kv_grad = kv_grad.astype(jnp.bfloat16)
    key_grad = kv_grad[:, :kv_cols]
    value_grad = kv_grad[:, kv_cols:]
    return (query_grad, key_grad, value_grad)


def solution(mesh):
    n_seq, n_head = mesh.shape["seq"], mesh.shape["head"]
    split = jax.sharding.Mesh(
        mesh.devices.reshape(n_seq // 8, 4, 2, n_head), ("zhi", "xx", "core", "head")
    )
    rows = ("zhi", "xx", "core")
    return jax.shard_map(
        shards,
        mesh=split,
        in_specs=(
            P(rows, "head"),
            P(rows, "head"),
            P(rows, "head"),
            P(rows, "head"),
            P("head", None),
            P(),
        ),
        out_specs=(P(rows, "head"), P(rows, "head"), P(rows, "head")),
        check_vma=False,
    )
```

```python
import functools
import math

import jax
import jax.numpy as jnp
from jax import lax
from jax.sharding import PartitionSpec as P
from jax.experimental import pallas as pl
from jax.experimental.pallas import tpu as pltpu

DH = 128


NEG_FILL = -1e30


def doc_index(doc_starts, places):
    return jnp.sum((places[:, None] >= doc_starts[None, :]).astype(jnp.int32), axis=1)


def allowed_pairs(doc_starts, row_ids, col_ids):
    earlier = col_ids[None, :] <= row_ids[:, None]
    same_doc = doc_index(doc_starts, row_ids)[:, None] == doc_index(doc_starts, col_ids)[None, :]
    return (earlier & same_doc)[None, None]


def _peer_kernel(n, axis, upward, per_target, own_copy, src_ref, out_ref, send_sem, recv_sem,
                 own_sem):
    me = lax.axis_index(axis)
    own = None
    if own_copy:
        own = pltpu.make_async_copy(src_ref, out_ref.at[me], own_sem)
        own.start()
    barrier = pltpu.get_barrier_semaphore()

    def greet(k, carry):
        pl.semaphore_signal(barrier, 1, device_id={axis: lax.rem(me + k, n)},
                            device_id_type=pl.DeviceIdType.MESH)
        return carry

    lax.fori_loop(1, n, greet, 0)
    pl.semaphore_wait(barrier, n - 1)
    step = -1 if upward is False else 1

    def send_desc(k):
        tgt = lax.rem(me + k, n) if upward is None else me + step * k
        src = src_ref.at[tgt] if per_target else src_ref
        return pltpu.make_async_remote_copy(
            src, out_ref.at[me], send_sem.at[k - 1], recv_sem.at[k - 1],
            device_id={axis: tgt}, device_id_type=pl.DeviceIdType.MESH)

    def recv_desc(k):
        origin = lax.rem(me + n - k, n) if upward is None else me - step * k
        src = src_ref.at[me] if per_target else src_ref
        return pltpu.make_async_remote_copy(
            src, out_ref.at[origin], send_sem.at[k - 1], recv_sem.at[k - 1],
            device_id={axis: origin}, device_id_type=pl.DeviceIdType.MESH)

    def can_send(k):
        if upward is None:
            return k > 0
        return (me + k < n) if upward else (me - k >= 0)

    def can_recv(k):
        if upward is None:
            return k > 0
        return (me - k >= 0) if upward else (me + k < n)

    def start_one(k, carry):
        @pl.when(can_send(k))
        def _():
            send_desc(k).start()
        return carry

    def finish_one(k, carry):
        @pl.when(can_send(k))
        def _():
            send_desc(k).wait_send()

        @pl.when(can_recv(k))
        def _():
            recv_desc(k).wait_recv()
        return carry

    lax.fori_loop(1, n, start_one, 0)
    lax.fori_loop(1, n, finish_one, 0)
    if own is not None:
        own.wait()


def peer_blocks(src, n, axis, upward, per_target, cid, own_copy=False):
    blk = src.shape[1:] if per_target else src.shape
    return pl.pallas_call(
        functools.partial(_peer_kernel, n, axis, upward, per_target, own_copy),
        out_shape=jax.ShapeDtypeStruct((n,) + tuple(blk), src.dtype),
        in_specs=[pl.BlockSpec(memory_space=pl.ANY)],
        out_specs=pl.BlockSpec(memory_space=pl.ANY),
        scratch_shapes=[pltpu.SemaphoreType.DMA((n - 1,)), pltpu.SemaphoreType.DMA((n - 1,)),
                        pltpu.SemaphoreType.DMA(())],
        compiler_params=pltpu.CompilerParams(collective_id=cid, has_side_effects=True),
    )(src)


def _tile_mask(j, tk, meta_ref, n_rows, rows_here, n_docs):
    col = j * tk + lax.broadcasted_iota(jnp.int32, (1, tk), 1)
    row = meta_ref[2] + lax.broadcasted_iota(jnp.int32, (n_rows, 1), 0) % rows_here
    col_doc = jnp.zeros((1, tk), jnp.int32)
    row_doc = jnp.zeros((n_rows, 1), jnp.int32)
    for k in range(n_docs):
        start = meta_ref[3 + k]
        col_doc = col_doc + (col >= start).astype(jnp.int32)
        row_doc = row_doc + (row >= start).astype(jnp.int32)
    return (col <= row) & (col_doc == row_doc)


def _key_tile(kv_ref):
    return jnp.concatenate([kv_ref[c, 0, 0] for c in range(kv_ref.shape[0])], axis=0)


def _stats_kernel(scaling, tk, dh, rows_here, n_docs, bounds_ref, q_ref, g_ref, kv_ref,
                  lt_ref, delta_ref, m_sc, l_sc, a_sc):
    j = pl.program_id(0)

    @pl.when(j == 0)
    def _():
        m_sc[...] = jnp.full(m_sc.shape, NEG_FILL, jnp.float32)
        l_sc[...] = jnp.zeros(l_sc.shape, jnp.float32)
        a_sc[...] = jnp.zeros(a_sc.shape, jnp.float32)

    @pl.when((j >= bounds_ref[0]) & (j <= bounds_ref[1]))
    def _():
        dims = (((1,), (1,)), ((), ()))
        kv = _key_tile(kv_ref)
        scores = lax.dot_general(q_ref[...], kv[:, :dh], dims,
                                 preferred_element_type=jnp.float32) * scaling
        allowed = _tile_mask(j, tk, bounds_ref, q_ref.shape[0], rows_here, n_docs)
        scores = jnp.where(allowed, scores, NEG_FILL)
        m_old = m_sc[...]
        m_new = jnp.maximum(m_old, jnp.max(scores, axis=1, keepdims=True))
        e = jnp.where(allowed, jnp.exp(scores - m_new), 0.0)
        gd = lax.dot_general(g_ref[...], kv[:, dh:], dims,
                             preferred_element_type=jnp.float32)
        alpha = jnp.exp(m_old - m_new)
        l_sc[...] = alpha * l_sc[...] + jnp.sum(e, axis=1, keepdims=True)
        a_sc[...] = alpha * a_sc[...] + jnp.sum(e * gd, axis=1, keepdims=True)
        m_sc[...] = m_new

    @pl.when(j == pl.num_programs(0) - 1)
    def _():
        lt_ref[...] = m_sc[...] + jnp.log(l_sc[...])
        delta_ref[...] = a_sc[...] / l_sc[...]


def _grad_kernel(scaling, tk, dh, rows_here, n_docs, bounds_ref, q_ref, g_ref, kv_ref,
                 lt_ref, delta_ref, dq_ref, dkv_ref, dq_sc):
    j = pl.program_id(0)
    active = (j >= bounds_ref[0]) & (j <= bounds_ref[1])

    @pl.when(j == 0)
    def _():
        dq_sc[...] = jnp.zeros(dq_sc.shape, jnp.float32)

    @pl.when(active)
    def _():
        dims = (((1,), (1,)), ((), ()))
        tdims = (((0,), (0,)), ((), ()))
        kv = _key_tile(kv_ref)
        k_t = kv[:, :dh]
        scores = lax.dot_general(q_ref[...], k_t, dims,
                                 preferred_element_type=jnp.float32) * scaling
        allowed = _tile_mask(j, tk, bounds_ref, q_ref.shape[0], rows_here, n_docs)
        probs = jnp.where(allowed, jnp.exp(scores - lt_ref[...]), 0.0)
        gd = lax.dot_general(g_ref[...], kv[:, dh:], dims,
                             preferred_element_type=jnp.float32)
        ds = (probs * (gd - delta_ref[...]) * scaling).astype(jnp.bfloat16)
        dq_sc[...] += jnp.dot(ds, k_t, preferred_element_type=jnp.float32)
        dk = lax.dot_general(ds, q_ref[...], tdims, preferred_element_type=jnp.float32)
        dv = lax.dot_general(probs.astype(jnp.bfloat16), g_ref[...], tdims,
                             preferred_element_type=jnp.float32)
        owner_rows = dkv_ref.shape[3]
        for c in range(dkv_ref.shape[0]):
            part = slice(c * owner_rows, (c + 1) * owner_rows)
            dkv_ref[c, 0, 0, :, :dh] = dk[part].astype(dkv_ref.dtype)
            dkv_ref[c, 0, 0, :, dh:] = dv[part].astype(dkv_ref.dtype)

    @pl.when(jnp.logical_not(active))
    def _():
        dkv_ref[...] = jnp.zeros(dkv_ref.shape, dkv_ref.dtype)

    @pl.when(j == pl.num_programs(0) - 1)
    def _():
        dq_ref[...] = dq_sc[...].astype(dq_ref.dtype)


def attention_grads(q_rows, g_rows, kv_full, doc_starts, first_row, rows_here, scaling, chips):
    n_rows, dh = q_rows.shape
    n_keys = kv_full.shape[0] * kv_full.shape[1] * kv_full.shape[2] * kv_full.shape[3]
    n_zh, n_x, n_core = chips
    tk = n_core * rows_here
    n_tiles = n_keys // tk
    n_docs = doc_starts.shape[0]
    doc_first = jnp.max(jnp.where(doc_starts <= first_row, doc_starts, 0))
    bounds = jnp.concatenate([
        jnp.stack([doc_first // tk, (first_row + rows_here - 1) // tk, first_row]),
        doc_starts,
    ]).astype(jnp.int32)

    def tile_of(j, b):
        return jnp.minimum(jnp.maximum(j, b[0]), b[1])

    full = lambda shape: pl.BlockSpec(shape, lambda j, b: (0, 0))
    in_specs = [
        full((n_rows, dh)),
        full((n_rows, dh)),
        pl.BlockSpec((n_core, 1, 1, rows_here, 2 * dh),
                     lambda j, b: (0, tile_of(j, b) % n_x, tile_of(j, b) // n_x, 0, 0)),
    ]
    params = pltpu.CompilerParams(dimension_semantics=("arbitrary",))
    mm = 2 * n_rows * n_keys * dh
    log_total, delta = pl.pallas_call(
        functools.partial(_stats_kernel, scaling, tk, dh, rows_here, n_docs),
        grid_spec=pltpu.PrefetchScalarGridSpec(
            num_scalar_prefetch=1,
            grid=(n_tiles,),
            in_specs=in_specs,
            out_specs=[full((n_rows, 1)), full((n_rows, 1))],
            scratch_shapes=[pltpu.VMEM((n_rows, 1), jnp.float32)] * 3,
        ),
        out_shape=[jax.ShapeDtypeStruct((n_rows, 1), jnp.float32)] * 2,
        compiler_params=params,
        cost_estimate=pl.CostEstimate(flops=2 * mm, transcendentals=n_rows * n_keys,
                                      bytes_accessed=n_keys * 4 * dh),
    )(bounds, q_rows, g_rows, kv_full)
    dq, dkv = pl.pallas_call(
        functools.partial(_grad_kernel, scaling, tk, dh, rows_here, n_docs),
        grid_spec=pltpu.PrefetchScalarGridSpec(
            num_scalar_prefetch=1,
            grid=(n_tiles,),
            in_specs=in_specs + [full((n_rows, 1)), full((n_rows, 1))],
            out_specs=[
                full((n_rows, dh)),
                pl.BlockSpec((n_core, 1, 1, rows_here, 2 * dh),
                             lambda j, b: (0, j % n_x, j // n_x, 0, 0)),
            ],
            scratch_shapes=[pltpu.VMEM((n_rows, dh), jnp.float32)],
        ),
        out_shape=[jax.ShapeDtypeStruct((n_rows, dh), jnp.bfloat16),
                   jax.ShapeDtypeStruct((n_core, n_x, n_zh, rows_here, 2 * dh), jnp.bfloat16)],
        compiler_params=params,
        cost_estimate=pl.CostEstimate(flops=5 * mm, transcendentals=n_rows * n_keys,
                                      bytes_accessed=n_keys * 8 * dh),
    )(bounds, q_rows, g_rows, kv_full, log_total, delta)
    return dq, dkv


def stage_reduce(parts, axis, cid):
    n = lax.axis_size(axis)
    me = lax.axis_index(axis)
    slots = peer_blocks(parts.astype(jnp.bfloat16), n, axis, None, True, cid)
    ids = jnp.arange(n, dtype=jnp.int32).reshape((n,) + (1,) * (parts.ndim - 1))
    total = lax.dynamic_index_in_dim(parts, me, 0, keepdims=False).astype(jnp.float32)
    for i in range(n):
        total = total + jnp.where(me == i, 0.0, slots[i].astype(jnp.float32))
    return total.astype(jnp.bfloat16)


def stage_gather(block, axis, cid):
    n = lax.axis_size(axis)
    if block.size * n * block.dtype.itemsize <= (1 << 21):
        return peer_blocks(block, n, axis, None, False, cid, own_copy=True)
    slots = peer_blocks(block, n, axis, None, False, cid)
    ids = jnp.arange(n, dtype=jnp.int32).reshape((n,) + (1,) * block.ndim)
    return jnp.where(ids == lax.axis_index(axis), block[None], slots)


def shards(queries, keys, values, d_out, w_out, doc_starts):
    rows_here = queries.shape[0]
    head_size = DH
    groups = keys.shape[1] // head_size
    per_group = queries.shape[1] // keys.shape[1]
    kv_cols = keys.shape[1]
    scaling = 1.0 / math.sqrt(head_size)
    n_zh = lax.axis_size("zhi")
    n_x = lax.axis_size("xx")
    n_core = lax.axis_size("core")
    me = (lax.axis_index("zhi") * n_x + lax.axis_index("xx")) * n_core + lax.axis_index("core")
    first_row = me * rows_here
    my_rows = first_row + jnp.arange(rows_here, dtype=jnp.int32)
    kv_block = jnp.concatenate([keys, values], axis=1)
    for cid, axis in enumerate(("zhi", "xx", "core")):
        kv_block = stage_gather(kv_block, axis, cid + 4)
    attn_grad = lax.dot_general(
        lax.all_gather(d_out, "head", axis=1, tiled=True),
        w_out,
        (((1,), (1,)), ((), ())),
        preferred_element_type=jnp.float32,
    ).astype(jnp.bfloat16)
    heads = groups * per_group
    q_rows = queries.reshape(rows_here, heads, head_size).transpose(1, 0, 2).reshape(
        heads * rows_here, head_size)
    g_rows = attn_grad.reshape(rows_here, heads, head_size).transpose(1, 0, 2).reshape(
        heads * rows_here, head_size)
    dq_rows, kv_terms = attention_grads(
        q_rows, g_rows, kv_block, doc_starts, first_row, rows_here, scaling,
        (n_zh, n_x, n_core))
    query_grad = dq_rows.reshape(heads, rows_here, head_size).transpose(1, 0, 2).reshape(
        rows_here, heads * head_size)
    kv_grad = kv_terms
    for cid, axis in enumerate(("core", "xx", "zhi")):
        kv_grad = stage_reduce(kv_grad, axis, cid + 1)
    kv_grad = kv_grad.astype(jnp.bfloat16)
    key_grad = kv_grad[:, :kv_cols]
    value_grad = kv_grad[:, kv_cols:]
    return (query_grad, key_grad, value_grad)


def solution(mesh):
    n_seq, n_head = mesh.shape["seq"], mesh.shape["head"]
    split = jax.sharding.Mesh(
        mesh.devices.reshape(n_seq // 8, 4, 2, n_head), ("zhi", "xx", "core", "head")
    )
    rows = ("zhi", "xx", "core")
    return jax.shard_map(
        shards,
        mesh=split,
        in_specs=(
            P(rows, "head"),
            P(rows, "head"),
            P(rows, "head"),
            P(rows, "head"),
            P("head", None),
            P(),
        ),
        out_specs=(P(rows, "head"), P(rows, "head"), P(rows, "head")),
        check_vma=False,
    )
```

```python
import functools
import math

import jax
import jax.numpy as jnp
from jax import lax
from jax.sharding import PartitionSpec as P
from jax.experimental import pallas as pl
from jax.experimental.pallas import tpu as pltpu

DH = 128


NEG_FILL = -1e30


def doc_index(doc_starts, places):
    return jnp.sum((places[:, None] >= doc_starts[None, :]).astype(jnp.int32), axis=1)


def allowed_pairs(doc_starts, row_ids, col_ids):
    earlier = col_ids[None, :] <= row_ids[:, None]
    same_doc = doc_index(doc_starts, row_ids)[:, None] == doc_index(doc_starts, col_ids)[None, :]
    return (earlier & same_doc)[None, None]


def _peer_kernel(n, axis, upward, per_target, own_copy, src_ref, out_ref, send_sem, recv_sem,
                 own_sem):
    me = lax.axis_index(axis)
    own = None
    if own_copy:
        own = pltpu.make_async_copy(src_ref, out_ref.at[me], own_sem)
        own.start()
    barrier = pltpu.get_barrier_semaphore()

    def greet(k, carry):
        pl.semaphore_signal(barrier, 1, device_id={axis: lax.rem(me + k, n)},
                            device_id_type=pl.DeviceIdType.MESH)
        return carry

    lax.fori_loop(1, n, greet, 0)
    pl.semaphore_wait(barrier, n - 1)
    step = -1 if upward is False else 1

    def send_desc(k):
        tgt = lax.rem(me + k, n) if upward is None else me + step * k
        src = src_ref.at[tgt] if per_target else src_ref
        return pltpu.make_async_remote_copy(
            src, out_ref.at[me], send_sem.at[k - 1], recv_sem.at[k - 1],
            device_id={axis: tgt}, device_id_type=pl.DeviceIdType.MESH)

    def recv_desc(k):
        origin = lax.rem(me + n - k, n) if upward is None else me - step * k
        src = src_ref.at[me] if per_target else src_ref
        return pltpu.make_async_remote_copy(
            src, out_ref.at[origin], send_sem.at[k - 1], recv_sem.at[k - 1],
            device_id={axis: origin}, device_id_type=pl.DeviceIdType.MESH)

    def can_send(k):
        if upward is None:
            return k > 0
        return (me + k < n) if upward else (me - k >= 0)

    def can_recv(k):
        if upward is None:
            return k > 0
        return (me - k >= 0) if upward else (me + k < n)

    def start_one(k, carry):
        @pl.when(can_send(k))
        def _():
            send_desc(k).start()
        return carry

    def finish_one(k, carry):
        @pl.when(can_send(k))
        def _():
            send_desc(k).wait_send()

        @pl.when(can_recv(k))
        def _():
            recv_desc(k).wait_recv()
        return carry

    lax.fori_loop(1, n, start_one, 0)
    lax.fori_loop(1, n, finish_one, 0)
    if own is not None:
        own.wait()


def peer_blocks(src, n, axis, upward, per_target, cid, own_copy=False):
    blk = src.shape[1:] if per_target else src.shape
    return pl.pallas_call(
        functools.partial(_peer_kernel, n, axis, upward, per_target, own_copy),
        out_shape=jax.ShapeDtypeStruct((n,) + tuple(blk), src.dtype),
        in_specs=[pl.BlockSpec(memory_space=pl.ANY)],
        out_specs=pl.BlockSpec(memory_space=pl.ANY),
        scratch_shapes=[pltpu.SemaphoreType.DMA((n - 1,)), pltpu.SemaphoreType.DMA((n - 1,)),
                        pltpu.SemaphoreType.DMA(())],
        compiler_params=pltpu.CompilerParams(collective_id=cid, has_side_effects=True),
    )(src)


def _tile_mask(j, tk, meta_ref, n_rows, rows_here, n_docs):
    col = j * tk + lax.broadcasted_iota(jnp.int32, (1, tk), 1)
    row = meta_ref[2] + lax.broadcasted_iota(jnp.int32, (n_rows, 1), 0) % rows_here
    col_doc = jnp.zeros((1, tk), jnp.int32)
    row_doc = jnp.zeros((n_rows, 1), jnp.int32)
    for k in range(n_docs):
        start = meta_ref[3 + k]
        col_doc = col_doc + (col >= start).astype(jnp.int32)
        row_doc = row_doc + (row >= start).astype(jnp.int32)
    return (col <= row) & (col_doc == row_doc)


def _key_tile(kv_ref):
    return jnp.concatenate([kv_ref[c, 0, 0] for c in range(kv_ref.shape[0])], axis=0)


def _stats_kernel(scaling, tk, dh, rows_here, n_docs, bounds_ref, q_ref, g_ref, kv_ref,
                  lt_ref, delta_ref, m_sc, l_sc, a_sc):
    j = pl.program_id(0)

    @pl.when(j == 0)
    def _():
        m_sc[...] = jnp.full(m_sc.shape, NEG_FILL, jnp.float32)
        l_sc[...] = jnp.zeros(l_sc.shape, jnp.float32)
        a_sc[...] = jnp.zeros(a_sc.shape, jnp.float32)

    @pl.when((j >= bounds_ref[0]) & (j <= bounds_ref[1]))
    def _():
        dims = (((1,), (1,)), ((), ()))
        kv = _key_tile(kv_ref)
        scores = lax.dot_general(q_ref[...], kv[:, :dh], dims,
                                 preferred_element_type=jnp.float32) * scaling
        allowed = _tile_mask(j, tk, bounds_ref, q_ref.shape[0], rows_here, n_docs)
        scores = jnp.where(allowed, scores, NEG_FILL)
        m_old = m_sc[...]
        m_new = jnp.maximum(m_old, jnp.max(scores, axis=1, keepdims=True))
        e = jnp.where(allowed, jnp.exp(scores - m_new), 0.0)
        gd = lax.dot_general(g_ref[...], kv[:, dh:], dims,
                             preferred_element_type=jnp.float32)
        alpha = jnp.exp(m_old - m_new)
        l_sc[...] = alpha * l_sc[...] + jnp.sum(e, axis=1, keepdims=True)
        a_sc[...] = alpha * a_sc[...] + jnp.sum(e * gd, axis=1, keepdims=True)
        m_sc[...] = m_new

    @pl.when(j == pl.num_programs(0) - 1)
    def _():
        lt_ref[...] = m_sc[...] + jnp.log(l_sc[...])
        delta_ref[...] = a_sc[...] / l_sc[...]


def _grad_kernel(scaling, tk, dh, rows_here, n_docs, bounds_ref, q_ref, g_ref, kv_ref,
                 lt_ref, delta_ref, dq_ref, dkv_ref, dq_sc):
    j = pl.program_id(0)
    active = (j >= bounds_ref[0]) & (j <= bounds_ref[1])

    @pl.when(j == 0)
    def _():
        dq_sc[...] = jnp.zeros(dq_sc.shape, jnp.float32)

    @pl.when(active)
    def _():
        dims = (((1,), (1,)), ((), ()))
        tdims = (((0,), (0,)), ((), ()))
        kv = _key_tile(kv_ref)
        k_t = kv[:, :dh]
        scores = lax.dot_general(q_ref[...], k_t, dims,
                                 preferred_element_type=jnp.float32) * scaling
        allowed = _tile_mask(j, tk, bounds_ref, q_ref.shape[0], rows_here, n_docs)
        probs = jnp.where(allowed, jnp.exp(scores - lt_ref[...]), 0.0)
        gd = lax.dot_general(g_ref[...], kv[:, dh:], dims,
                             preferred_element_type=jnp.float32)
        ds = (probs * (gd - delta_ref[...]) * scaling).astype(jnp.bfloat16)
        dq_sc[...] += jnp.dot(ds, k_t, preferred_element_type=jnp.float32)
        dk = lax.dot_general(ds, q_ref[...], tdims, preferred_element_type=jnp.float32)
        dv = lax.dot_general(probs.astype(jnp.bfloat16), g_ref[...], tdims,
                             preferred_element_type=jnp.float32)
        owner_rows = dkv_ref.shape[3]
        for c in range(dkv_ref.shape[0]):
            part = slice(c * owner_rows, (c + 1) * owner_rows)
            dkv_ref[c, 0, 0, :, :dh] = dk[part].astype(dkv_ref.dtype)
            dkv_ref[c, 0, 0, :, dh:] = dv[part].astype(dkv_ref.dtype)

    @pl.when(jnp.logical_not(active))
    def _():
        dkv_ref[...] = jnp.zeros(dkv_ref.shape, dkv_ref.dtype)

    @pl.when(j == pl.num_programs(0) - 1)
    def _():
        for h in range(dq_ref.shape[1] // dh):
            dq_ref[:, h * dh:(h + 1) * dh] = dq_sc[h * rows_here:(h + 1) * rows_here, :].astype(
                dq_ref.dtype)


def attention_grads(q_rows, g_rows, kv_full, doc_starts, first_row, rows_here, scaling, chips):
    n_rows, dh = q_rows.shape
    n_keys = kv_full.shape[0] * kv_full.shape[1] * kv_full.shape[2] * kv_full.shape[3]
    n_zh, n_x, n_core = chips
    tk = n_core * rows_here
    n_tiles = n_keys // tk
    n_docs = doc_starts.shape[0]
    doc_first = jnp.max(jnp.where(doc_starts <= first_row, doc_starts, 0))
    bounds = jnp.concatenate([
        jnp.stack([doc_first // tk, (first_row + rows_here - 1) // tk, first_row]),
        doc_starts,
    ]).astype(jnp.int32)

    def tile_of(j, b):
        return jnp.minimum(jnp.maximum(j, b[0]), b[1])

    full = lambda shape: pl.BlockSpec(shape, lambda j, b: (0, 0))
    in_specs = [
        full((n_rows, dh)),
        full((n_rows, dh)),
        pl.BlockSpec((n_core, 1, 1, rows_here, 2 * dh),
                     lambda j, b: (0, tile_of(j, b) % n_x, tile_of(j, b) // n_x, 0, 0)),
    ]
    params = pltpu.CompilerParams(dimension_semantics=("arbitrary",))
    mm = 2 * n_rows * n_keys * dh
    log_total, delta = pl.pallas_call(
        functools.partial(_stats_kernel, scaling, tk, dh, rows_here, n_docs),
        grid_spec=pltpu.PrefetchScalarGridSpec(
            num_scalar_prefetch=1,
            grid=(n_tiles,),
            in_specs=in_specs,
            out_specs=[full((n_rows, 1)), full((n_rows, 1))],
            scratch_shapes=[pltpu.VMEM((n_rows, 1), jnp.float32)] * 3,
        ),
        out_shape=[jax.ShapeDtypeStruct((n_rows, 1), jnp.float32)] * 2,
        compiler_params=params,
        cost_estimate=pl.CostEstimate(flops=2 * mm, transcendentals=n_rows * n_keys,
                                      bytes_accessed=n_keys * 4 * dh),
    )(bounds, q_rows, g_rows, kv_full)
    dq, dkv = pl.pallas_call(
        functools.partial(_grad_kernel, scaling, tk, dh, rows_here, n_docs),
        grid_spec=pltpu.PrefetchScalarGridSpec(
            num_scalar_prefetch=1,
            grid=(n_tiles,),
            in_specs=in_specs + [full((n_rows, 1)), full((n_rows, 1))],
            out_specs=[
                full((rows_here, n_rows // rows_here * dh)),
                pl.BlockSpec((n_core, 1, 1, rows_here, 2 * dh),
                             lambda j, b: (0, j % n_x, j // n_x, 0, 0)),
            ],
            scratch_shapes=[pltpu.VMEM((n_rows, dh), jnp.float32)],
        ),
        out_shape=[jax.ShapeDtypeStruct((rows_here, n_rows // rows_here * dh), jnp.bfloat16),
                   jax.ShapeDtypeStruct((n_core, n_x, n_zh, rows_here, 2 * dh), jnp.bfloat16)],
        compiler_params=params,
        cost_estimate=pl.CostEstimate(flops=5 * mm, transcendentals=n_rows * n_keys,
                                      bytes_accessed=n_keys * 8 * dh),
    )(bounds, q_rows, g_rows, kv_full, log_total, delta)
    return dq, dkv


def stage_reduce(parts, axis, cid):
    n = lax.axis_size(axis)
    me = lax.axis_index(axis)
    slots = peer_blocks(parts.astype(jnp.bfloat16), n, axis, None, True, cid)
    ids = jnp.arange(n, dtype=jnp.int32).reshape((n,) + (1,) * (parts.ndim - 1))
    others = jnp.sum(jnp.where(ids == me, 0.0, slots.astype(jnp.float32)), axis=0)
    return others + lax.dynamic_index_in_dim(parts, me, 0, keepdims=False).astype(jnp.float32)


def stage_gather(block, axis, cid):
    n = lax.axis_size(axis)
    if block.size * n * block.dtype.itemsize <= (1 << 21):
        return peer_blocks(block, n, axis, None, False, cid, own_copy=True)
    slots = peer_blocks(block, n, axis, None, False, cid)
    ids = jnp.arange(n, dtype=jnp.int32).reshape((n,) + (1,) * block.ndim)
    return jnp.where(ids == lax.axis_index(axis), block[None], slots)


def shards(queries, keys, values, d_out, w_out, doc_starts):
    rows_here = queries.shape[0]
    head_size = DH
    groups = keys.shape[1] // head_size
    per_group = queries.shape[1] // keys.shape[1]
    kv_cols = keys.shape[1]
    scaling = 1.0 / math.sqrt(head_size)
    n_zh = lax.axis_size("zhi")
    n_x = lax.axis_size("xx")
    n_core = lax.axis_size("core")
    me = (lax.axis_index("zhi") * n_x + lax.axis_index("xx")) * n_core + lax.axis_index("core")
    first_row = me * rows_here
    my_rows = first_row + jnp.arange(rows_here, dtype=jnp.int32)
    kv_block = jnp.concatenate([keys, values], axis=1)
    for cid, axis in enumerate(("zhi", "xx", "core")):
        kv_block = stage_gather(kv_block, axis, cid + 4)
    attn_grad = lax.dot_general(
        lax.all_gather(d_out, "head", axis=1, tiled=True),
        w_out,
        (((1,), (1,)), ((), ())),
        preferred_element_type=jnp.float32,
    ).astype(jnp.bfloat16)
    heads = groups * per_group
    q_rows = queries.reshape(rows_here, heads, head_size).transpose(1, 0, 2).reshape(
        heads * rows_here, head_size)
    g_rows = attn_grad.reshape(rows_here, heads, head_size).transpose(1, 0, 2).reshape(
        heads * rows_here, head_size)
    dq_rows, kv_terms = attention_grads(
        q_rows, g_rows, kv_block, doc_starts, first_row, rows_here, scaling,
        (n_zh, n_x, n_core))
    query_grad = dq_rows
    kv_grad = kv_terms
    for cid, axis in enumerate(("core", "xx", "zhi")):
        kv_grad = stage_reduce(kv_grad, axis, cid + 1)
    kv_grad = kv_grad.astype(jnp.bfloat16)
    key_grad = kv_grad[:, :kv_cols]
    value_grad = kv_grad[:, kv_cols:]
    return (query_grad, key_grad, value_grad)


def solution(mesh):
    n_seq, n_head = mesh.shape["seq"], mesh.shape["head"]
    split = jax.sharding.Mesh(
        mesh.devices.reshape(n_seq // 8, 4, 2, n_head), ("zhi", "xx", "core", "head")
    )
    rows = ("zhi", "xx", "core")
    return jax.shard_map(
        shards,
        mesh=split,
        in_specs=(
            P(rows, "head"),
            P(rows, "head"),
            P(rows, "head"),
            P(rows, "head"),
            P("head", None),
            P(),
        ),
        out_specs=(P(rows, "head"), P(rows, "head"), P(rows, "head")),
        check_vma=False,
    )
```
